32 devices in a mesh: groups: 2 (over y), seq: 8 (over z, x), head: 2 (over core).
Axes of the slice: x: 2, y: 2, z: 4, core: 2. Of those that a mesh axis runs over, the one named last changes fastest.
Arguments:
- queries: bfloat16 [2048, 1024], P(('groups', 'seq'), 'head'), parts along dimension 0, may hold values from -600 to 600
- keys: bfloat16 [2048, 1024], P(('groups', 'seq'), 'head'), parts along dimension 0, may hold values from -600 to 600
- values: bfloat16 [2048, 1024], P(('groups', 'seq'), 'head'), parts along dimension 0, may hold values from -600 to 600
- out_weight: bfloat16 [2048, 1024], P('seq', 'head'), may hold values from -0.1875 to 0.1875
- grad_y: bfloat16 [2048, 2048], P(('groups', 'seq')), parts along dimension 0, may hold values from -6 to 6
Outputs:
- out_y: bfloat16 [2048, 2048], P(('groups', 'seq')), parts along dimension 0
- grad_queries: bfloat16 [2048, 1024], P(('groups', 'seq'), 'head'), parts along dimension 0
- grad_keys: bfloat16 [2048, 1024], P(('groups', 'seq'), 'head'), parts along dimension 0
- grad_values: bfloat16 [2048, 1024], P(('groups', 'seq'), 'head'), parts along dimension 0
- grad_weight: float32 [4096, 1024], P(('groups', 'seq'), 'head'), parts along dimension 0
The draws below stay inside these ranges and needn't reach their ends.
There are 2 independent parts, one for each index of `groups`. The reference program is written for one: setup_inputs(seed, part) draws one part's arguments, and reference() takes and returns one part's arrays. A program takes and returns all parts, laid end to end along the dimension named above; an argument that names none is the same for every part. Nothing has to cross between parts.
All inputs are finite; a program needn't handle non-finite values.
Results may differ from the reference program's by a relative error of at most 0.009.
Values may be sent and summed in bfloat16 or wider, within the bound.
No kernel may reach another device: no remote copies, remote signals or barrier semaphores. Data moves between devices by JAX's collectives and lax.ppermute only.
A program may use at most 192 MiB of HBM per device.

```python
import math
import jax
import jax.numpy as jnp
from jax import lax

D = 2048
H = 8
DH = 128
TILE = 128
HD = 1024
SEQ = 1024


def draw_scaled(key, draw_tag):
    base_key = jax.random.fold_in(key, draw_tag)
    noise_key, row_key, column_key = jax.random.split(base_key, 3)
    noise_part = jnp.clip(jax.random.normal(noise_key, (SEQ, HD), jnp.float32), -6.0, 6.0)
    row_scale = jnp.exp(jax.random.uniform(row_key, (SEQ, 1), jnp.float32) * math.log(10.0))
    column_scale = jnp.exp(jax.random.uniform(column_key, (1, HD), jnp.float32) * math.log(10.0))
    return (noise_part * row_scale * column_scale).astype(jnp.bfloat16)


def draw_queries(key, part):
    return draw_scaled(key, 101)


def draw_keys(key, part):
    return draw_scaled(key, 202)


def draw_values(key, part):
    return draw_scaled(key, 303)


def strengthened(values, key, source, target, blocks, factor):
    owner, partner = [(jnp.arange(values.shape[axis_at]) // (values.shape[axis_at] // blocks)).reshape([-1 if axis == axis_at else 1 for axis in range(values.ndim)]) for axis_at in (source, target)]
    chosen = jax.random.permutation(key, blocks)[partner]
    strong = (owner == chosen) | (owner == (partner + blocks // 2) % blocks)
    return jnp.where(strong, factor * values, values)


def level_of(rng, extent, cuts, smallest, largest):
    def one(dim, shards_of):
        steps = jax.random.uniform(jax.random.fold_in(jax.random.fold_in(rng, 6), dim), (shards_of,), jnp.float32, smallest / len(cuts), largest / len(cuts))
        return jnp.repeat(jnp.exp(steps), extent[dim] // shards_of).reshape((-1,) + (1,) * (len(extent) - dim - 1))

    factor_of = one(*cuts[0])
    for cut in cuts[1:]:
        factor_of = factor_of * one(*cut)
    return factor_of


def noise(stream_key, extent, deviation, limit, cuts=(), dtype=jnp.bfloat16):
    factor_of = level_of(stream_key, extent, cuts, -0.22, 0.18) if cuts else 1.0
    values = jax.random.normal(stream_key, extent, jnp.float32) * deviation * factor_of
    return jnp.minimum(jnp.maximum(values, -limit), limit).astype(dtype)


def bell_draw_with(key, shape, spread, limit, cuts, heavy, held_as=jnp.bfloat16):
    result = spread * jax.random.normal(key, shape, jnp.float32)
    if cuts:
        result = result * level_of(key, shape, cuts, -0.22, 0.18)
    return jnp.clip(strengthened(result, jax.random.fold_in(key, 3), *heavy), -limit, limit).astype(held_as)


def setup_inputs(seed: int = 0, part: int = 0) -> dict:
    splits = jax.random.split(jax.random.key(seed), 6)
    part_keys = jax.random.split(jax.random.fold_in(splits[5], part), 6)
    return {
        "queries": draw_queries(jax.random.fold_in(jax.random.fold_in(splits[5], part), 71), part),
        "keys": draw_keys(jax.random.fold_in(jax.random.fold_in(splits[5], part), 71), part),
        "values": draw_values(jax.random.fold_in(jax.random.fold_in(splits[5], part), 71), part),
        "out_weight": noise(splits[3], (D, HD), HD ** -0.5, 0.1875, ((0, 8), (1, 2))),
        "grad_y": bell_draw_with(part_keys[4], (SEQ, D), 1.0, 6.0, ((0, 8),), (0, 1, 8, 2.0)),
    }


epsilon = 1e-06

def tiled(array):
    return array.astype(jnp.float32).reshape(SEQ // TILE, TILE, H, DH)

def reference(queries, keys, values, out_weight, grad_y):
    query_tiles = tiled(queries)
    key_tiles = tiled(keys)
    value_tiles = tiled(values)
    causal = jnp.arange(TILE)[:, None] >= jnp.arange(TILE)[None, :]
    raw_scores = jnp.einsum('nthd,nshd->nhts', query_tiles, key_tiles)
    scores = jnp.where(causal, raw_scores, jnp.float32(0.0)).astype(jnp.bfloat16)
    states = jnp.einsum('nshd,nshe->nhde', key_tiles, value_tiles)
    prefix_sum = jnp.cumsum(states, axis=0) - states
    prefix_state = prefix_sum.astype(jnp.bfloat16).astype(jnp.float32)
    attended = jnp.einsum('nhts,nshe->nthe', scores.astype(jnp.float32), value_tiles)
    attended = attended + jnp.einsum('nthd,nhde->nthe', query_tiles, prefix_state)
    inverse_rms = lax.rsqrt(lax.optimization_barrier(jnp.mean(attended * attended, axis=-1, keepdims=True)) + epsilon)
    normed_exact = attended * inverse_rms
    normed = normed_exact.astype(jnp.bfloat16).reshape(SEQ, HD)
    out_y = jnp.dot(normed, out_weight.T, preferred_element_type=jnp.float32).astype(jnp.bfloat16)
    grad_normed = jnp.dot(grad_y, out_weight, preferred_element_type=jnp.float32).reshape(SEQ // TILE, TILE, H, DH)
    projected = lax.optimization_barrier(jnp.mean(grad_normed * normed_exact, axis=-1, keepdims=True))
    grad_out = (inverse_rms * (grad_normed - normed_exact * projected)).astype(jnp.bfloat16).astype(jnp.float32)
    raw_grad = jnp.einsum('nthe,nshe->nhts', grad_out, value_tiles)
    grad_scores = jnp.where(causal, raw_grad, jnp.float32(0.0)).astype(jnp.bfloat16).astype(jnp.float32)
    adjoint = jnp.einsum('nthd,nthe->nhde', query_tiles, grad_out)
    suffix_sum = jnp.flip(jnp.cumsum(jnp.flip(adjoint, 0), axis=0), 0) - adjoint
    suffix_state = suffix_sum.astype(jnp.bfloat16).astype(jnp.float32)
    score_values = scores.astype(jnp.float32)
    grad_queries = jnp.einsum('nhts,nshd->nthd', grad_scores, key_tiles)
    grad_queries = grad_queries + jnp.einsum('nthe,nhde->nthd', grad_out, prefix_state)
    grad_keys = jnp.einsum('nhts,nthd->nshd', grad_scores, query_tiles)
    grad_keys = grad_keys + jnp.einsum('nshe,nhde->nshd', value_tiles, suffix_state)
    grad_values = jnp.einsum('nhts,nthe->nshe', score_values, grad_out)
    grad_values = grad_values + jnp.einsum('nshd,nhde->nshe', key_tiles, suffix_state)
    grad_weight = jnp.dot(grad_y.T, normed, preferred_element_type=jnp.float32)
    return (out_y, grad_queries.reshape(SEQ, HD).astype(jnp.bfloat16), grad_keys.reshape(SEQ, HD).astype(jnp.bfloat16), grad_values.reshape(SEQ, HD).astype(jnp.bfloat16), grad_weight)
```

```python
import jax
import jax.numpy as jnp
from jax import lax
from jax.experimental import pallas as pl
from jax.experimental.pallas import tpu as pltpu
from jax.sharding import PartitionSpec as P

DH = 128
TILE = 128


epsilon = 1e-06
F32 = jnp.float32
BF16 = jnp.bfloat16
ROWS_T = (((0,), (0,)), ((), ()))
LAST_T = (((1,), (1,)), ((), ()))
PLAIN = (((1,), (0,)), ((), ()))


def carried_in(value, axis, join, neutral, backward):
    count, mine = (lax.axis_size(axis), lax.axis_index(axis))
    pieces = lax.all_gather(value, axis)
    if backward:
        pieces = pieces[::-1]
        mine = count - 1 - mine
    so_far = jnp.full_like(value, 0) + jnp.asarray(neutral, value.dtype)

    def turn(position, so_far):
        longer = join(so_far, pieces[position])
        return jnp.where(position < mine, longer, so_far)

    return lax.fori_loop(0, count - 1, turn, so_far)


def add_states(earlier, later):
    return earlier + later


def on_device(queries, keys, values, out_weight, grad_y):
    row_count = queries.shape[0]
    tile_count = row_count // TILE
    head_count = queries.shape[1] // DH

    def tiled(array):
        return array.reshape(tile_count, TILE, head_count, DH)

    query_tiles = tiled(queries)
    key_tiles = tiled(keys)
    value_tiles = tiled(values)
    causal = lax.broadcasted_iota(jnp.int32, (TILE, TILE), 0) >= lax.broadcasted_iota(
        jnp.int32, (TILE, TILE), 1
    )
    raw_scores = jnp.einsum(
        "nthd,nshd->nhts", query_tiles, key_tiles, preferred_element_type=jnp.float32
    )
    scores = jnp.where(causal, raw_scores, 0.0).astype(jnp.bfloat16)
    states = jnp.einsum(
        "nshd,nshe->nhde", key_tiles, value_tiles, preferred_element_type=jnp.float32
    )
    empty_state = jnp.zeros(states.shape[1:], jnp.float32)
    device_prefix = carried_in(jnp.sum(states, axis=0), "seq", add_states, empty_state, False)
    prefix_state = (device_prefix[None] + (jnp.cumsum(states, axis=0) - states)).astype(
        jnp.bfloat16
    )
    attended = jnp.einsum(
        "nhts,nshe->nthe", scores, value_tiles, preferred_element_type=jnp.float32
    )
    attended = attended + jnp.einsum(
        "nthd,nhde->nthe", query_tiles, prefix_state, preferred_element_type=jnp.float32
    )
    inverse_rms = lax.rsqrt(jnp.mean(attended * attended, axis=-1, keepdims=True) + epsilon)
    normed_exact = attended * inverse_rms
    normed = normed_exact.astype(jnp.bfloat16).reshape(row_count, -1)
    back_weight = lax.all_gather(out_weight, "seq", axis=0, tiled=True)
    grad_normed = jnp.dot(grad_y, back_weight, preferred_element_type=jnp.float32)
    fore_weight = lax.all_gather(out_weight, "seq", axis=0, tiled=True)
    partial_out = lax.dot_general(
        normed, fore_weight, LAST_T, preferred_element_type=jnp.float32
    )
    out_y = lax.psum(partial_out.astype(jnp.bfloat16), "head")
    grad_tiles = tiled(grad_normed)
    projected = jnp.mean(grad_tiles * normed_exact, axis=-1, keepdims=True)
    grad_out = (inverse_rms * (grad_tiles - normed_exact * projected)).astype(jnp.bfloat16)
    raw_grad = jnp.einsum(
        "nthe,nshe->nhts", grad_out, value_tiles, preferred_element_type=jnp.float32
    )
    grad_scores = jnp.where(causal, raw_grad, 0.0).astype(jnp.bfloat16)
    adjoint = jnp.einsum(
        "nthd,nthe->nhde", query_tiles, grad_out, preferred_element_type=jnp.float32
    )
    own_adjoint = jnp.sum(adjoint, axis=0)
    device_suffix = carried_in(own_adjoint, "seq", add_states, empty_state, True)
    later_tiles = jnp.flip(jnp.cumsum(jnp.flip(adjoint, 0), axis=0), 0) - adjoint
    suffix_state = (device_suffix[None] + later_tiles).astype(jnp.bfloat16)
    grad_queries = jnp.einsum(
        "nhts,nshd->nthd", grad_scores, key_tiles, preferred_element_type=jnp.float32
    )
    grad_queries = grad_queries + jnp.einsum(
        "nthe,nhde->nthd", grad_out, prefix_state, preferred_element_type=jnp.float32
    )
    grad_keys = jnp.einsum(
        "nhts,nthd->nshd", grad_scores, query_tiles, preferred_element_type=jnp.float32
    )
    grad_keys = grad_keys + jnp.einsum(
        "nshe,nhde->nshd", value_tiles, suffix_state, preferred_element_type=jnp.float32
    )
    grad_values = jnp.einsum(
        "nhts,nthe->nshe", scores, grad_out, preferred_element_type=jnp.float32
    )
    grad_values = grad_values + jnp.einsum(
        "nshd,nhde->nshe", key_tiles, suffix_state, preferred_element_type=jnp.float32
    )
    grad_weight = lax.psum_scatter(
        lax.dot_general(
            grad_y, normed, (((0,), (0,)), ((), ())), preferred_element_type=jnp.float32
        ),
        "seq",
        scatter_dimension=0,
        tiled=True,
    )
    return (
        out_y,
        grad_queries.reshape(row_count, -1).astype(jnp.bfloat16),
        grad_keys.reshape(row_count, -1).astype(jnp.bfloat16),
        grad_values.reshape(row_count, -1).astype(jnp.bfloat16),
        grad_weight,
    )


def dot(a, b, dims):
    return lax.dot_general(a, b, dims, preferred_element_type=F32)


def call(body, shapes, *args, flops=2**27, moved=2**20):
    return pl.pallas_call(
        body,
        out_shape=[jax.ShapeDtypeStruct(s, d) for s, d in shapes],
        in_specs=[pl.BlockSpec(memory_space=pltpu.VMEM)] * len(args),
        out_specs=[pl.BlockSpec(memory_space=pltpu.VMEM)] * len(shapes),
        cost_estimate=pl.CostEstimate(
            flops=flops, bytes_accessed=moved, transcendentals=0
        ),
        compiler_params=pltpu.CompilerParams(vmem_limit_bytes=24 * 2**20),
    )(*args)


def lanes(i, size):
    return pl.ds(pl.multiple_of(i * size, size), size)


def head_of(i):
    return slice(i * DH, (i + 1) * DH)


def causal_mask():
    rows = lax.broadcasted_iota(jnp.int32, (TILE, TILE), 0)
    return rows >= lax.broadcasted_iota(jnp.int32, (TILE, TILE), 1)


def place():
    s = lax.axis_index("seq")
    return lax.axis_index("groups"), s // 2, s % 2, lax.axis_index("head")


def on_short_line(seq, queries, keys, values, out_weight, grad_y):
    rows, feats = queries.shape
    heads = feats // DH
    wrows = out_weight.shape[0]
    half = wrows // 2
    line = seq // 2
    turns = range(1, line)
    outs = grad_y.shape[1]
    state = (heads * DH, DH)

    def rotate(array, k):
        return lax.ppermute(
            array, "seq", [(i, (i + 2 * k) % seq) for i in range(seq)]
        )

    def swap_x(array):
        return lax.ppermute(array, "seq", [(i, i ^ 1) for i in range(seq)])

    def swap_y(array):
        return lax.ppermute(array, "groups", [(0, 1), (1, 0)])

    def swap_core(array):
        return lax.ppermute(array, "head", [(0, 1), (1, 0)])

    def first(k_ref, v_ref, w_ref, gy_ref, s_ref, wh_ref, ys_ref, *gz_refs):
        g, z, x, h = place()
        for i in range(heads):
            s_ref[head_of(i), :] = dot(
                k_ref[:, head_of(i)], v_ref[:, head_of(i)], ROWS_T
            ).astype(BF16)
        wh_ref[...] = w_ref[pl.ds(pl.multiple_of(g * half, half), half), :]
        for i in range(seq):
            ys_ref[:, i * half : (i + 1) * half] = gy_ref[:, lanes(2 * i + 1 - g, half)]
        for k, gz_ref in zip(turns, gz_refs):
            gz_ref[...] = gy_ref[:, lanes(lax.rem(z + k, line) * 2 + h, wrows)]

    states, my_weight, y_send, *gz_send = call(
        first,
        [(state, BF16), ((half, feats), BF16), ((rows, seq * half), BF16)]
        + [((rows, wrows), BF16) for _ in turns],
        keys, values, out_weight, grad_y,
    )
    x_states = swap_x(states)
    z_weight = [rotate(my_weight, k) for k in turns]
    y_cols = swap_y(y_send)

    def local(q_ref, k_ref, v_ref, sc_ref, att_ref):
        mask = causal_mask()
        for i in range(heads):
            sc = dot(q_ref[:, head_of(i)], k_ref[:, head_of(i)], LAST_T)
            sc = jnp.where(mask, sc, 0.0).astype(BF16)
            sc_ref[:, head_of(i)] = sc
            att_ref[:, head_of(i)] = dot(sc, v_ref[:, head_of(i)], PLAIN)

    scores, att_local = call(
        local, [((rows, feats), BF16), ((rows, feats), F32)], queries, keys, values
    )

    pair_states = (states.astype(F32) + x_states.astype(F32)).astype(BF16)
    z_states = [rotate(pair_states, k) for k in turns]

    x_weight_a = swap_x(jnp.concatenate([my_weight, z_weight[0]], axis=0))
    x_weight_b = swap_x(jnp.concatenate(z_weight[1:], axis=0))

    def weight_blocks(refs):
        own, *others, xa_ref, xb_ref = refs
        g, z, x, h = place()
        blocks = []
        for k in range(line):
            zk = lax.rem(z - k + line, line)
            blocks.append((zk * 2 + x, (own, *others)[k][...]))
            far = xa_ref if k < 2 else xb_ref
            at = k if k < 2 else k - 2
            blocks.append((zk * 2 + 1 - x, far[at * half : (at + 1) * half, :]))
        return blocks

    weight_args = (my_weight, *z_weight, x_weight_a, x_weight_b)

    def back(gy_ref, yc_ref, *refs):
        *w_refs, own_ref, send_ref = refs
        g = lax.axis_index("groups")
        own = jnp.zeros((rows, feats), F32)
        other = jnp.zeros((rows, feats), F32)
        for s, block in weight_blocks(w_refs):
            own += dot(gy_ref[:, lanes(2 * s + g, half)], block, PLAIN)
            other += dot(yc_ref[:, lanes(s, half)], block, PLAIN)
        own_ref[...] = own
        send_ref[...] = other

    grad_own, grad_send = call(
        back, [((rows, feats), F32), ((rows, feats), F32)],
        grad_y, y_cols, *weight_args,
    )
    grad_other = swap_y(grad_send)

    z_cols = [rotate(a, k) for a, k in zip(gz_send, turns)]
    h_cols = [swap_core(a) for a in z_cols]

    def forward(q_ref, local_ref, xs_ref, *refs):
        *z_refs, att_ref, normed_ref, prefix_ref = refs
        g, z, x, h = place()
        total = jnp.where(x == 1, xs_ref[...].astype(F32), 0.0)
        for k, z_ref in zip(turns, z_refs):
            total += jnp.where(z >= k, z_ref[...].astype(F32), 0.0)
        prefix = total.astype(BF16)
        prefix_ref[...] = prefix
        for i in range(heads):
            att = local_ref[:, head_of(i)] + dot(
                q_ref[:, head_of(i)], prefix[head_of(i), :], PLAIN
            )
            att_ref[:, head_of(i)] = att
            inv = lax.rsqrt(jnp.mean(att * att, axis=-1, keepdims=True) + epsilon)
            normed_ref[:, head_of(i)] = (att * inv).astype(BF16)

    attended, normed, prefix = call(
        forward,
        [((rows, feats), F32), ((rows, feats), BF16), (state, BF16)],
        queries, att_local, x_states, *z_states,
    )
    y_normed = swap_y(normed)
    z_normed = [rotate(normed, k) for k in turns]

    def turn_back(att_ref, own_ref, other_ref, q_ref, go_ref, adj_ref):
        for i in range(heads):
            att = att_ref[:, head_of(i)]
            inv = lax.rsqrt(jnp.mean(att * att, axis=-1, keepdims=True) + epsilon)
            exact = att * inv
            grad = own_ref[:, head_of(i)] + other_ref[:, head_of(i)]
            along = jnp.mean(grad * exact, axis=-1, keepdims=True)
            go = (inv * (grad - exact * along)).astype(BF16)
            go_ref[:, head_of(i)] = go
            adj_ref[head_of(i), :] = dot(q_ref[:, head_of(i)], go, ROWS_T).astype(BF16)

    grad_out, adjoint = call(
        turn_back, [((rows, feats), BF16), (state, BF16)],
        attended, grad_own, grad_other, queries,
    )
    x_adjoint = swap_x(adjoint)

    def local_grads(go_ref, q_ref, k_ref, v_ref, sc_ref, pre_ref, gq_ref, gk_ref, gv_ref):
        mask = causal_mask()
        for i in range(heads):
            at = head_of(i)
            go = go_ref[:, at]
            gs = dot(go, v_ref[:, at], LAST_T)
            gs = jnp.where(mask, gs, 0.0).astype(BF16)
            gq = dot(gs, k_ref[:, at], PLAIN) + dot(go, pre_ref[at, :], LAST_T)
            gq_ref[:, at] = gq.astype(BF16)
            gk_ref[:, at] = dot(gs, q_ref[:, at], ROWS_T)
            gv_ref[:, at] = dot(sc_ref[:, at], go, ROWS_T)

    grad_queries, gk_local, gv_local = call(
        local_grads,
        [((rows, feats), BF16), ((rows, feats), F32), ((rows, feats), F32)],
        grad_out, queries, keys, values, scores, prefix,
    )
    pair_adjoint = (adjoint.astype(F32) + x_adjoint.astype(F32)).astype(BF16)
    z_adjoint = [rotate(pair_adjoint, k) for k in turns]

    def project(n_ref, yn_ref, *refs):
        *w_refs, own_ref, other_ref = refs
        for s, block in weight_blocks(w_refs):
            own_ref[:, lanes(s, half)] = dot(n_ref[...], block, LAST_T).astype(BF16)
            other_ref[:, lanes(s, half)] = dot(yn_ref[...], block, LAST_T).astype(BF16)

    out_own, out_send = call(
        project, [((rows, seq * half), BF16)] * 2, normed, y_normed, *weight_args
    )
    out_other = swap_y(out_send)
    core_own = swap_core(out_own)
    core_other = swap_core(out_other)

    def join(a_ref, b_ref, c_ref, d_ref, y_ref):
        g = lax.axis_index("groups")
        for i in range(seq):
            at = slice(i * half, (i + 1) * half)
            y_ref[:, lanes(2 * i + g, half)] = (
                a_ref[:, at].astype(F32) + b_ref[:, at].astype(F32)
            ).astype(BF16)
            y_ref[:, lanes(2 * i + 1 - g, half)] = (
                c_ref[:, at].astype(F32) + d_ref[:, at].astype(F32)
            ).astype(BF16)

    (out_y,) = call(
        join, [((rows, outs), BF16)], out_own, core_own, out_other, core_other
    )

    def weight_grad(gy_ref, n_ref, *refs):
        *ins, keep_ref, send_ref = refs
        count = line - 1
        c_refs, o_refs, z_refs = ins[:count], ins[count : 2 * count], ins[2 * count :]
        g, z, x, h = place()
        same = dot(gy_ref[:, lanes(z * 2 + h, wrows)], n_ref[...], ROWS_T)
        other = dot(gy_ref[:, lanes(z * 2 + 1 - h, wrows)], n_ref[...], ROWS_T)
        for c_ref, o_ref, z_ref in zip(c_refs, o_refs, z_refs):
            same += dot(c_ref[...], z_ref[...], ROWS_T)
            other += dot(o_ref[...], z_ref[...], ROWS_T)
        keep_ref[...] = jnp.where(x == h, same, other)
        send_ref[...] = jnp.where(x == h, other, same).astype(BF16)

    gw_keep, gw_send = call(
        weight_grad, [((wrows, feats), F32), ((wrows, feats), BF16)],
        grad_y, normed, *z_cols, *h_cols, *z_normed,
    )
    grad_weight = gw_keep + swap_x(gw_send).astype(F32)

    def last(gk_ref, gv_ref, k_ref, v_ref, xa_ref, *refs):
        *z_refs, ok_ref, ov_ref = refs
        g, z, x, h = place()
        total = jnp.where(x == 0, xa_ref[...].astype(F32), 0.0)
        for k, z_ref in zip(turns, z_refs):
            total += jnp.where(z < k, z_ref[...].astype(F32), 0.0)
        suffix = total.astype(BF16)
        for i in range(heads):
            at = head_of(i)
            ok_ref[:, at] = (
                gk_ref[:, at] + dot(v_ref[:, at], suffix[at, :], LAST_T)
            ).astype(BF16)
            ov_ref[:, at] = (
                gv_ref[:, at] + dot(k_ref[:, at], suffix[at, :], PLAIN)
            ).astype(BF16)

    grad_keys, grad_values = call(
        last, [((rows, feats), BF16)] * 2,
        gk_local, gv_local, keys, values, x_adjoint, *z_adjoint,
    )
    return out_y, grad_queries, grad_keys, grad_values, grad_weight


def solution(mesh):
    placed = (
        P(("groups", "seq"), "head"),
        P(("groups", "seq"), "head"),
        P(("groups", "seq"), "head"),
        P("seq", "head"),
        P(("groups", "seq"), None),
    )
    size = dict(mesh.shape)

    def program(queries, keys, values, out_weight, grad_y):
        short = size["seq"] == 8 and size["groups"] == 2 and size["head"] == 2
        if short and queries.shape[0] == TILE and out_weight.shape[0] % 256 == 0:
            return on_short_line(
                size["seq"], queries, keys, values, out_weight, grad_y
            )
        return on_device(queries, keys, values, out_weight, grad_y)

    return jax.shard_map(
        program,
        mesh=mesh,
        in_specs=placed,
        out_specs=(
            P(("groups", "seq"), None),
            P(("groups", "seq"), "head"),
            P(("groups", "seq"), "head"),
            P(("groups", "seq"), "head"),
            P(("groups", "seq"), "head"),
        ),
        check_vma=False,
    )
```

```python
import jax
import jax.numpy as jnp
from jax import lax
from jax.experimental import pallas as pl
from jax.experimental.pallas import tpu as pltpu
from jax.sharding import PartitionSpec as P

DH = 128
TILE = 128


epsilon = 1e-06
F32 = jnp.float32
BF16 = jnp.bfloat16
ROWS_T = (((0,), (0,)), ((), ()))
LAST_T = (((1,), (1,)), ((), ()))
PLAIN = (((1,), (0,)), ((), ()))


def carried_in(value, axis, join, neutral, backward):
    count, mine = (lax.axis_size(axis), lax.axis_index(axis))
    pieces = lax.all_gather(value, axis)
    if backward:
        pieces = pieces[::-1]
        mine = count - 1 - mine
    so_far = jnp.full_like(value, 0) + jnp.asarray(neutral, value.dtype)

    def turn(position, so_far):
        longer = join(so_far, pieces[position])
        return jnp.where(position < mine, longer, so_far)

    return lax.fori_loop(0, count - 1, turn, so_far)


def add_states(earlier, later):
    return earlier + later


def on_device(queries, keys, values, out_weight, grad_y):
    row_count = queries.shape[0]
    tile_count = row_count // TILE
    head_count = queries.shape[1] // DH

    def tiled(array):
        return array.reshape(tile_count, TILE, head_count, DH)

    query_tiles = tiled(queries)
    key_tiles = tiled(keys)
    value_tiles = tiled(values)
    causal = lax.broadcasted_iota(jnp.int32, (TILE, TILE), 0) >= lax.broadcasted_iota(
        jnp.int32, (TILE, TILE), 1
    )
    raw_scores = jnp.einsum(
        "nthd,nshd->nhts", query_tiles, key_tiles, preferred_element_type=jnp.float32
    )
    scores = jnp.where(causal, raw_scores, 0.0).astype(jnp.bfloat16)
    states = jnp.einsum(
        "nshd,nshe->nhde", key_tiles, value_tiles, preferred_element_type=jnp.float32
    )
    empty_state = jnp.zeros(states.shape[1:], jnp.float32)
    device_prefix = carried_in(jnp.sum(states, axis=0), "seq", add_states, empty_state, False)
    prefix_state = (device_prefix[None] + (jnp.cumsum(states, axis=0) - states)).astype(
        jnp.bfloat16
    )
    attended = jnp.einsum(
        "nhts,nshe->nthe", scores, value_tiles, preferred_element_type=jnp.float32
    )
    attended = attended + jnp.einsum(
        "nthd,nhde->nthe", query_tiles, prefix_state, preferred_element_type=jnp.float32
    )
    inverse_rms = lax.rsqrt(jnp.mean(attended * attended, axis=-1, keepdims=True) + epsilon)
    normed_exact = attended * inverse_rms
    normed = normed_exact.astype(jnp.bfloat16).reshape(row_count, -1)
    back_weight = lax.all_gather(out_weight, "seq", axis=0, tiled=True)
    grad_normed = jnp.dot(grad_y, back_weight, preferred_element_type=jnp.float32)
    fore_weight = lax.all_gather(out_weight, "seq", axis=0, tiled=True)
    partial_out = lax.dot_general(
        normed, fore_weight, LAST_T, preferred_element_type=jnp.float32
    )
    out_y = lax.psum(partial_out.astype(jnp.bfloat16), "head")
    grad_tiles = tiled(grad_normed)
    projected = jnp.mean(grad_tiles * normed_exact, axis=-1, keepdims=True)
    grad_out = (inverse_rms * (grad_tiles - normed_exact * projected)).astype(jnp.bfloat16)
    raw_grad = jnp.einsum(
        "nthe,nshe->nhts", grad_out, value_tiles, preferred_element_type=jnp.float32
    )
    grad_scores = jnp.where(causal, raw_grad, 0.0).astype(jnp.bfloat16)
    adjoint = jnp.einsum(
        "nthd,nthe->nhde", query_tiles, grad_out, preferred_element_type=jnp.float32
    )
    own_adjoint = jnp.sum(adjoint, axis=0)
    device_suffix = carried_in(own_adjoint, "seq", add_states, empty_state, True)
    later_tiles = jnp.flip(jnp.cumsum(jnp.flip(adjoint, 0), axis=0), 0) - adjoint
    suffix_state = (device_suffix[None] + later_tiles).astype(jnp.bfloat16)
    grad_queries = jnp.einsum(
        "nhts,nshd->nthd", grad_scores, key_tiles, preferred_element_type=jnp.float32
    )
    grad_queries = grad_queries + jnp.einsum(
        "nthe,nhde->nthd", grad_out, prefix_state, preferred_element_type=jnp.float32
    )
    grad_keys = jnp.einsum(
        "nhts,nthd->nshd", grad_scores, query_tiles, preferred_element_type=jnp.float32
    )
    grad_keys = grad_keys + jnp.einsum(
        "nshe,nhde->nshd", value_tiles, suffix_state, preferred_element_type=jnp.float32
    )
    grad_values = jnp.einsum(
        "nhts,nthe->nshe", scores, grad_out, preferred_element_type=jnp.float32
    )
    grad_values = grad_values + jnp.einsum(
        "nshd,nhde->nshe", key_tiles, suffix_state, preferred_element_type=jnp.float32
    )
    grad_weight = lax.psum_scatter(
        lax.dot_general(
            grad_y, normed, (((0,), (0,)), ((), ())), preferred_element_type=jnp.float32
        ),
        "seq",
        scatter_dimension=0,
        tiled=True,
    )
    return (
        out_y,
        grad_queries.reshape(row_count, -1).astype(jnp.bfloat16),
        grad_keys.reshape(row_count, -1).astype(jnp.bfloat16),
        grad_values.reshape(row_count, -1).astype(jnp.bfloat16),
        grad_weight,
    )


def dot(a, b, dims):
    return lax.dot_general(a, b, dims, preferred_element_type=F32)


def call(body, shapes, *args, flops=2**27, moved=2**20):
    return pl.pallas_call(
        body,
        out_shape=[jax.ShapeDtypeStruct(s, d) for s, d in shapes],
        in_specs=[pl.BlockSpec(memory_space=pltpu.VMEM)] * len(args),
        out_specs=[pl.BlockSpec(memory_space=pltpu.VMEM)] * len(shapes),
        cost_estimate=pl.CostEstimate(
            flops=flops, bytes_accessed=moved, transcendentals=0
        ),
        compiler_params=pltpu.CompilerParams(vmem_limit_bytes=24 * 2**20),
    )(*args)


def lanes(i, size):
    return pl.ds(pl.multiple_of(i * size, size), size)


def head_of(i):
    return slice(i * DH, (i + 1) * DH)


def causal_mask():
    rows = lax.broadcasted_iota(jnp.int32, (TILE, TILE), 0)
    return rows >= lax.broadcasted_iota(jnp.int32, (TILE, TILE), 1)


def place():
    s = lax.axis_index("seq")
    return lax.axis_index("groups"), s // 2, s % 2, lax.axis_index("head")


def on_short_line(seq, queries, keys, values, out_weight, grad_y):
    rows, feats = queries.shape
    heads = feats // DH
    wrows = out_weight.shape[0]
    half = wrows // 2
    line = seq // 2
    turns = range(1, line)
    outs = grad_y.shape[1]
    state = (heads * DH, DH)

    def permute(array, pairs):
        return lax.ppermute(array, "seq", pairs)

    def rotate(array, k):
        return permute(array, [(i, (i + 2 * k) % seq) for i in range(seq)])

    def swap(array, bit):
        return permute(array, [(i, i ^ bit) for i in range(seq)])

    def swap_y(array):
        return lax.ppermute(array, "groups", [(0, 1), (1, 0)])

    def swap_core(array):
        return lax.ppermute(array, "head", [(0, 1), (1, 0)])

    def side_by_side(*arrays):
        return jnp.concatenate(arrays, axis=0)

    g = lax.axis_index("groups")
    my_weight = lax.dynamic_slice_in_dim(out_weight, g * half, half, 0)
    z_weight = [rotate(my_weight, k) for k in turns]

    def first(k_hbm, v_hbm, gy_hbm, s_ref, ys_ref, gz_ref, k_ref, v_ref, gy_ref, sems):
        copies = [
            pltpu.make_async_copy(src, dst, sems.at[i])
            for i, (src, dst) in enumerate(
                ((k_hbm, k_ref), (v_hbm, v_ref), (gy_hbm, gy_ref))
            )
        ]
        for copy in copies:
            copy.start()
        g, z, x, h = place()
        copies[0].wait()
        copies[1].wait()
        for i in range(heads):
            s_ref[head_of(i), :] = dot(
                k_ref[:, head_of(i)], v_ref[:, head_of(i)], ROWS_T
            ).astype(BF16)
        copies[2].wait()
        for i in range(seq):
            ys_ref[:, i * half : (i + 1) * half] = gy_ref[:, lanes(2 * i + 1 - g, half)]
        far = z // 2 * 2
        far = 2 - far
        for b in range(2):
            gz_ref[b * rows : (b + 1) * rows, :] = gy_ref[
                :, lanes((far + b) * 2 + h, wrows)
            ]

    states, y_send, far_send = pl.pallas_call(
        first,
        out_shape=[
            jax.ShapeDtypeStruct(s, BF16)
            for s in (state, (rows, seq * half), (2 * rows, wrows))
        ],
        in_specs=[pl.BlockSpec(memory_space=pltpu.HBM)] * 3,
        out_specs=[pl.BlockSpec(memory_space=pltpu.VMEM)] * 3,
        scratch_shapes=[
            pltpu.VMEM(keys.shape, BF16),
            pltpu.VMEM(values.shape, BF16),
            pltpu.VMEM(grad_y.shape, BF16),
            pltpu.SemaphoreType.DMA((3,)),
        ],
        cost_estimate=pl.CostEstimate(
            flops=2**27, bytes_accessed=2**20, transcendentals=0
        ),
        compiler_params=pltpu.CompilerParams(vmem_limit_bytes=24 * 2**20),
    )(keys, values, grad_y)
    y_cols = swap_y(y_send)

    def local(q_ref, k_ref, v_ref, sc_ref, att_ref):
        mask = causal_mask()
        for i in range(heads):
            sc = dot(q_ref[:, head_of(i)], k_ref[:, head_of(i)], LAST_T)
            sc = jnp.where(mask, sc, 0.0).astype(BF16)
            sc_ref[:, head_of(i)] = sc
            att_ref[:, head_of(i)] = dot(sc, v_ref[:, head_of(i)], PLAIN)

    scores, att_local = call(
        local, [((rows, feats), BF16), ((rows, feats), F32)], queries, keys, values
    )

    def spread(own):
        by_x = swap(own, 1)
        total = own.astype(F32) + by_x.astype(F32)
        by_near = swap(total.astype(BF16), 2)
        total = total + by_near.astype(F32)
        return by_x, by_near, swap(total.astype(BF16), 4)

    got_states = spread(states)

    x_weight_a = swap(side_by_side(my_weight, z_weight[0]), 1)
    x_weight_b = swap(side_by_side(*z_weight[1:]), 1)

    def weight_blocks(refs):
        own, *others, xa_ref, xb_ref = refs
        g, z, x, h = place()
        blocks = []
        for k in range(line):
            zk = lax.rem(z - k + line, line)
            blocks.append((zk * 2 + x, (own, *others)[k][...]))
            far = xa_ref if k < 2 else xb_ref
            at = k if k < 2 else k - 2
            blocks.append((zk * 2 + 1 - x, far[at * half : (at + 1) * half, :]))
        return blocks

    weight_args = (my_weight, *z_weight, x_weight_a, x_weight_b)

    def back(gy_ref, yc_ref, *refs):
        *w_refs, own_ref, send_ref = refs
        g = lax.axis_index("groups")
        own = jnp.zeros((rows, feats), F32)
        other = jnp.zeros((rows, feats), F32)
        for s, block in weight_blocks(w_refs):
            own += dot(gy_ref[:, lanes(2 * s + g, half)], block, PLAIN)
            other += dot(yc_ref[:, lanes(s, half)], block, PLAIN)
        own_ref[...] = own
        send_ref[...] = other

    grad_own, grad_send = call(
        back, [((rows, feats), F32), ((rows, feats), F32)],
        grad_y, y_cols, *weight_args,
    )
    grad_other = swap_y(grad_send)

    far_cols = swap(far_send, 4)

    def relay(gy_ref, far_ref, near_ref):
        g, z, x, h = place()
        other = lax.rem(z + 1, 2)
        near = z + 1 - 2 * lax.rem(z, 2)
        near_ref[:rows, :] = gy_ref[:, lanes(near * 2 + h, wrows)]
        near_ref[rows:, :] = far_ref[pl.ds(pl.multiple_of(other * rows, rows), rows), :]

    (near_send,) = call(relay, [((2 * rows, wrows), BF16)], grad_y, far_cols)
    near_cols = swap(near_send, 2)

    def collect(far_ref, near_ref, out_ref):
        g, z, x, h = place()
        mine = lax.rem(z, 2)
        out_ref[:rows, :] = far_ref[pl.ds(pl.multiple_of(mine * rows, rows), rows), :]
        out_ref[rows:, :] = near_ref[...]

    (my_cols,) = call(collect, [((3 * rows, wrows), BF16)], far_cols, near_cols)
    core_cols = swap_core(my_cols)

    def forward(q_ref, local_ref, x_ref, near_ref, far_ref, att_ref, normed_ref, prefix_ref):
        g, z, x, h = place()
        total = jnp.where(x == 1, x_ref[...].astype(F32), 0.0)
        total += jnp.where(lax.rem(z, 2) == 1, near_ref[...].astype(F32), 0.0)
        total += jnp.where(z >= 2, far_ref[...].astype(F32), 0.0)
        prefix = total.astype(BF16)
        prefix_ref[...] = prefix
        for i in range(heads):
            att = local_ref[:, head_of(i)] + dot(
                q_ref[:, head_of(i)], prefix[head_of(i), :], PLAIN
            )
            att_ref[:, head_of(i)] = att
            inv = lax.rsqrt(jnp.mean(att * att, axis=-1, keepdims=True) + epsilon)
            normed_ref[:, head_of(i)] = (att * inv).astype(BF16)

    attended, normed, prefix = call(
        forward,
        [((rows, feats), F32), ((rows, feats), BF16), (state, BF16)],
        queries, att_local, *got_states,
    )
    y_normed = swap_y(normed)
    far_normed = swap(normed, 4)
    near_normed = swap(side_by_side(normed, far_normed), 2)

    def turn_back(att_ref, own_ref, other_ref, q_ref, go_ref, adj_ref):
        for i in range(heads):
            att = att_ref[:, head_of(i)]
            inv = lax.rsqrt(jnp.mean(att * att, axis=-1, keepdims=True) + epsilon)
            exact = att * inv
            grad = own_ref[:, head_of(i)] + other_ref[:, head_of(i)]
            along = jnp.mean(grad * exact, axis=-1, keepdims=True)
            go = (inv * (grad - exact * along)).astype(BF16)
            go_ref[:, head_of(i)] = go
            adj_ref[head_of(i), :] = dot(q_ref[:, head_of(i)], go, ROWS_T).astype(BF16)

    grad_out, adjoint = call(
        turn_back, [((rows, feats), BF16), (state, BF16)],
        attended, grad_own, grad_other, queries,
    )
    got_adjoint = spread(adjoint)

    def local_grads(go_ref, q_ref, k_ref, v_ref, sc_ref, pre_ref, gq_ref, gk_ref, gv_ref):
        mask = causal_mask()
        for i in range(heads):
            at = head_of(i)
            go = go_ref[:, at]
            gs = dot(go, v_ref[:, at], LAST_T)
            gs = jnp.where(mask, gs, 0.0).astype(BF16)
            gq = dot(gs, k_ref[:, at], PLAIN) + dot(go, pre_ref[at, :], LAST_T)
            gq_ref[:, at] = gq.astype(BF16)
            gk_ref[:, at] = dot(gs, q_ref[:, at], ROWS_T)
            gv_ref[:, at] = dot(sc_ref[:, at], go, ROWS_T)

    grad_queries, gk_local, gv_local = call(
        local_grads,
        [((rows, feats), BF16), ((rows, feats), F32), ((rows, feats), F32)],
        grad_out, queries, keys, values, scores, prefix,
    )

    def project(n_ref, yn_ref, *refs):
        *w_refs, own_ref, other_ref = refs
        for s, block in weight_blocks(w_refs):
            own_ref[:, lanes(s, half)] = dot(n_ref[...], block, LAST_T).astype(BF16)
            other_ref[:, lanes(s, half)] = dot(yn_ref[...], block, LAST_T).astype(BF16)

    out_own, out_send = call(
        project, [((rows, seq * half), BF16)] * 2, normed, y_normed, *weight_args
    )
    out_other = swap_y(out_send)
    core_own = swap_core(out_own)
    core_other = swap_core(out_other)

    def weight_grad(gy_ref, c_ref, o_ref, n_ref, far_ref, near_ref, keep_ref, send_ref):
        g, z, x, h = place()
        same = dot(gy_ref[:, lanes(z * 2 + h, wrows)], n_ref[...], ROWS_T)
        other = dot(gy_ref[:, lanes(z * 2 + 1 - h, wrows)], n_ref[...], ROWS_T)
        same += dot(c_ref[:rows, :], far_ref[...], ROWS_T)
        other += dot(o_ref[:rows, :], far_ref[...], ROWS_T)
        same += dot(c_ref[rows:, :], near_ref[...], ROWS_T)
        other += dot(o_ref[rows:, :], near_ref[...], ROWS_T)
        keep_ref[...] = jnp.where(x == h, same, other)
        send_ref[...] = jnp.where(x == h, other, same).astype(BF16)

    gw_keep, gw_send = call(
        weight_grad, [((wrows, feats), F32), ((wrows, feats), BF16)],
        grad_y, my_cols, core_cols, normed, far_normed, near_normed,
    )
    gw_other = swap(gw_send, 1)

    def join(a_ref, b_ref, c_ref, d_ref, y_ref):
        g = lax.axis_index("groups")
        for i in range(seq):
            at = slice(i * half, (i + 1) * half)
            y_ref[:, lanes(2 * i + g, half)] = (
                a_ref[:, at].astype(F32) + b_ref[:, at].astype(F32)
            ).astype(BF16)
            y_ref[:, lanes(2 * i + 1 - g, half)] = (
                c_ref[:, at].astype(F32) + d_ref[:, at].astype(F32)
            ).astype(BF16)

    (out_y,) = call(
        join, [((rows, outs), BF16)], out_own, core_own, out_other, core_other
    )
    grad_weight = gw_keep + gw_other.astype(F32)

    def last(gk_ref, gv_ref, k_ref, v_ref, x_ref, near_ref, far_ref, ok_ref, ov_ref):
        g, z, x, h = place()
        total = jnp.where(x == 0, x_ref[...].astype(F32), 0.0)
        total += jnp.where(lax.rem(z, 2) == 0, near_ref[...].astype(F32), 0.0)
        total += jnp.where(z < 2, far_ref[...].astype(F32), 0.0)
        suffix = total.astype(BF16)
        for i in range(heads):
            at = head_of(i)
            ok_ref[:, at] = (
                gk_ref[:, at] + dot(v_ref[:, at], suffix[at, :], LAST_T)
            ).astype(BF16)
            ov_ref[:, at] = (
                gv_ref[:, at] + dot(k_ref[:, at], suffix[at, :], PLAIN)
            ).astype(BF16)

    grad_keys, grad_values = call(
        last, [((rows, feats), BF16)] * 2,
        gk_local, gv_local, keys, values, *got_adjoint,
    )
    return out_y, grad_queries, grad_keys, grad_values, grad_weight


def solution(mesh):
    placed = (
        P(("groups", "seq"), "head"),
        P(("groups", "seq"), "head"),
        P(("groups", "seq"), "head"),
        P("seq", "head"),
        P(("groups", "seq"), None),
    )
    size = dict(mesh.shape)

    def program(queries, keys, values, out_weight, grad_y):
        short = size["seq"] == 8 and size["groups"] == 2 and size["head"] == 2
        if short and queries.shape[0] == TILE and out_weight.shape[0] % 256 == 0:
            return on_short_line(
                size["seq"], queries, keys, values, out_weight, grad_y
            )
        return on_device(queries, keys, values, out_weight, grad_y)

    return jax.shard_map(
        program,
        mesh=mesh,
        in_specs=placed,
        out_specs=(
            P(("groups", "seq"), None),
            P(("groups", "seq"), "head"),
            P(("groups", "seq"), "head"),
            P(("groups", "seq"), "head"),
            P(("groups", "seq"), "head"),
        ),
        check_vma=False,
    )
```

```python
import jax
import jax.numpy as jnp
from jax import lax
from jax.experimental import pallas as pl
from jax.experimental.pallas import tpu as pltpu
from jax.sharding import PartitionSpec as P

DH = 128
TILE = 128


epsilon = 1e-06
F32 = jnp.float32
BF16 = jnp.bfloat16
ROWS_T = (((0,), (0,)), ((), ()))
LAST_T = (((1,), (1,)), ((), ()))
PLAIN = (((1,), (0,)), ((), ()))


def carried_in(value, axis, join, neutral, backward):
    count, mine = (lax.axis_size(axis), lax.axis_index(axis))
    pieces = lax.all_gather(value, axis)
    if backward:
        pieces = pieces[::-1]
        mine = count - 1 - mine
    so_far = jnp.full_like(value, 0) + jnp.asarray(neutral, value.dtype)

    def turn(position, so_far):
        longer = join(so_far, pieces[position])
        return jnp.where(position < mine, longer, so_far)

    return lax.fori_loop(0, count - 1, turn, so_far)


def add_states(earlier, later):
    return earlier + later


def on_device(queries, keys, values, out_weight, grad_y):
    row_count = queries.shape[0]
    tile_count = row_count // TILE
    head_count = queries.shape[1] // DH

    def tiled(array):
        return array.reshape(tile_count, TILE, head_count, DH)

    query_tiles = tiled(queries)
    key_tiles = tiled(keys)
    value_tiles = tiled(values)
    causal = lax.broadcasted_iota(jnp.int32, (TILE, TILE), 0) >= lax.broadcasted_iota(
        jnp.int32, (TILE, TILE), 1
    )
    raw_scores = jnp.einsum(
        "nthd,nshd->nhts", query_tiles, key_tiles, preferred_element_type=jnp.float32
    )
    scores = jnp.where(causal, raw_scores, 0.0).astype(jnp.bfloat16)
    states = jnp.einsum(
        "nshd,nshe->nhde", key_tiles, value_tiles, preferred_element_type=jnp.float32
    )
    empty_state = jnp.zeros(states.shape[1:], jnp.float32)
    device_prefix = carried_in(jnp.sum(states, axis=0), "seq", add_states, empty_state, False)
    prefix_state = (device_prefix[None] + (jnp.cumsum(states, axis=0) - states)).astype(
        jnp.bfloat16
    )
    attended = jnp.einsum(
        "nhts,nshe->nthe", scores, value_tiles, preferred_element_type=jnp.float32
    )
    attended = attended + jnp.einsum(
        "nthd,nhde->nthe", query_tiles, prefix_state, preferred_element_type=jnp.float32
    )
    inverse_rms = lax.rsqrt(jnp.mean(attended * attended, axis=-1, keepdims=True) + epsilon)
    normed_exact = attended * inverse_rms
    normed = normed_exact.astype(jnp.bfloat16).reshape(row_count, -1)
    back_weight = lax.all_gather(out_weight, "seq", axis=0, tiled=True)
    grad_normed = jnp.dot(grad_y, back_weight, preferred_element_type=jnp.float32)
    fore_weight = lax.all_gather(out_weight, "seq", axis=0, tiled=True)
    partial_out = lax.dot_general(
        normed, fore_weight, LAST_T, preferred_element_type=jnp.float32
    )
    out_y = lax.psum(partial_out.astype(jnp.bfloat16), "head")
    grad_tiles = tiled(grad_normed)
    projected = jnp.mean(grad_tiles * normed_exact, axis=-1, keepdims=True)
    grad_out = (inverse_rms * (grad_tiles - normed_exact * projected)).astype(jnp.bfloat16)
    raw_grad = jnp.einsum(
        "nthe,nshe->nhts", grad_out, value_tiles, preferred_element_type=jnp.float32
    )
    grad_scores = jnp.where(causal, raw_grad, 0.0).astype(jnp.bfloat16)
    adjoint = jnp.einsum(
        "nthd,nthe->nhde", query_tiles, grad_out, preferred_element_type=jnp.float32
    )
    own_adjoint = jnp.sum(adjoint, axis=0)
    device_suffix = carried_in(own_adjoint, "seq", add_states, empty_state, True)
    later_tiles = jnp.flip(jnp.cumsum(jnp.flip(adjoint, 0), axis=0), 0) - adjoint
    suffix_state = (device_suffix[None] + later_tiles).astype(jnp.bfloat16)
    grad_queries = jnp.einsum(
        "nhts,nshd->nthd", grad_scores, key_tiles, preferred_element_type=jnp.float32
    )
    grad_queries = grad_queries + jnp.einsum(
        "nthe,nhde->nthd", grad_out, prefix_state, preferred_element_type=jnp.float32
    )
    grad_keys = jnp.einsum(
        "nhts,nthd->nshd", grad_scores, query_tiles, preferred_element_type=jnp.float32
    )
    grad_keys = grad_keys + jnp.einsum(
        "nshe,nhde->nshd", value_tiles, suffix_state, preferred_element_type=jnp.float32
    )
    grad_values = jnp.einsum(
        "nhts,nthe->nshe", scores, grad_out, preferred_element_type=jnp.float32
    )
    grad_values = grad_values + jnp.einsum(
        "nshd,nhde->nshe", key_tiles, suffix_state, preferred_element_type=jnp.float32
    )
    grad_weight = lax.psum_scatter(
        lax.dot_general(
            grad_y, normed, (((0,), (0,)), ((), ())), preferred_element_type=jnp.float32
        ),
        "seq",
        scatter_dimension=0,
        tiled=True,
    )
    return (
        out_y,
        grad_queries.reshape(row_count, -1).astype(jnp.bfloat16),
        grad_keys.reshape(row_count, -1).astype(jnp.bfloat16),
        grad_values.reshape(row_count, -1).astype(jnp.bfloat16),
        grad_weight,
    )


def dot(a, b, dims):
    return lax.dot_general(a, b, dims, preferred_element_type=F32)


def call(body, shapes, *args, flops=500000000, moved=2**20):
    return pl.pallas_call(
        body,
        out_shape=[jax.ShapeDtypeStruct(s, d) for s, d in shapes],
        in_specs=[pl.BlockSpec(memory_space=pltpu.VMEM)] * len(args),
        out_specs=[pl.BlockSpec(memory_space=pltpu.VMEM)] * len(shapes),
        cost_estimate=pl.CostEstimate(
            flops=flops, bytes_accessed=moved, transcendentals=0
        ),
        compiler_params=pltpu.CompilerParams(vmem_limit_bytes=24 * 2**20),
    )(*args)


def lanes(i, size):
    return pl.ds(pl.multiple_of(i * size, size), size)


def head_of(i):
    return slice(i * DH, (i + 1) * DH)


def causal_mask():
    rows = lax.broadcasted_iota(jnp.int32, (TILE, TILE), 0)
    return rows >= lax.broadcasted_iota(jnp.int32, (TILE, TILE), 1)


def place():
    s = lax.axis_index("seq")
    return lax.axis_index("groups"), s // 2, s % 2, lax.axis_index("head")


def on_short_line(seq, queries, keys, values, out_weight, grad_y):
    rows, feats = queries.shape
    heads = feats // DH
    wrows = out_weight.shape[0]
    half = wrows // 2
    line = seq // 2
    turns = range(1, line)
    outs = grad_y.shape[1]
    state = (heads * DH, DH)

    def permute(array, pairs):
        return lax.ppermute(array, "seq", pairs)

    def rotate(array, k):
        return permute(array, [(i, (i + 2 * k) % seq) for i in range(seq)])

    def swap(array, bit):
        return permute(array, [(i, i ^ bit) for i in range(seq)])

    def swap_y(array):
        return lax.ppermute(array, "groups", [(0, 1), (1, 0)])

    def swap_core(array):
        return lax.ppermute(array, "head", [(0, 1), (1, 0)])

    def side_by_side(*arrays):
        return jnp.concatenate(arrays, axis=0)

    def after(array, *others):
        return lax.optimization_barrier((array, *others))[0]

    g = lax.axis_index("groups")
    my_weight = lax.dynamic_slice_in_dim(out_weight, g * half, half, 0)
    z_weight = [rotate(my_weight, k) for k in turns]

    def own_state(k_ref, v_ref, s_ref):
        for i in range(heads):
            s_ref[head_of(i), :] = dot(
                k_ref[:, head_of(i)], v_ref[:, head_of(i)], ROWS_T
            ).astype(BF16)

    (states,) = call(own_state, [(state, BF16)], keys, values)
    x_weight_own = swap(my_weight, 1)

    def pack(gy_ref, ys_ref, gz_ref):
        g, z, x, h = place()
        for i in range(seq):
            ys_ref[:, i * half : (i + 1) * half] = gy_ref[:, lanes(2 * i + 1 - g, half)]
        far = 2 - z // 2 * 2
        for b in range(2):
            gz_ref[b * rows : (b + 1) * rows, :] = gy_ref[
                :, lanes((far + b) * 2 + h, wrows)
            ]

    y_send, far_send = call(
        pack, [((rows, seq * half), BF16), ((2 * rows, wrows), BF16)], grad_y
    )
    y_cols = swap_y(y_send)

    def local(q_ref, k_ref, v_ref, sc_ref, att_ref):
        mask = causal_mask()
        for i in range(heads):
            sc = dot(q_ref[:, head_of(i)], k_ref[:, head_of(i)], LAST_T)
            sc = jnp.where(mask, sc, 0.0).astype(BF16)
            sc_ref[:, head_of(i)] = sc
            att_ref[:, head_of(i)] = dot(sc, v_ref[:, head_of(i)], PLAIN)

    scores, att_local = call(
        local, [((rows, feats), BF16), ((rows, feats), F32)], queries, keys, values
    )

    def add(a, b):
        return (a.astype(F32) + b.astype(F32)).astype(BF16)

    x_states = swap(states, 1)
    pair_states = add(states, x_states)
    near_states = swap(pair_states, 2)
    quad_states = add(pair_states, near_states)
    got_states = x_states, near_states, swap(quad_states, 4)

    x_weight_far = swap(side_by_side(*z_weight[1:]), 1)
    x_weight_near = swap(after(z_weight[0], pair_states), 1)

    def weight_blocks(refs):
        own, *others, x_own, x_near, x_far = refs
        g, z, x, h = place()
        blocks = []
        for k in range(line):
            zk = lax.rem(z - k + line, line)
            blocks.append((zk * 2 + x, (own, *others)[k][...]))
            if k < 2:
                block = (x_own, x_near)[k][...]
            else:
                block = x_far[(k - 2) * half : (k - 1) * half, :]
            blocks.append((zk * 2 + 1 - x, block))
        return blocks

    weight_args = (my_weight, *z_weight, x_weight_own, x_weight_near, x_weight_far)

    def back_other(yc_ref, *refs):
        *w_refs, out_ref = refs
        total = jnp.zeros((rows, feats), F32)
        for s, block in weight_blocks(w_refs):
            total += dot(yc_ref[:, lanes(s, half)], block, PLAIN)
        out_ref[...] = total

    def back_own(gy_ref, *refs):
        *w_refs, out_ref = refs
        g = lax.axis_index("groups")
        total = jnp.zeros((rows, feats), F32)
        for s, block in weight_blocks(w_refs):
            total += dot(gy_ref[:, lanes(2 * s + g, half)], block, PLAIN)
        out_ref[...] = total

    (grad_send,) = call(
        back_other, [((rows, feats), F32)], after(y_cols, quad_states), *weight_args
    )
    grad_other = swap_y(grad_send)
    (grad_own,) = call(
        back_own, [((rows, feats), F32)], after(grad_y, grad_send), *weight_args
    )

    far_cols = swap(after(far_send, grad_send), 4)

    def relay(gy_ref, far_ref, near_ref):
        g, z, x, h = place()
        other = lax.rem(z + 1, 2)
        near = z + 1 - 2 * lax.rem(z, 2)
        near_ref[:rows, :] = gy_ref[:, lanes(near * 2 + h, wrows)]
        near_ref[rows:, :] = far_ref[pl.ds(pl.multiple_of(other * rows, rows), rows), :]

    (near_send,) = call(relay, [((2 * rows, wrows), BF16)], grad_y, far_cols)
    near_cols = swap(near_send, 2)

    def collect(far_ref, near_ref, out_ref):
        g, z, x, h = place()
        mine = lax.rem(z, 2)
        out_ref[:rows, :] = far_ref[pl.ds(pl.multiple_of(mine * rows, rows), rows), :]
        out_ref[rows:, :] = near_ref[...]

    (my_cols,) = call(collect, [((3 * rows, wrows), BF16)], far_cols, near_cols)
    core_cols = swap_core(my_cols)

    def forward(q_ref, local_ref, x_ref, near_ref, far_ref, att_ref, normed_ref, prefix_ref):
        g, z, x, h = place()
        total = jnp.where(x == 1, x_ref[...].astype(F32), 0.0)
        total += jnp.where(lax.rem(z, 2) == 1, near_ref[...].astype(F32), 0.0)
        total += jnp.where(z >= 2, far_ref[...].astype(F32), 0.0)
        prefix = total.astype(BF16)
        prefix_ref[...] = prefix
        for i in range(heads):
            att = local_ref[:, head_of(i)] + dot(
                q_ref[:, head_of(i)], prefix[head_of(i), :], PLAIN
            )
            att_ref[:, head_of(i)] = att
            inv = lax.rsqrt(jnp.mean(att * att, axis=-1, keepdims=True) + epsilon)
            normed_ref[:, head_of(i)] = (att * inv).astype(BF16)

    attended, normed, prefix = call(
        forward,
        [((rows, feats), F32), ((rows, feats), BF16), (state, BF16)],
        queries, att_local, *got_states,
    )
    y_normed = swap_y(normed)
    far_normed = swap(normed, 4)
    near_normed = swap(normed, 2)
    last_normed = swap(far_normed, 2)

    def turn_back(att_ref, own_ref, other_ref, q_ref, go_ref, adj_ref):
        for i in range(heads):
            att = att_ref[:, head_of(i)]
            inv = lax.rsqrt(jnp.mean(att * att, axis=-1, keepdims=True) + epsilon)
            exact = att * inv
            grad = own_ref[:, head_of(i)] + other_ref[:, head_of(i)]
            along = jnp.mean(grad * exact, axis=-1, keepdims=True)
            go = (inv * (grad - exact * along)).astype(BF16)
            go_ref[:, head_of(i)] = go
            adj_ref[head_of(i), :] = dot(q_ref[:, head_of(i)], go, ROWS_T).astype(BF16)

    grad_out, adjoint = call(
        turn_back, [((rows, feats), BF16), (state, BF16)],
        attended, grad_own, grad_other, queries,
    )
    x_adjoint = swap(adjoint, 1)
    pair_adjoint = add(adjoint, x_adjoint)
    near_adjoint = swap(pair_adjoint, 2)
    quad_adjoint = add(pair_adjoint, near_adjoint)
    got_adjoint = x_adjoint, near_adjoint, swap(quad_adjoint, 4)

    def local_grads(go_ref, q_ref, k_ref, v_ref, sc_ref, pre_ref, gq_ref, gk_ref, gv_ref):
        mask = causal_mask()
        for i in range(heads):
            at = head_of(i)
            go = go_ref[:, at]
            gs = dot(go, v_ref[:, at], LAST_T)
            gs = jnp.where(mask, gs, 0.0).astype(BF16)
            gq = dot(gs, k_ref[:, at], PLAIN) + dot(go, pre_ref[at, :], LAST_T)
            gq_ref[:, at] = gq.astype(BF16)
            gk_ref[:, at] = dot(gs, q_ref[:, at], ROWS_T)
            gv_ref[:, at] = dot(sc_ref[:, at], go, ROWS_T)

    grad_queries, gk_local, gv_local = call(
        local_grads,
        [((rows, feats), BF16), ((rows, feats), F32), ((rows, feats), F32)],
        grad_out, queries, keys, values, scores, prefix,
    )

    def project(n_ref, yn_ref, *refs):
        *w_refs, own_ref, other_ref = refs
        for s, block in weight_blocks(w_refs):
            own_ref[:, lanes(s, half)] = dot(n_ref[...], block, LAST_T).astype(BF16)
            other_ref[:, lanes(s, half)] = dot(yn_ref[...], block, LAST_T).astype(BF16)

    out_own, out_send = call(
        project, [((rows, seq * half), BF16)] * 2, normed, y_normed, *weight_args
    )
    out_other = swap_y(out_send)
    core_own = swap_core(out_own)
    core_other = swap_core(out_other)

    def weight_grad(gy_ref, c_ref, o_ref, n_ref, *refs):
        *n_refs, keep_ref, send_ref = refs
        g, z, x, h = place()
        same = dot(gy_ref[:, lanes(z * 2 + h, wrows)], n_ref[...], ROWS_T)
        other = dot(gy_ref[:, lanes(z * 2 + 1 - h, wrows)], n_ref[...], ROWS_T)
        for i, there_ref in enumerate(n_refs):
            at = slice(i * rows, (i + 1) * rows)
            same += dot(c_ref[at, :], there_ref[...], ROWS_T)
            other += dot(o_ref[at, :], there_ref[...], ROWS_T)
        keep_ref[...] = jnp.where(x == h, same, other)
        send_ref[...] = jnp.where(x == h, other, same).astype(BF16)

    gw_keep, gw_send = call(
        weight_grad, [((wrows, feats), F32), ((wrows, feats), BF16)],
        grad_y, my_cols, core_cols, normed, far_normed, near_normed, last_normed,
    )
    gw_other = swap(gw_send, 1)

    def join(a_ref, b_ref, c_ref, d_ref, y_ref):
        g = lax.axis_index("groups")
        for i in range(seq):
            at = slice(i * half, (i + 1) * half)
            y_ref[:, lanes(2 * i + g, half)] = (
                a_ref[:, at].astype(F32) + b_ref[:, at].astype(F32)
            ).astype(BF16)
            y_ref[:, lanes(2 * i + 1 - g, half)] = (
                c_ref[:, at].astype(F32) + d_ref[:, at].astype(F32)
            ).astype(BF16)

    (out_y,) = call(
        join, [((rows, outs), BF16)], out_own, core_own, out_other, core_other
    )
    grad_weight = gw_keep + gw_other.astype(F32)

    def last(gk_ref, gv_ref, k_ref, v_ref, x_ref, near_ref, far_ref, ok_ref, ov_ref):
        g, z, x, h = place()
        total = jnp.where(x == 0, x_ref[...].astype(F32), 0.0)
        total += jnp.where(lax.rem(z, 2) == 0, near_ref[...].astype(F32), 0.0)
        total += jnp.where(z < 2, far_ref[...].astype(F32), 0.0)
        suffix = total.astype(BF16)
        for i in range(heads):
            at = head_of(i)
            ok_ref[:, at] = (
                gk_ref[:, at] + dot(v_ref[:, at], suffix[at, :], LAST_T)
            ).astype(BF16)
            ov_ref[:, at] = (
                gv_ref[:, at] + dot(k_ref[:, at], suffix[at, :], PLAIN)
            ).astype(BF16)

    grad_keys, grad_values = call(
        last, [((rows, feats), BF16)] * 2,
        gk_local, gv_local, keys, values, *got_adjoint,
    )
    return out_y, grad_queries, grad_keys, grad_values, grad_weight


def solution(mesh):
    placed = (
        P(("groups", "seq"), "head"),
        P(("groups", "seq"), "head"),
        P(("groups", "seq"), "head"),
        P("seq", "head"),
        P(("groups", "seq"), None),
    )
    size = dict(mesh.shape)

    def program(queries, keys, values, out_weight, grad_y):
        short = size["seq"] == 8 and size["groups"] == 2 and size["head"] == 2
        if short and queries.shape[0] == TILE and out_weight.shape[0] % 256 == 0:
            return on_short_line(
                size["seq"], queries, keys, values, out_weight, grad_y
            )
        return on_device(queries, keys, values, out_weight, grad_y)

    return jax.shard_map(
        program,
        mesh=mesh,
        in_specs=placed,
        out_specs=(
            P(("groups", "seq"), None),
            P(("groups", "seq"), "head"),
            P(("groups", "seq"), "head"),
            P(("groups", "seq"), "head"),
            P(("groups", "seq"), "head"),
        ),
        check_vma=False,
    )
```

```python
import jax
import jax.numpy as jnp
from jax import lax
from jax.experimental import pallas as pl
from jax.experimental.pallas import tpu as pltpu
from jax.sharding import PartitionSpec as P

DH = 128
TILE = 128


epsilon = 1e-06
F32 = jnp.float32
BF16 = jnp.bfloat16
ROWS_T = (((0,), (0,)), ((), ()))
LAST_T = (((1,), (1,)), ((), ()))
PLAIN = (((1,), (0,)), ((), ()))


def carried_in(value, axis, join, neutral, backward):
    count, mine = (lax.axis_size(axis), lax.axis_index(axis))
    pieces = lax.all_gather(value, axis)
    if backward:
        pieces = pieces[::-1]
        mine = count - 1 - mine
    so_far = jnp.full_like(value, 0) + jnp.asarray(neutral, value.dtype)

    def turn(position, so_far):
        longer = join(so_far, pieces[position])
        return jnp.where(position < mine, longer, so_far)

    return lax.fori_loop(0, count - 1, turn, so_far)


def add_states(earlier, later):
    return earlier + later


def on_device(queries, keys, values, out_weight, grad_y):
    row_count = queries.shape[0]
    tile_count = row_count // TILE
    head_count = queries.shape[1] // DH

    def tiled(array):
        return array.reshape(tile_count, TILE, head_count, DH)

    query_tiles = tiled(queries)
    key_tiles = tiled(keys)
    value_tiles = tiled(values)
    causal = lax.broadcasted_iota(jnp.int32, (TILE, TILE), 0) >= lax.broadcasted_iota(
        jnp.int32, (TILE, TILE), 1
    )
    raw_scores = jnp.einsum(
        "nthd,nshd->nhts", query_tiles, key_tiles, preferred_element_type=jnp.float32
    )
    scores = jnp.where(causal, raw_scores, 0.0).astype(jnp.bfloat16)
    states = jnp.einsum(
        "nshd,nshe->nhde", key_tiles, value_tiles, preferred_element_type=jnp.float32
    )
    empty_state = jnp.zeros(states.shape[1:], jnp.float32)
    device_prefix = carried_in(jnp.sum(states, axis=0), "seq", add_states, empty_state, False)
    prefix_state = (device_prefix[None] + (jnp.cumsum(states, axis=0) - states)).astype(
        jnp.bfloat16
    )
    attended = jnp.einsum(
        "nhts,nshe->nthe", scores, value_tiles, preferred_element_type=jnp.float32
    )
    attended = attended + jnp.einsum(
        "nthd,nhde->nthe", query_tiles, prefix_state, preferred_element_type=jnp.float32
    )
    inverse_rms = lax.rsqrt(jnp.mean(attended * attended, axis=-1, keepdims=True) + epsilon)
    normed_exact = attended * inverse_rms
    normed = normed_exact.astype(jnp.bfloat16).reshape(row_count, -1)
    back_weight = lax.all_gather(out_weight, "seq", axis=0, tiled=True)
    grad_normed = jnp.dot(grad_y, back_weight, preferred_element_type=jnp.float32)
    fore_weight = lax.all_gather(out_weight, "seq", axis=0, tiled=True)
    partial_out = lax.dot_general(
        normed, fore_weight, LAST_T, preferred_element_type=jnp.float32
    )
    out_y = lax.psum(partial_out.astype(jnp.bfloat16), "head")
    grad_tiles = tiled(grad_normed)
    projected = jnp.mean(grad_tiles * normed_exact, axis=-1, keepdims=True)
    grad_out = (inverse_rms * (grad_tiles - normed_exact * projected)).astype(jnp.bfloat16)
    raw_grad = jnp.einsum(
        "nthe,nshe->nhts", grad_out, value_tiles, preferred_element_type=jnp.float32
    )
    grad_scores = jnp.where(causal, raw_grad, 0.0).astype(jnp.bfloat16)
    adjoint = jnp.einsum(
        "nthd,nthe->nhde", query_tiles, grad_out, preferred_element_type=jnp.float32
    )
    own_adjoint = jnp.sum(adjoint, axis=0)
    device_suffix = carried_in(own_adjoint, "seq", add_states, empty_state, True)
    later_tiles = jnp.flip(jnp.cumsum(jnp.flip(adjoint, 0), axis=0), 0) - adjoint
    suffix_state = (device_suffix[None] + later_tiles).astype(jnp.bfloat16)
    grad_queries = jnp.einsum(
        "nhts,nshd->nthd", grad_scores, key_tiles, preferred_element_type=jnp.float32
    )
    grad_queries = grad_queries + jnp.einsum(
        "nthe,nhde->nthd", grad_out, prefix_state, preferred_element_type=jnp.float32
    )
    grad_keys = jnp.einsum(
        "nhts,nthd->nshd", grad_scores, query_tiles, preferred_element_type=jnp.float32
    )
    grad_keys = grad_keys + jnp.einsum(
        "nshe,nhde->nshd", value_tiles, suffix_state, preferred_element_type=jnp.float32
    )
    grad_values = jnp.einsum(
        "nhts,nthe->nshe", scores, grad_out, preferred_element_type=jnp.float32
    )
    grad_values = grad_values + jnp.einsum(
        "nshd,nhde->nshe", key_tiles, suffix_state, preferred_element_type=jnp.float32
    )
    grad_weight = lax.psum_scatter(
        lax.dot_general(
            grad_y, normed, (((0,), (0,)), ((), ())), preferred_element_type=jnp.float32
        ),
        "seq",
        scatter_dimension=0,
        tiled=True,
    )
    return (
        out_y,
        grad_queries.reshape(row_count, -1).astype(jnp.bfloat16),
        grad_keys.reshape(row_count, -1).astype(jnp.bfloat16),
        grad_values.reshape(row_count, -1).astype(jnp.bfloat16),
        grad_weight,
    )


def dot(a, b, dims):
    return lax.dot_general(a, b, dims, preferred_element_type=F32)


def call(body, shapes, *args, flops=1000000000, moved=2**20):
    return pl.pallas_call(
        body,
        out_shape=[jax.ShapeDtypeStruct(s, d) for s, d in shapes],
        in_specs=[pl.BlockSpec(memory_space=pltpu.VMEM)] * len(args),
        out_specs=[pl.BlockSpec(memory_space=pltpu.VMEM)] * len(shapes),
        cost_estimate=pl.CostEstimate(
            flops=flops, bytes_accessed=moved, transcendentals=0
        ),
        compiler_params=pltpu.CompilerParams(vmem_limit_bytes=24 * 2**20),
    )(*args)


def lanes(i, size):
    return pl.ds(pl.multiple_of(i * size, size), size)


def head_of(i):
    return slice(i * DH, (i + 1) * DH)


def causal_mask():
    rows = lax.broadcasted_iota(jnp.int32, (TILE, TILE), 0)
    return rows >= lax.broadcasted_iota(jnp.int32, (TILE, TILE), 1)


def place():
    s = lax.axis_index("seq")
    return lax.axis_index("groups"), s // 2, s % 2, lax.axis_index("head")


def on_short_line(seq, queries, keys, values, out_weight, grad_y):
    rows, feats = queries.shape
    heads = feats // DH
    wrows = out_weight.shape[0]
    half = wrows // 2
    line = seq // 2
    turns = range(1, line)
    outs = grad_y.shape[1]
    state = (DH, heads * DH)

    def permute(array, pairs):
        return lax.ppermute(array, "seq", pairs)

    def rotate(array, k):
        return permute(array, [(i, (i + 2 * k) % seq) for i in range(seq)])

    def swap(array, bit):
        return permute(array, [(i, i ^ bit) for i in range(seq)])

    def swap_y(array):
        return lax.ppermute(array, "groups", [(0, 1), (1, 0)])

    def swap_core(array):
        return lax.ppermute(array, "head", [(0, 1), (1, 0)])

    def side_by_side(*arrays):
        return jnp.concatenate(arrays, axis=0)

    def tie(*arrays):
        return lax.optimization_barrier(arrays)

    g = lax.axis_index("groups")
    my_weight = lax.dynamic_slice_in_dim(out_weight, g * half, half, 0)
    z_weight = [rotate(my_weight, k) for k in turns]

    def own_state(k_ref, v_ref, w_ref, out_ref):
        out_ref[:half, :] = w_ref[...]
        for i in range(heads):
            out_ref[half:, head_of(i)] = dot(
                k_ref[:, head_of(i)], v_ref[:, head_of(i)], ROWS_T
            ).astype(BF16)

    (weight_states,) = call(
        own_state, [((half + DH, feats), BF16)], keys, values, my_weight
    )
    x_weight_states = swap(weight_states, 1)
    states, x_states = weight_states[half:], x_weight_states[half:]

    def columns(gy_ref, z, h):
        return gy_ref[:, lanes(z * 2 + h, wrows)]

    def pack(gy_ref, ys_ref, near_ref):
        g, z, x, h = place()
        for i in range(seq):
            ys_ref[:, i * half : (i + 1) * half] = gy_ref[:, lanes(2 * i + 1 - g, half)]
        near = z + 1 - 2 * lax.rem(z, 2)
        near_ref[:rows, :] = columns(gy_ref, near, h)
        near_ref[rows:, :] = columns(gy_ref, lax.rem(near + 2, line), h)

    y_send, near_send = call(
        pack, [((rows, seq * half), BF16), ((2 * rows, wrows), BF16)], grad_y
    )
    near_cols = swap(near_send, 2)
    y_cols = swap_y(y_send)

    def local(q_ref, k_ref, v_ref, sc_ref, att_ref):
        mask = causal_mask()
        for i in range(heads):
            sc = dot(q_ref[:, head_of(i)], k_ref[:, head_of(i)], LAST_T)
            sc = jnp.where(mask, sc, 0.0).astype(BF16)
            sc_ref[:, head_of(i)] = sc
            att_ref[:, head_of(i)] = dot(sc, v_ref[:, head_of(i)], PLAIN)

    scores, att_local = call(
        local, [((rows, feats), BF16), ((rows, feats), F32)], queries, keys, values
    )

    def add(a, b):
        return (a.astype(F32) + b.astype(F32)).astype(BF16)

    x_weight_far = swap(side_by_side(*z_weight[1:]), 1)
    x_states, *z_weight[1:] = tie(x_states, *z_weight[1:])
    pair_states = add(states, x_states)
    near_states = swap(pair_states, 2)
    pair_states, z_weight[0] = tie(pair_states, z_weight[0])
    quad_states = add(pair_states, near_states)
    got_states = x_states, near_states, swap(quad_states, 4)

    x_weight_near = swap(z_weight[0], 1)
    near_cols, z_weight[0] = tie(near_cols, z_weight[0])

    def relay(gy_ref, near_ref, far_ref):
        g, z, x, h = place()
        far_ref[:rows, :] = columns(gy_ref, lax.rem(z + 2, line), h)
        far_ref[rows:, :] = near_ref[rows:, :]

    (far_send,) = call(relay, [((2 * rows, wrows), BF16)], grad_y, near_cols)

    far_cols = swap(far_send, 4)

    def weight_blocks(refs):
        own, *others, x_own, x_near, x_far = refs
        x_own = x_own.at[:half, :]
        g, z, x, h = place()
        blocks = []
        for k in range(line):
            zk = lax.rem(z - k + line, line)
            blocks.append((zk * 2 + x, (own, *others)[k][...]))
            if k < 2:
                block = (x_own, x_near)[k][...]
            else:
                block = x_far[(k - 2) * half : (k - 1) * half, :]
            blocks.append((zk * 2 + 1 - x, block))
        return blocks

    weight_args = (my_weight, *z_weight, x_weight_states, x_weight_near, x_weight_far)

    def back_other(yc_ref, *refs):
        *w_refs, out_ref = refs
        total = jnp.zeros((rows, feats), F32)
        for s, block in weight_blocks(w_refs):
            total += dot(yc_ref[:, lanes(s, half)], block, PLAIN)
        out_ref[...] = total

    def back_own(gy_ref, *refs):
        *w_refs, out_ref = refs
        g = lax.axis_index("groups")
        total = jnp.zeros((rows, feats), F32)
        for s, block in weight_blocks(w_refs):
            total += dot(gy_ref[:, lanes(2 * s + g, half)], block, PLAIN)
        out_ref[...] = total

    (grad_send,) = call(
        back_other, [((rows, feats), F32)], y_cols, *weight_args
    )
    grad_other = swap_y(grad_send)
    (grad_own,) = call(
        back_own, [((rows, feats), F32)], grad_y, *weight_args
    )

    my_cols = side_by_side(near_cols[:rows], far_cols)
    core_cols = swap_core(my_cols)

    def forward(q_ref, local_ref, x_ref, near_ref, far_ref, att_ref, normed_ref, prefix_ref):
        g, z, x, h = place()
        total = jnp.where(x == 1, x_ref[...].astype(F32), 0.0)
        total += jnp.where(lax.rem(z, 2) == 1, near_ref[...].astype(F32), 0.0)
        total += jnp.where(z >= 2, far_ref[...].astype(F32), 0.0)
        prefix = total.astype(BF16)
        prefix_ref[...] = prefix
        for i in range(heads):
            att = local_ref[:, head_of(i)] + dot(
                q_ref[:, head_of(i)], prefix[:, head_of(i)], PLAIN
            )
            att_ref[:, head_of(i)] = att
            inv = lax.rsqrt(jnp.mean(att * att, axis=-1, keepdims=True) + epsilon)
            normed_ref[:, head_of(i)] = (att * inv).astype(BF16)

    attended, normed, prefix = call(
        forward,
        [((rows, feats), F32), ((rows, feats), BF16), (state, BF16)],
        queries, att_local, *got_states,
    )
    y_normed = swap_y(normed)
    far_normed = swap(normed, 4)
    near_normed = swap(normed, 2)
    last_normed = swap(far_normed, 2)

    def turn_back(att_ref, own_ref, other_ref, q_ref, go_ref, adj_ref):
        for i in range(heads):
            att = att_ref[:, head_of(i)]
            inv = lax.rsqrt(jnp.mean(att * att, axis=-1, keepdims=True) + epsilon)
            exact = att * inv
            grad = own_ref[:, head_of(i)] + other_ref[:, head_of(i)]
            along = jnp.mean(grad * exact, axis=-1, keepdims=True)
            go = (inv * (grad - exact * along)).astype(BF16)
            go_ref[:, head_of(i)] = go
            adj_ref[:, head_of(i)] = dot(q_ref[:, head_of(i)], go, ROWS_T).astype(BF16)

    grad_out, adjoint = call(
        turn_back, [((rows, feats), BF16), (state, BF16)],
        attended, grad_own, grad_other, queries,
    )
    x_adjoint = swap(adjoint, 1)
    pair_adjoint = add(adjoint, x_adjoint)
    near_adjoint = swap(pair_adjoint, 2)
    quad_adjoint = add(pair_adjoint, near_adjoint)
    got_adjoint = x_adjoint, near_adjoint, swap(quad_adjoint, 4)

    def local_grads(go_ref, q_ref, k_ref, v_ref, sc_ref, pre_ref, gq_ref, gk_ref, gv_ref):
        mask = causal_mask()
        for i in range(heads):
            at = head_of(i)
            go = go_ref[:, at]
            gs = dot(go, v_ref[:, at], LAST_T)
            gs = jnp.where(mask, gs, 0.0).astype(BF16)
            gq = dot(gs, k_ref[:, at], PLAIN) + dot(go, pre_ref[:, at], LAST_T)
            gq_ref[:, at] = gq.astype(BF16)
            gk_ref[:, at] = dot(gs, q_ref[:, at], ROWS_T)
            gv_ref[:, at] = dot(sc_ref[:, at], go, ROWS_T)

    grad_queries, gk_local, gv_local = call(
        local_grads,
        [((rows, feats), BF16), ((rows, feats), F32), ((rows, feats), F32)],
        grad_out, queries, keys, values, scores, prefix,
    )

    def project(n_ref, yn_ref, *refs):
        *w_refs, own_ref, other_ref = refs
        for s, block in weight_blocks(w_refs):
            own_ref[:, lanes(s, half)] = dot(n_ref[...], block, LAST_T).astype(BF16)
            other_ref[:, lanes(s, half)] = dot(yn_ref[...], block, LAST_T).astype(BF16)

    out_own, out_send = call(
        project, [((rows, seq * half), BF16)] * 2, normed, y_normed, *weight_args
    )
    out_other = swap_y(out_send)
    core_own = swap_core(out_own)
    core_other = swap_core(out_other)

    def weight_grad(gy_ref, c_ref, o_ref, n_ref, *refs):
        *n_refs, keep_ref, send_ref = refs
        g, z, x, h = place()
        same = dot(columns(gy_ref, z, h), n_ref[...], ROWS_T)
        other = dot(columns(gy_ref, z, 1 - h), n_ref[...], ROWS_T)
        for i, there_ref in enumerate(n_refs):
            at = slice(i * rows, (i + 1) * rows)
            same += dot(c_ref[at, :], there_ref[...], ROWS_T)
            other += dot(o_ref[at, :], there_ref[...], ROWS_T)
        keep_ref[...] = jnp.where(x == h, same, other)
        send_ref[...] = jnp.where(x == h, other, same).astype(BF16)

    gw_keep, gw_send = call(
        weight_grad, [((wrows, feats), F32), ((wrows, feats), BF16)],
        grad_y, my_cols, core_cols, normed, near_normed, far_normed, last_normed,
    )
    gw_other = swap(gw_send, 1)

    def join(a_ref, b_ref, c_ref, d_ref, y_ref):
        g = lax.axis_index("groups")
        for i in range(seq):
            at = slice(i * half, (i + 1) * half)
            y_ref[:, lanes(2 * i + g, half)] = (
                a_ref[:, at].astype(F32) + b_ref[:, at].astype(F32)
            ).astype(BF16)
            y_ref[:, lanes(2 * i + 1 - g, half)] = (
                c_ref[:, at].astype(F32) + d_ref[:, at].astype(F32)
            ).astype(BF16)

    (out_y,) = call(
        join, [((rows, outs), BF16)], out_own, core_own, out_other, core_other
    )
    grad_weight = gw_keep + gw_other.astype(F32)

    def last(gk_ref, gv_ref, k_ref, v_ref, x_ref, near_ref, far_ref, ok_ref, ov_ref):
        g, z, x, h = place()
        total = jnp.where(x == 0, x_ref[...].astype(F32), 0.0)
        total += jnp.where(lax.rem(z, 2) == 0, near_ref[...].astype(F32), 0.0)
        total += jnp.where(z < 2, far_ref[...].astype(F32), 0.0)
        suffix = total.astype(BF16)
        for i in range(heads):
            at = head_of(i)
            ok_ref[:, at] = (
                gk_ref[:, at] + dot(v_ref[:, at], suffix[:, at], LAST_T)
            ).astype(BF16)
            ov_ref[:, at] = (
                gv_ref[:, at] + dot(k_ref[:, at], suffix[:, at], PLAIN)
            ).astype(BF16)

    grad_keys, grad_values = call(
        last, [((rows, feats), BF16)] * 2,
        gk_local, gv_local, keys, values, *got_adjoint,
    )
    return out_y, grad_queries, grad_keys, grad_values, grad_weight


def solution(mesh):
    placed = (
        P(("groups", "seq"), "head"),
        P(("groups", "seq"), "head"),
        P(("groups", "seq"), "head"),
        P("seq", "head"),
        P(("groups", "seq"), None),
    )
    size = dict(mesh.shape)

    def program(queries, keys, values, out_weight, grad_y):
        short = size["seq"] == 8 and size["groups"] == 2 and size["head"] == 2
        if short and queries.shape[0] == TILE and out_weight.shape[0] % 256 == 0:
            return on_short_line(
                size["seq"], queries, keys, values, out_weight, grad_y
            )
        return on_device(queries, keys, values, out_weight, grad_y)

    return jax.shard_map(
        program,
        mesh=mesh,
        in_specs=placed,
        out_specs=(
            P(("groups", "seq"), None),
            P(("groups", "seq"), "head"),
            P(("groups", "seq"), "head"),
            P(("groups", "seq"), "head"),
            P(("groups", "seq"), "head"),
        ),
        check_vma=False,
    )
```

```python
import jax
import jax.numpy as jnp
from jax import lax
from jax.experimental import pallas as pl
from jax.experimental.pallas import tpu as pltpu
from jax.sharding import PartitionSpec as P

DH = 128
TILE = 128


epsilon = 1e-06
F32 = jnp.float32
BF16 = jnp.bfloat16
ROWS_T = (((0,), (0,)), ((), ()))
LAST_T = (((1,), (1,)), ((), ()))
LIGHT = 2**20
PLAIN = (((1,), (0,)), ((), ()))


def carried_in(value, axis, join, neutral, backward):
    count, mine = (lax.axis_size(axis), lax.axis_index(axis))
    pieces = lax.all_gather(value, axis)
    if backward:
        pieces = pieces[::-1]
        mine = count - 1 - mine
    so_far = jnp.full_like(value, 0) + jnp.asarray(neutral, value.dtype)

    def turn(position, so_far):
        longer = join(so_far, pieces[position])
        return jnp.where(position < mine, longer, so_far)

    return lax.fori_loop(0, count - 1, turn, so_far)


def add_states(earlier, later):
    return earlier + later


def on_device(queries, keys, values, out_weight, grad_y):
    row_count = queries.shape[0]
    tile_count = row_count // TILE
    head_count = queries.shape[1] // DH

    def tiled(array):
        return array.reshape(tile_count, TILE, head_count, DH)

    query_tiles = tiled(queries)
    key_tiles = tiled(keys)
    value_tiles = tiled(values)
    causal = lax.broadcasted_iota(jnp.int32, (TILE, TILE), 0) >= lax.broadcasted_iota(
        jnp.int32, (TILE, TILE), 1
    )
    raw_scores = jnp.einsum(
        "nthd,nshd->nhts", query_tiles, key_tiles, preferred_element_type=jnp.float32
    )
    scores = jnp.where(causal, raw_scores, 0.0).astype(jnp.bfloat16)
    states = jnp.einsum(
        "nshd,nshe->nhde", key_tiles, value_tiles, preferred_element_type=jnp.float32
    )
    empty_state = jnp.zeros(states.shape[1:], jnp.float32)
    device_prefix = carried_in(jnp.sum(states, axis=0), "seq", add_states, empty_state, False)
    prefix_state = (device_prefix[None] + (jnp.cumsum(states, axis=0) - states)).astype(
        jnp.bfloat16
    )
    attended = jnp.einsum(
        "nhts,nshe->nthe", scores, value_tiles, preferred_element_type=jnp.float32
    )
    attended = attended + jnp.einsum(
        "nthd,nhde->nthe", query_tiles, prefix_state, preferred_element_type=jnp.float32
    )
    inverse_rms = lax.rsqrt(jnp.mean(attended * attended, axis=-1, keepdims=True) + epsilon)
    normed_exact = attended * inverse_rms
    normed = normed_exact.astype(jnp.bfloat16).reshape(row_count, -1)
    back_weight = lax.all_gather(out_weight, "seq", axis=0, tiled=True)
    grad_normed = jnp.dot(grad_y, back_weight, preferred_element_type=jnp.float32)
    fore_weight = lax.all_gather(out_weight, "seq", axis=0, tiled=True)
    partial_out = lax.dot_general(
        normed, fore_weight, LAST_T, preferred_element_type=jnp.float32
    )
    out_y = lax.psum(partial_out.astype(jnp.bfloat16), "head")
    grad_tiles = tiled(grad_normed)
    projected = jnp.mean(grad_tiles * normed_exact, axis=-1, keepdims=True)
    grad_out = (inverse_rms * (grad_tiles - normed_exact * projected)).astype(jnp.bfloat16)
    raw_grad = jnp.einsum(
        "nthe,nshe->nhts", grad_out, value_tiles, preferred_element_type=jnp.float32
    )
    grad_scores = jnp.where(causal, raw_grad, 0.0).astype(jnp.bfloat16)
    adjoint = jnp.einsum(
        "nthd,nthe->nhde", query_tiles, grad_out, preferred_element_type=jnp.float32
    )
    own_adjoint = jnp.sum(adjoint, axis=0)
    device_suffix = carried_in(own_adjoint, "seq", add_states, empty_state, True)
    later_tiles = jnp.flip(jnp.cumsum(jnp.flip(adjoint, 0), axis=0), 0) - adjoint
    suffix_state = (device_suffix[None] + later_tiles).astype(jnp.bfloat16)
    grad_queries = jnp.einsum(
        "nhts,nshd->nthd", grad_scores, key_tiles, preferred_element_type=jnp.float32
    )
    grad_queries = grad_queries + jnp.einsum(
        "nthe,nhde->nthd", grad_out, prefix_state, preferred_element_type=jnp.float32
    )
    grad_keys = jnp.einsum(
        "nhts,nthd->nshd", grad_scores, query_tiles, preferred_element_type=jnp.float32
    )
    grad_keys = grad_keys + jnp.einsum(
        "nshe,nhde->nshd", value_tiles, suffix_state, preferred_element_type=jnp.float32
    )
    grad_values = jnp.einsum(
        "nhts,nthe->nshe", scores, grad_out, preferred_element_type=jnp.float32
    )
    grad_values = grad_values + jnp.einsum(
        "nshd,nhde->nshe", key_tiles, suffix_state, preferred_element_type=jnp.float32
    )
    grad_weight = lax.psum_scatter(
        lax.dot_general(
            grad_y, normed, (((0,), (0,)), ((), ())), preferred_element_type=jnp.float32
        ),
        "seq",
        scatter_dimension=0,
        tiled=True,
    )
    return (
        out_y,
        grad_queries.reshape(row_count, -1).astype(jnp.bfloat16),
        grad_keys.reshape(row_count, -1).astype(jnp.bfloat16),
        grad_values.reshape(row_count, -1).astype(jnp.bfloat16),
        grad_weight,
    )


def dot(a, b, dims):
    return lax.dot_general(a, b, dims, preferred_element_type=F32)


def call(body, shapes, *args, flops=1000000000, moved=2**20):
    return pl.pallas_call(
        body,
        out_shape=[jax.ShapeDtypeStruct(s, d) for s, d in shapes],
        in_specs=[pl.BlockSpec(memory_space=pltpu.VMEM)] * len(args),
        out_specs=[pl.BlockSpec(memory_space=pltpu.VMEM)] * len(shapes),
        cost_estimate=pl.CostEstimate(
            flops=flops, bytes_accessed=moved, transcendentals=0
        ),
        compiler_params=pltpu.CompilerParams(vmem_limit_bytes=24 * 2**20),
    )(*args)


def lanes(i, size):
    return pl.ds(pl.multiple_of(i * size, size), size)


def head_of(i):
    return slice(i * DH, (i + 1) * DH)


def causal_mask():
    rows = lax.broadcasted_iota(jnp.int32, (TILE, TILE), 0)
    return rows >= lax.broadcasted_iota(jnp.int32, (TILE, TILE), 1)


def place():
    s = lax.axis_index("seq")
    return lax.axis_index("groups"), s // 2, s % 2, lax.axis_index("head")


def on_short_line(seq, queries, keys, values, out_weight, grad_y):
    rows, feats = queries.shape
    heads = feats // DH
    wrows = out_weight.shape[0]
    half = wrows // 2
    line = seq // 2
    turns = range(1, line)
    outs = grad_y.shape[1]
    state = (DH, heads * DH)

    def permute(array, pairs):
        return lax.ppermute(array, "seq", pairs)

    def rotate(array, k):
        return permute(array, [(i, (i + 2 * k) % seq) for i in range(seq)])

    def swap(array, bit):
        return permute(array, [(i, i ^ bit) for i in range(seq)])

    def swap_y(array):
        return lax.ppermute(array, "groups", [(0, 1), (1, 0)])

    def swap_core(array):
        return lax.ppermute(array, "head", [(0, 1), (1, 0)])

    def side_by_side(*arrays):
        return jnp.concatenate(arrays, axis=0)

    def tie(*arrays):
        return lax.optimization_barrier(arrays)

    g = lax.axis_index("groups")
    my_weight = lax.dynamic_slice_in_dim(out_weight, g * half, half, 0)
    z_weight = [rotate(my_weight, k) for k in turns]

    def own_state(k_ref, v_ref, w_ref, out_ref):
        out_ref[:half, :] = w_ref[...]
        for i in range(heads):
            out_ref[half:, head_of(i)] = dot(
                k_ref[:, head_of(i)], v_ref[:, head_of(i)], ROWS_T
            ).astype(BF16)

    (weight_states,) = call(
        own_state, [((half + DH, feats), BF16)], keys, values, my_weight
    )
    x_weight_states = swap(weight_states, 1)
    states, x_states = weight_states[half:], x_weight_states[half:]

    def columns(gy_ref, z, h):
        return gy_ref[:, lanes(z * 2 + h, wrows)]

    def pack(gy_ref, ys_ref, near_ref):
        g, z, x, h = place()
        for i in range(seq):
            ys_ref[:, i * half : (i + 1) * half] = gy_ref[:, lanes(2 * i + 1 - g, half)]
        near = z + 1 - 2 * lax.rem(z, 2)
        near_ref[:rows, :] = columns(gy_ref, near, h)
        near_ref[rows:, :] = columns(gy_ref, lax.rem(near + 2, line), h)

    y_send, near_send = call(
        pack, [((rows, seq * half), BF16), ((2 * rows, wrows), BF16)], grad_y
    )
    near_cols = swap(near_send, 2)
    y_cols = swap_y(y_send)

    def local(q_ref, k_ref, v_ref, sc_ref, att_ref):
        mask = causal_mask()
        for i in range(heads):
            sc = dot(q_ref[:, head_of(i)], k_ref[:, head_of(i)], LAST_T)
            sc = jnp.where(mask, sc, 0.0).astype(BF16)
            sc_ref[:, head_of(i)] = sc
            att_ref[:, head_of(i)] = dot(sc, v_ref[:, head_of(i)], PLAIN)

    scores, att_local = call(
        local, [((rows, feats), BF16), ((rows, feats), F32)], queries, keys, values
    )

    def add(a, b):
        return (a.astype(F32) + b.astype(F32)).astype(BF16)

    pair_states = add(states, x_states)
    near_states = swap(pair_states, 2)
    pair_states, *z_weight = tie(pair_states, *z_weight)
    near_states, near_cols, y_cols = tie(near_states, near_cols, y_cols)
    quad_states = add(pair_states, near_states)
    got_states = x_states, near_states, swap(quad_states, 4)

    x_weight = swap(side_by_side(*z_weight), 1)
    near_cols, quad_states = tie(near_cols, quad_states)

    def relay(gy_ref, near_ref, far_ref):
        g, z, x, h = place()
        far_ref[:rows, :] = columns(gy_ref, lax.rem(z + 2, line), h)
        far_ref[rows:, :] = near_ref[rows:, :]

    (far_send,) = call(relay, [((2 * rows, wrows), BF16)], grad_y, near_cols)

    far_cols = swap(far_send, 4)

    def weight_blocks(refs):
        own, *others, x_own, x_others = refs
        g, z, x, h = place()
        blocks = []
        for k in range(line):
            zk = lax.rem(z - k + line, line)
            blocks.append((zk * 2 + x, (own, *others)[k][...]))
            if k == 0:
                block = x_own[:half, :]
            else:
                block = x_others[(k - 1) * half : k * half, :]
            blocks.append((zk * 2 + 1 - x, block))
        return blocks

    weight_args = (my_weight, *z_weight, x_weight_states, x_weight)

    def back_other(yc_ref, *refs):
        *w_refs, out_ref = refs
        total = jnp.zeros((rows, feats), F32)
        for s, block in weight_blocks(w_refs):
            total += dot(yc_ref[:, lanes(s, half)], block, PLAIN)
        out_ref[...] = total

    def back_own(gy_ref, *refs):
        *w_refs, out_ref = refs
        g = lax.axis_index("groups")
        total = jnp.zeros((rows, feats), F32)
        for s, block in weight_blocks(w_refs):
            total += dot(gy_ref[:, lanes(2 * s + g, half)], block, PLAIN)
        out_ref[...] = total

    (grad_send,) = call(
        back_other, [((rows, feats), F32)], y_cols, *weight_args
    )
    grad_other = swap_y(grad_send)
    (grad_own,) = call(
        back_own, [((rows, feats), F32)], grad_y, *weight_args
    )

    def forward(q_ref, local_ref, x_ref, near_ref, far_ref, att_ref, normed_ref, prefix_ref):
        g, z, x, h = place()
        total = jnp.where(x == 1, x_ref[...].astype(F32), 0.0)
        total += jnp.where(lax.rem(z, 2) == 1, near_ref[...].astype(F32), 0.0)
        total += jnp.where(z >= 2, far_ref[...].astype(F32), 0.0)
        prefix = total.astype(BF16)
        prefix_ref[...] = prefix
        for i in range(heads):
            att = local_ref[:, head_of(i)] + dot(
                q_ref[:, head_of(i)], prefix[:, head_of(i)], PLAIN
            )
            att_ref[:, head_of(i)] = att
            inv = lax.rsqrt(jnp.mean(att * att, axis=-1, keepdims=True) + epsilon)
            normed_ref[:, head_of(i)] = (att * inv).astype(BF16)

    attended, normed, prefix = call(
        forward,
        [((rows, feats), F32), ((rows, feats), BF16), (state, BF16)],
        queries, att_local, *got_states,
    )
    far_cols, normed = tie(far_cols, normed)
    y_normed = swap_y(normed)
    far_normed = swap(normed, 4)

    def turn_back(att_ref, own_ref, other_ref, q_ref, go_ref, adj_ref):
        for i in range(heads):
            att = att_ref[:, head_of(i)]
            inv = lax.rsqrt(jnp.mean(att * att, axis=-1, keepdims=True) + epsilon)
            exact = att * inv
            grad = own_ref[:, head_of(i)] + other_ref[:, head_of(i)]
            along = jnp.mean(grad * exact, axis=-1, keepdims=True)
            go = (inv * (grad - exact * along)).astype(BF16)
            go_ref[:, head_of(i)] = go
            adj_ref[:, head_of(i)] = dot(q_ref[:, head_of(i)], go, ROWS_T).astype(BF16)

    grad_out, adjoint = call(
        turn_back, [((rows, feats), BF16), (state, BF16)],
        attended, grad_own, grad_other, queries,
    )
    my_cols = side_by_side(near_cols[:rows], far_cols)
    core_cols = swap_core(my_cols)

    near_normed = swap(normed, 2)
    x_adjoint, near_normed, far_normed, core_cols = tie(
        swap(adjoint, 1), near_normed, far_normed, core_cols
    )
    def project(n_ref, yn_ref, *refs):
        *w_refs, own_ref, other_ref = refs
        for s, block in weight_blocks(w_refs):
            own_ref[:, lanes(s, half)] = dot(n_ref[...], block, LAST_T).astype(BF16)
            other_ref[:, lanes(s, half)] = dot(yn_ref[...], block, LAST_T).astype(BF16)

    out_own, out_send = call(
        project, [((rows, seq * half), BF16)] * 2, normed, y_normed, *weight_args
    )
    out_other = swap_y(out_send)
    last_normed = swap(far_normed, 2)
    pair_adjoint = add(adjoint, x_adjoint)
    near_adjoint = swap(pair_adjoint, 2)
    def local_grads(go_ref, q_ref, k_ref, v_ref, sc_ref, pre_ref, gq_ref, gk_ref, gv_ref):
        mask = causal_mask()
        for i in range(heads):
            at = head_of(i)
            go = go_ref[:, at]
            gs = dot(go, v_ref[:, at], LAST_T)
            gs = jnp.where(mask, gs, 0.0).astype(BF16)
            gq = dot(gs, k_ref[:, at], PLAIN) + dot(go, pre_ref[:, at], LAST_T)
            gq_ref[:, at] = gq.astype(BF16)
            gk_ref[:, at] = dot(gs, q_ref[:, at], ROWS_T)
            gv_ref[:, at] = dot(sc_ref[:, at], go, ROWS_T)

    grad_queries, gk_local, gv_local = call(
        local_grads,
        [((rows, feats), BF16), ((rows, feats), F32), ((rows, feats), F32)],
        grad_out, queries, keys, values, scores, prefix,
        flops=LIGHT,
    )

    near_adjoint, last_normed, out_other, gk_local = tie(
        near_adjoint, last_normed, out_other, gk_local
    )
    quad_adjoint = add(pair_adjoint, near_adjoint)
    far_adjoint = swap(quad_adjoint, 4)
    quad_adjoint, last_normed = tie(quad_adjoint, last_normed)

    core_own = swap_core(out_own)
    core_other = swap_core(out_other)

    def weight_grad(gy_ref, c_ref, o_ref, n_ref, *refs):
        *n_refs, keep_ref, send_ref = refs
        g, z, x, h = place()
        same = dot(columns(gy_ref, z, h), n_ref[...], ROWS_T)
        other = dot(columns(gy_ref, z, 1 - h), n_ref[...], ROWS_T)
        for i, there_ref in enumerate(n_refs):
            at = slice(i * rows, (i + 1) * rows)
            same += dot(c_ref[at, :], there_ref[...], ROWS_T)
            other += dot(o_ref[at, :], there_ref[...], ROWS_T)
        keep_ref[...] = jnp.where(x == h, same, other)
        send_ref[...] = jnp.where(x == h, other, same).astype(BF16)

    gw_keep, gw_send = call(
        weight_grad, [((wrows, feats), F32), ((wrows, feats), BF16)],
        grad_y, my_cols, core_cols, normed, near_normed, far_normed, last_normed,
        flops=LIGHT,
    )
    gw_other = swap(gw_send, 1)

    def join(a_ref, b_ref, c_ref, d_ref, y_ref):
        g = lax.axis_index("groups")
        for i in range(seq):
            at = slice(i * half, (i + 1) * half)
            y_ref[:, lanes(2 * i + g, half)] = (
                a_ref[:, at].astype(F32) + b_ref[:, at].astype(F32)
            ).astype(BF16)
            y_ref[:, lanes(2 * i + 1 - g, half)] = (
                c_ref[:, at].astype(F32) + d_ref[:, at].astype(F32)
            ).astype(BF16)

    (out_y,) = call(
        join, [((rows, outs), BF16)], out_own, core_own, out_other, core_other,
        flops=LIGHT,
    )
    grad_weight = gw_keep + gw_other.astype(F32)

    far_adjoint, out_y, grad_weight = tie(far_adjoint, out_y, grad_weight)

    def last(gk_ref, gv_ref, k_ref, v_ref, x_ref, near_ref, far_ref, ok_ref, ov_ref):
        g, z, x, h = place()
        total = jnp.where(x == 0, x_ref[...].astype(F32), 0.0)
        total += jnp.where(lax.rem(z, 2) == 0, near_ref[...].astype(F32), 0.0)
        total += jnp.where(z < 2, far_ref[...].astype(F32), 0.0)
        suffix = total.astype(BF16)
        for i in range(heads):
            at = head_of(i)
            ok_ref[:, at] = (
                gk_ref[:, at] + dot(v_ref[:, at], suffix[:, at], LAST_T)
            ).astype(BF16)
            ov_ref[:, at] = (
                gv_ref[:, at] + dot(k_ref[:, at], suffix[:, at], PLAIN)
            ).astype(BF16)

    grad_keys, grad_values = call(
        last, [((rows, feats), BF16)] * 2,
        gk_local, gv_local, keys, values, x_adjoint, near_adjoint, far_adjoint,
    )
    return out_y, grad_queries, grad_keys, grad_values, grad_weight


def solution(mesh):
    placed = (
        P(("groups", "seq"), "head"),
        P(("groups", "seq"), "head"),
        P(("groups", "seq"), "head"),
        P("seq", "head"),
        P(("groups", "seq"), None),
    )
    size = dict(mesh.shape)

    def program(queries, keys, values, out_weight, grad_y):
        short = size["seq"] == 8 and size["groups"] == 2 and size["head"] == 2
        if short and queries.shape[0] == TILE and out_weight.shape[0] % 256 == 0:
            return on_short_line(
                size["seq"], queries, keys, values, out_weight, grad_y
            )
        return on_device(queries, keys, values, out_weight, grad_y)

    return jax.shard_map(
        program,
        mesh=mesh,
        in_specs=placed,
        out_specs=(
            P(("groups", "seq"), None),
            P(("groups", "seq"), "head"),
            P(("groups", "seq"), "head"),
            P(("groups", "seq"), "head"),
            P(("groups", "seq"), "head"),
        ),
        check_vma=False,
    )
```

```python
import jax
import jax.numpy as jnp
from jax import lax
from jax.experimental import pallas as pl
from jax.experimental.pallas import tpu as pltpu
from jax.sharding import PartitionSpec as P

DH = 128
TILE = 128


epsilon = 1e-06
F32 = jnp.float32
BF16 = jnp.bfloat16
ROWS_T = (((0,), (0,)), ((), ()))
LAST_T = (((1,), (1,)), ((), ()))
HINTS = {
    "own_state": 1000000000,
    "pack": 3000000000,
    "local": 1000000000,
    "back_other": 1000000000,
    "back_own": 1000000000,
    "forward": 3000000000,
    "turn_back": 1000000000,
    "relay": 1000000000,
    "project": 3000000000,
    "local_grads": 1048576,
    "weight_grad": 1048576,
    "join": 1048576,
    "last": 3000000000,
}
PLAIN = (((1,), (0,)), ((), ()))


def carried_in(value, axis, join, neutral, backward):
    count, mine = (lax.axis_size(axis), lax.axis_index(axis))
    pieces = lax.all_gather(value, axis)
    if backward:
        pieces = pieces[::-1]
        mine = count - 1 - mine
    so_far = jnp.full_like(value, 0) + jnp.asarray(neutral, value.dtype)

    def turn(position, so_far):
        longer = join(so_far, pieces[position])
        return jnp.where(position < mine, longer, so_far)

    return lax.fori_loop(0, count - 1, turn, so_far)


def add_states(earlier, later):
    return earlier + later


def on_device(queries, keys, values, out_weight, grad_y):
    row_count = queries.shape[0]
    tile_count = row_count // TILE
    head_count = queries.shape[1] // DH

    def tiled(array):
        return array.reshape(tile_count, TILE, head_count, DH)

    query_tiles = tiled(queries)
    key_tiles = tiled(keys)
    value_tiles = tiled(values)
    causal = lax.broadcasted_iota(jnp.int32, (TILE, TILE), 0) >= lax.broadcasted_iota(
        jnp.int32, (TILE, TILE), 1
    )
    raw_scores = jnp.einsum(
        "nthd,nshd->nhts", query_tiles, key_tiles, preferred_element_type=jnp.float32
    )
    scores = jnp.where(causal, raw_scores, 0.0).astype(jnp.bfloat16)
    states = jnp.einsum(
        "nshd,nshe->nhde", key_tiles, value_tiles, preferred_element_type=jnp.float32
    )
    empty_state = jnp.zeros(states.shape[1:], jnp.float32)
    device_prefix = carried_in(jnp.sum(states, axis=0), "seq", add_states, empty_state, False)
    prefix_state = (device_prefix[None] + (jnp.cumsum(states, axis=0) - states)).astype(
        jnp.bfloat16
    )
    attended = jnp.einsum(
        "nhts,nshe->nthe", scores, value_tiles, preferred_element_type=jnp.float32
    )
    attended = attended + jnp.einsum(
        "nthd,nhde->nthe", query_tiles, prefix_state, preferred_element_type=jnp.float32
    )
    inverse_rms = lax.rsqrt(jnp.mean(attended * attended, axis=-1, keepdims=True) + epsilon)
    normed_exact = attended * inverse_rms
    normed = normed_exact.astype(jnp.bfloat16).reshape(row_count, -1)
    back_weight = lax.all_gather(out_weight, "seq", axis=0, tiled=True)
    grad_normed = jnp.dot(grad_y, back_weight, preferred_element_type=jnp.float32)
    fore_weight = lax.all_gather(out_weight, "seq", axis=0, tiled=True)
    partial_out = lax.dot_general(
        normed, fore_weight, LAST_T, preferred_element_type=jnp.float32
    )
    out_y = lax.psum(partial_out.astype(jnp.bfloat16), "head")
    grad_tiles = tiled(grad_normed)
    projected = jnp.mean(grad_tiles * normed_exact, axis=-1, keepdims=True)
    grad_out = (inverse_rms * (grad_tiles - normed_exact * projected)).astype(jnp.bfloat16)
    raw_grad = jnp.einsum(
        "nthe,nshe->nhts", grad_out, value_tiles, preferred_element_type=jnp.float32
    )
    grad_scores = jnp.where(causal, raw_grad, 0.0).astype(jnp.bfloat16)
    adjoint = jnp.einsum(
        "nthd,nthe->nhde", query_tiles, grad_out, preferred_element_type=jnp.float32
    )
    own_adjoint = jnp.sum(adjoint, axis=0)
    device_suffix = carried_in(own_adjoint, "seq", add_states, empty_state, True)
    later_tiles = jnp.flip(jnp.cumsum(jnp.flip(adjoint, 0), axis=0), 0) - adjoint
    suffix_state = (device_suffix[None] + later_tiles).astype(jnp.bfloat16)
    grad_queries = jnp.einsum(
        "nhts,nshd->nthd", grad_scores, key_tiles, preferred_element_type=jnp.float32
    )
    grad_queries = grad_queries + jnp.einsum(
        "nthe,nhde->nthd", grad_out, prefix_state, preferred_element_type=jnp.float32
    )
    grad_keys = jnp.einsum(
        "nhts,nthd->nshd", grad_scores, query_tiles, preferred_element_type=jnp.float32
    )
    grad_keys = grad_keys + jnp.einsum(
        "nshe,nhde->nshd", value_tiles, suffix_state, preferred_element_type=jnp.float32
    )
    grad_values = jnp.einsum(
        "nhts,nthe->nshe", scores, grad_out, preferred_element_type=jnp.float32
    )
    grad_values = grad_values + jnp.einsum(
        "nshd,nhde->nshe", key_tiles, suffix_state, preferred_element_type=jnp.float32
    )
    grad_weight = lax.psum_scatter(
        lax.dot_general(
            grad_y, normed, (((0,), (0,)), ((), ())), preferred_element_type=jnp.float32
        ),
        "seq",
        scatter_dimension=0,
        tiled=True,
    )
    return (
        out_y,
        grad_queries.reshape(row_count, -1).astype(jnp.bfloat16),
        grad_keys.reshape(row_count, -1).astype(jnp.bfloat16),
        grad_values.reshape(row_count, -1).astype(jnp.bfloat16),
        grad_weight,
    )


def dot(a, b, dims):
    return lax.dot_general(a, b, dims, preferred_element_type=F32)


def call(body, shapes, *args):
    return pl.pallas_call(
        body,
        out_shape=[jax.ShapeDtypeStruct(s, d) for s, d in shapes],
        in_specs=[pl.BlockSpec(memory_space=pltpu.VMEM)] * len(args),
        out_specs=[pl.BlockSpec(memory_space=pltpu.VMEM)] * len(shapes),
        cost_estimate=pl.CostEstimate(
            flops=HINTS[body.__name__], bytes_accessed=2**20, transcendentals=0
        ),
        compiler_params=pltpu.CompilerParams(vmem_limit_bytes=24 * 2**20),
    )(*args)


def lanes(i, size):
    return pl.ds(pl.multiple_of(i * size, size), size)


def head_of(i):
    return slice(i * DH, (i + 1) * DH)


def causal_mask():
    rows = lax.broadcasted_iota(jnp.int32, (TILE, TILE), 0)
    return rows >= lax.broadcasted_iota(jnp.int32, (TILE, TILE), 1)


def place():
    s = lax.axis_index("seq")
    return lax.axis_index("groups"), s // 2, s % 2, lax.axis_index("head")


def on_short_line(seq, queries, keys, values, out_weight, grad_y):
    rows, feats = queries.shape
    heads = feats // DH
    wrows = out_weight.shape[0]
    half = wrows // 2
    line = seq // 2
    turns = range(1, line)
    outs = grad_y.shape[1]
    state = (DH, heads * DH)

    def permute(array, pairs):
        return lax.ppermute(array, "seq", pairs)

    def rotate(array, k):
        return permute(array, [(i, (i + 2 * k) % seq) for i in range(seq)])

    def swap(array, bit):
        return permute(array, [(i, i ^ bit) for i in range(seq)])

    def swap_y(array):
        return lax.ppermute(array, "groups", [(0, 1), (1, 0)])

    def swap_core(array):
        return lax.ppermute(array, "head", [(0, 1), (1, 0)])

    def side_by_side(*arrays):
        return jnp.concatenate(arrays, axis=0)

    def tie(*arrays):
        return lax.optimization_barrier(arrays)

    g = lax.axis_index("groups")
    my_weight = lax.dynamic_slice_in_dim(out_weight, g * half, half, 0)
    z_weight = [rotate(my_weight, k) for k in turns]

    def own_state(k_ref, v_ref, w_ref, out_ref):
        out_ref[:half, :] = w_ref[...]
        for i in range(heads):
            out_ref[half:, head_of(i)] = dot(
                k_ref[:, head_of(i)], v_ref[:, head_of(i)], ROWS_T
            ).astype(BF16)

    (weight_states,) = call(
        own_state, [((half + DH, feats), BF16)], keys, values, my_weight
    )
    x_weight_states = swap(weight_states, 1)
    states, x_states = weight_states[half:], x_weight_states[half:]

    def columns(gy_ref, z, h):
        return gy_ref[:, lanes(z * 2 + h, wrows)]

    def pack(gy_ref, ys_ref, near_ref):
        g, z, x, h = place()
        for i in range(seq):
            ys_ref[:, i * half : (i + 1) * half] = gy_ref[:, lanes(2 * i + 1 - g, half)]
        near = z + 1 - 2 * lax.rem(z, 2)
        near_ref[:rows, :] = columns(gy_ref, near, h)
        near_ref[rows:, :] = columns(gy_ref, lax.rem(near + 2, line), h)

    y_send, near_send = call(
        pack, [((rows, seq * half), BF16), ((2 * rows, wrows), BF16)], grad_y
    )
    near_cols = swap(near_send, 2)
    y_cols = swap_y(y_send)

    def local(q_ref, k_ref, v_ref, sc_ref, att_ref):
        mask = causal_mask()
        for i in range(heads):
            sc = dot(q_ref[:, head_of(i)], k_ref[:, head_of(i)], LAST_T)
            sc = jnp.where(mask, sc, 0.0).astype(BF16)
            sc_ref[:, head_of(i)] = sc
            att_ref[:, head_of(i)] = dot(sc, v_ref[:, head_of(i)], PLAIN)

    scores, att_local = call(
        local, [((rows, feats), BF16), ((rows, feats), F32)], queries, keys, values
    )

    def add(a, b):
        return (a.astype(F32) + b.astype(F32)).astype(BF16)

    pair_states = add(states, x_states)
    near_states = swap(pair_states, 2)
    pair_states, *z_weight = tie(pair_states, *z_weight)
    near_states, y_cols = tie(near_states, y_cols)
    quad_states = add(pair_states, near_states)
    got_states = x_states, near_states, swap(quad_states, 4)

    x_weight = swap(side_by_side(*z_weight), 1)

    def weight_blocks(refs):
        own, *others, x_own, x_others = refs
        g, z, x, h = place()
        blocks = []
        for k in range(line):
            zk = lax.rem(z - k + line, line)
            blocks.append((zk * 2 + x, (own, *others)[k][...]))
            if k == 0:
                block = x_own[:half, :]
            else:
                block = x_others[(k - 1) * half : k * half, :]
            blocks.append((zk * 2 + 1 - x, block))
        return blocks

    weight_args = (my_weight, *z_weight, x_weight_states, x_weight)

    def back_other(yc_ref, *refs):
        *w_refs, out_ref = refs
        total = jnp.zeros((rows, feats), F32)
        for s, block in weight_blocks(w_refs):
            total += dot(yc_ref[:, lanes(s, half)], block, PLAIN)
        out_ref[...] = total

    def back_own(gy_ref, *refs):
        *w_refs, out_ref = refs
        g = lax.axis_index("groups")
        total = jnp.zeros((rows, feats), F32)
        for s, block in weight_blocks(w_refs):
            total += dot(gy_ref[:, lanes(2 * s + g, half)], block, PLAIN)
        out_ref[...] = total

    (grad_send,) = call(
        back_other, [((rows, feats), F32)], y_cols, *weight_args
    )
    grad_other = swap_y(grad_send)
    (grad_own,) = call(
        back_own, [((rows, feats), F32)], grad_y, *weight_args
    )

    def forward(q_ref, local_ref, x_ref, near_ref, far_ref, att_ref, normed_ref, prefix_ref):
        g, z, x, h = place()
        total = jnp.where(x == 1, x_ref[...].astype(F32), 0.0)
        total += jnp.where(lax.rem(z, 2) == 1, near_ref[...].astype(F32), 0.0)
        total += jnp.where(z >= 2, far_ref[...].astype(F32), 0.0)
        prefix = total.astype(BF16)
        prefix_ref[...] = prefix
        for i in range(heads):
            att = local_ref[:, head_of(i)] + dot(
                q_ref[:, head_of(i)], prefix[:, head_of(i)], PLAIN
            )
            att_ref[:, head_of(i)] = att
            inv = lax.rsqrt(jnp.mean(att * att, axis=-1, keepdims=True) + epsilon)
            normed_ref[:, head_of(i)] = (att * inv).astype(BF16)

    attended, normed, prefix = call(
        forward,
        [((rows, feats), F32), ((rows, feats), BF16), (state, BF16)],
        queries, att_local, *got_states,
    )
    y_normed = swap_y(normed)
    far_normed = swap(normed, 4)

    def turn_back(att_ref, own_ref, other_ref, q_ref, go_ref, adj_ref):
        for i in range(heads):
            att = att_ref[:, head_of(i)]
            inv = lax.rsqrt(jnp.mean(att * att, axis=-1, keepdims=True) + epsilon)
            exact = att * inv
            grad = own_ref[:, head_of(i)] + other_ref[:, head_of(i)]
            along = jnp.mean(grad * exact, axis=-1, keepdims=True)
            go = (inv * (grad - exact * along)).astype(BF16)
            go_ref[:, head_of(i)] = go
            adj_ref[:, head_of(i)] = dot(q_ref[:, head_of(i)], go, ROWS_T).astype(BF16)

    grad_out, adjoint = call(
        turn_back, [((rows, feats), BF16), (state, BF16)],
        attended, grad_own, grad_other, queries,
    )
    near_normed = swap(normed, 2)
    x_adjoint = swap(adjoint, 1)
    near_cols, adjoint = tie(near_cols, adjoint)

    def relay(gy_ref, near_ref, far_ref):
        g, z, x, h = place()
        far_ref[:rows, :] = columns(gy_ref, lax.rem(z + 2, line), h)
        far_ref[rows:, :] = near_ref[rows:, :]

    (far_send,) = call(relay, [((2 * rows, wrows), BF16)], grad_y, near_cols)

    far_cols = swap(far_send, 4)
    x_adjoint, near_normed, far_normed = tie(x_adjoint, near_normed, far_normed)
    def project(n_ref, yn_ref, *refs):
        *w_refs, own_ref, other_ref = refs
        for s, block in weight_blocks(w_refs):
            own_ref[:, lanes(s, half)] = dot(n_ref[...], block, LAST_T).astype(BF16)
            other_ref[:, lanes(s, half)] = dot(yn_ref[...], block, LAST_T).astype(BF16)

    out_own, out_send = call(
        project, [((rows, seq * half), BF16)] * 2, normed, y_normed, *weight_args
    )
    out_other = swap_y(out_send)
    last_normed = swap(far_normed, 2)
    pair_adjoint = add(adjoint, x_adjoint)
    near_adjoint = swap(pair_adjoint, 2)
    def local_grads(go_ref, q_ref, k_ref, v_ref, sc_ref, pre_ref, gq_ref, gk_ref, gv_ref):
        mask = causal_mask()
        for i in range(heads):
            at = head_of(i)
            go = go_ref[:, at]
            gs = dot(go, v_ref[:, at], LAST_T)
            gs = jnp.where(mask, gs, 0.0).astype(BF16)
            gq = dot(gs, k_ref[:, at], PLAIN) + dot(go, pre_ref[:, at], LAST_T)
            gq_ref[:, at] = gq.astype(BF16)
            gk_ref[:, at] = dot(gs, q_ref[:, at], ROWS_T)
            gv_ref[:, at] = dot(sc_ref[:, at], go, ROWS_T)

    grad_queries, gk_local, gv_local = call(
        local_grads,
        [((rows, feats), BF16), ((rows, feats), F32), ((rows, feats), F32)],
        grad_out, queries, keys, values, scores, prefix,
    )

    near_adjoint, last_normed, out_other, gk_local, far_cols = tie(
        near_adjoint, last_normed, out_other, gk_local, far_cols
    )
    my_cols = side_by_side(near_cols[:rows], far_cols)
    core_cols = swap_core(my_cols)

    quad_adjoint = add(pair_adjoint, near_adjoint)
    far_adjoint = swap(quad_adjoint, 4)
    quad_adjoint, last_normed = tie(quad_adjoint, last_normed)

    core_own = swap_core(out_own)
    core_other = swap_core(out_other)

    def weight_grad(gy_ref, c_ref, o_ref, n_ref, *refs):
        *n_refs, keep_ref, send_ref = refs
        g, z, x, h = place()
        same = dot(columns(gy_ref, z, h), n_ref[...], ROWS_T)
        other = dot(columns(gy_ref, z, 1 - h), n_ref[...], ROWS_T)
        for i, there_ref in enumerate(n_refs):
            at = slice(i * rows, (i + 1) * rows)
            same += dot(c_ref[at, :], there_ref[...], ROWS_T)
            other += dot(o_ref[at, :], there_ref[...], ROWS_T)
        keep_ref[...] = jnp.where(x == h, same, other)
        send_ref[...] = jnp.where(x == h, other, same).astype(BF16)

    gw_keep, gw_send = call(
        weight_grad, [((wrows, feats), F32), ((wrows, feats), BF16)],
        grad_y, my_cols, core_cols, normed, near_normed, far_normed, last_normed,
    )
    gw_other = swap(gw_send, 1)

    def join(a_ref, b_ref, c_ref, d_ref, y_ref):
        g = lax.axis_index("groups")
        for i in range(seq):
            at = slice(i * half, (i + 1) * half)
            y_ref[:, lanes(2 * i + g, half)] = (
                a_ref[:, at].astype(F32) + b_ref[:, at].astype(F32)
            ).astype(BF16)
            y_ref[:, lanes(2 * i + 1 - g, half)] = (
                c_ref[:, at].astype(F32) + d_ref[:, at].astype(F32)
            ).astype(BF16)

    (out_y,) = call(
        join, [((rows, outs), BF16)], out_own, core_own, out_other, core_other,
    )
    far_adjoint, out_y = tie(far_adjoint, out_y)

    def last(gk_ref, gv_ref, k_ref, v_ref, x_ref, near_ref, far_ref, ok_ref, ov_ref):
        g, z, x, h = place()
        total = jnp.where(x == 0, x_ref[...].astype(F32), 0.0)
        total += jnp.where(lax.rem(z, 2) == 0, near_ref[...].astype(F32), 0.0)
        total += jnp.where(z < 2, far_ref[...].astype(F32), 0.0)
        suffix = total.astype(BF16)
        for i in range(heads):
            at = head_of(i)
            ok_ref[:, at] = (
                gk_ref[:, at] + dot(v_ref[:, at], suffix[:, at], LAST_T)
            ).astype(BF16)
            ov_ref[:, at] = (
                gv_ref[:, at] + dot(k_ref[:, at], suffix[:, at], PLAIN)
            ).astype(BF16)

    grad_keys, grad_values = call(
        last, [((rows, feats), BF16)] * 2,
        gk_local, gv_local, keys, values, x_adjoint, near_adjoint, far_adjoint,
    )
    gw_other, grad_keys = tie(gw_other, grad_keys)
    grad_weight = gw_keep + gw_other.astype(F32)
    return out_y, grad_queries, grad_keys, grad_values, grad_weight


def solution(mesh):
    placed = (
        P(("groups", "seq"), "head"),
        P(("groups", "seq"), "head"),
        P(("groups", "seq"), "head"),
        P("seq", "head"),
        P(("groups", "seq"), None),
    )
    size = dict(mesh.shape)

    def program(queries, keys, values, out_weight, grad_y):
        short = size["seq"] == 8 and size["groups"] == 2 and size["head"] == 2
        if short and queries.shape[0] == TILE and out_weight.shape[0] % 256 == 0:
            return on_short_line(
                size["seq"], queries, keys, values, out_weight, grad_y
            )
        return on_device(queries, keys, values, out_weight, grad_y)

    return jax.shard_map(
        program,
        mesh=mesh,
        in_specs=placed,
        out_specs=(
            P(("groups", "seq"), None),
            P(("groups", "seq"), "head"),
            P(("groups", "seq"), "head"),
            P(("groups", "seq"), "head"),
            P(("groups", "seq"), "head"),
        ),
        check_vma=False,
    )
```

```python
import jax
import jax.numpy as jnp
from jax import lax
from jax.experimental import pallas as pl
from jax.experimental.pallas import tpu as pltpu
from jax.sharding import PartitionSpec as P

DH = 128
TILE = 128


epsilon = 1e-06
F32 = jnp.float32
BF16 = jnp.bfloat16
ROWS_T = (((0,), (0,)), ((), ()))
LAST_T = (((1,), (1,)), ((), ()))
HINTS = {
    "own_state": 300000000,
    "pack": 3000000000,
    "local": 1000000000,
    "back_other": 3000000000,
    "back_own": 1000000000,
    "forward": 3000000000,
    "turn_back": 600000000,
    "project": 3000000000,
    "local_grads": 1048576,
    "weight_grad": 1500000000,
    "join": 1048576,
    "last": 3000000000,
}
PLAIN = (((1,), (0,)), ((), ()))


def carried_in(value, axis, join, neutral, backward):
    count, mine = (lax.axis_size(axis), lax.axis_index(axis))
    pieces = lax.all_gather(value, axis)
    if backward:
        pieces = pieces[::-1]
        mine = count - 1 - mine
    so_far = jnp.full_like(value, 0) + jnp.asarray(neutral, value.dtype)

    def turn(position, so_far):
        longer = join(so_far, pieces[position])
        return jnp.where(position < mine, longer, so_far)

    return lax.fori_loop(0, count - 1, turn, so_far)


def add_states(earlier, later):
    return earlier + later


def on_device(queries, keys, values, out_weight, grad_y):
    row_count = queries.shape[0]
    tile_count = row_count // TILE
    head_count = queries.shape[1] // DH

    def tiled(array):
        return array.reshape(tile_count, TILE, head_count, DH)

    query_tiles = tiled(queries)
    key_tiles = tiled(keys)
    value_tiles = tiled(values)
    causal = lax.broadcasted_iota(jnp.int32, (TILE, TILE), 0) >= lax.broadcasted_iota(
        jnp.int32, (TILE, TILE), 1
    )
    raw_scores = jnp.einsum(
        "nthd,nshd->nhts", query_tiles, key_tiles, preferred_element_type=jnp.float32
    )
    scores = jnp.where(causal, raw_scores, 0.0).astype(jnp.bfloat16)
    states = jnp.einsum(
        "nshd,nshe->nhde", key_tiles, value_tiles, preferred_element_type=jnp.float32
    )
    empty_state = jnp.zeros(states.shape[1:], jnp.float32)
    device_prefix = carried_in(jnp.sum(states, axis=0), "seq", add_states, empty_state, False)
    prefix_state = (device_prefix[None] + (jnp.cumsum(states, axis=0) - states)).astype(
        jnp.bfloat16
    )
    attended = jnp.einsum(
        "nhts,nshe->nthe", scores, value_tiles, preferred_element_type=jnp.float32
    )
    attended = attended + jnp.einsum(
        "nthd,nhde->nthe", query_tiles, prefix_state, preferred_element_type=jnp.float32
    )
    inverse_rms = lax.rsqrt(jnp.mean(attended * attended, axis=-1, keepdims=True) + epsilon)
    normed_exact = attended * inverse_rms
    normed = normed_exact.astype(jnp.bfloat16).reshape(row_count, -1)
    back_weight = lax.all_gather(out_weight, "seq", axis=0, tiled=True)
    grad_normed = jnp.dot(grad_y, back_weight, preferred_element_type=jnp.float32)
    fore_weight = lax.all_gather(out_weight, "seq", axis=0, tiled=True)
    partial_out = lax.dot_general(
        normed, fore_weight, LAST_T, preferred_element_type=jnp.float32
    )
    out_y = lax.psum(partial_out.astype(jnp.bfloat16), "head")
    grad_tiles = tiled(grad_normed)
    projected = jnp.mean(grad_tiles * normed_exact, axis=-1, keepdims=True)
    grad_out = (inverse_rms * (grad_tiles - normed_exact * projected)).astype(jnp.bfloat16)
    raw_grad = jnp.einsum(
        "nthe,nshe->nhts", grad_out, value_tiles, preferred_element_type=jnp.float32
    )
    grad_scores = jnp.where(causal, raw_grad, 0.0).astype(jnp.bfloat16)
    adjoint = jnp.einsum(
        "nthd,nthe->nhde", query_tiles, grad_out, preferred_element_type=jnp.float32
    )
    own_adjoint = jnp.sum(adjoint, axis=0)
    device_suffix = carried_in(own_adjoint, "seq", add_states, empty_state, True)
    later_tiles = jnp.flip(jnp.cumsum(jnp.flip(adjoint, 0), axis=0), 0) - adjoint
    suffix_state = (device_suffix[None] + later_tiles).astype(jnp.bfloat16)
    grad_queries = jnp.einsum(
        "nhts,nshd->nthd", grad_scores, key_tiles, preferred_element_type=jnp.float32
    )
    grad_queries = grad_queries + jnp.einsum(
        "nthe,nhde->nthd", grad_out, prefix_state, preferred_element_type=jnp.float32
    )
    grad_keys = jnp.einsum(
        "nhts,nthd->nshd", grad_scores, query_tiles, preferred_element_type=jnp.float32
    )
    grad_keys = grad_keys + jnp.einsum(
        "nshe,nhde->nshd", value_tiles, suffix_state, preferred_element_type=jnp.float32
    )
    grad_values = jnp.einsum(
        "nhts,nthe->nshe", scores, grad_out, preferred_element_type=jnp.float32
    )
    grad_values = grad_values + jnp.einsum(
        "nshd,nhde->nshe", key_tiles, suffix_state, preferred_element_type=jnp.float32
    )
    grad_weight = lax.psum_scatter(
        lax.dot_general(
            grad_y, normed, (((0,), (0,)), ((), ())), preferred_element_type=jnp.float32
        ),
        "seq",
        scatter_dimension=0,
        tiled=True,
    )
    return (
        out_y,
        grad_queries.reshape(row_count, -1).astype(jnp.bfloat16),
        grad_keys.reshape(row_count, -1).astype(jnp.bfloat16),
        grad_values.reshape(row_count, -1).astype(jnp.bfloat16),
        grad_weight,
    )


def dot(a, b, dims):
    return lax.dot_general(a, b, dims, preferred_element_type=F32)


def call(body, shapes, *args):
    return pl.pallas_call(
        body,
        out_shape=[jax.ShapeDtypeStruct(s, d) for s, d in shapes],
        in_specs=[pl.BlockSpec(memory_space=pltpu.VMEM)] * len(args),
        out_specs=[pl.BlockSpec(memory_space=pltpu.VMEM)] * len(shapes),
        cost_estimate=pl.CostEstimate(
            flops=HINTS[body.__name__], bytes_accessed=2**20, transcendentals=0
        ),
        compiler_params=pltpu.CompilerParams(vmem_limit_bytes=24 * 2**20),
    )(*args)


def lanes(i, size):
    return pl.ds(pl.multiple_of(i * size, size), size)


def head_of(i):
    return slice(i * DH, (i + 1) * DH)


def causal_mask():
    rows = lax.broadcasted_iota(jnp.int32, (TILE, TILE), 0)
    return rows >= lax.broadcasted_iota(jnp.int32, (TILE, TILE), 1)


def place():
    s = lax.axis_index("seq")
    return lax.axis_index("groups"), s // 2, s % 2, lax.axis_index("head")


def on_short_line(seq, queries, keys, values, out_weight, grad_y):
    rows, feats = queries.shape
    heads = feats // DH
    wrows = out_weight.shape[0]
    half = wrows // 2
    line = seq // 2
    turns = range(1, line)
    outs = grad_y.shape[1]
    state = (DH, heads * DH)

    def permute(array, pairs):
        return lax.ppermute(array, "seq", pairs)

    def rotate(array, k):
        return permute(array, [(i, (i + 2 * k) % seq) for i in range(seq)])

    def swap(array, bit):
        return permute(array, [(i, i ^ bit) for i in range(seq)])

    def swap_y(array):
        return lax.ppermute(array, "groups", [(0, 1), (1, 0)])

    def swap_core(array):
        return lax.ppermute(array, "head", [(0, 1), (1, 0)])

    def side_by_side(*arrays):
        return jnp.concatenate(arrays, axis=0)

    def tie(*arrays):
        return lax.optimization_barrier(arrays)

    g = lax.axis_index("groups")
    my_weight = lax.dynamic_slice_in_dim(out_weight, g * half, half, 0)
    z_weight = [rotate(my_weight, k) for k in turns]

    def own_state(k_ref, v_ref, w_ref, out_ref):
        out_ref[:half, :] = w_ref[...]
        for i in range(heads):
            out_ref[half:, head_of(i)] = dot(
                k_ref[:, head_of(i)], v_ref[:, head_of(i)], ROWS_T
            ).astype(BF16)

    (weight_states,) = call(
        own_state, [((half + DH, feats), BF16)], keys, values, my_weight
    )
    x_weight_states = swap(weight_states, 1)
    states, x_states = weight_states[half:], x_weight_states[half:]

    def columns(gy_ref, z, h):
        return gy_ref[:, lanes(z * 2 + h, wrows)]

    def pack(gy_ref, ys_ref, near_ref):
        g, z, x, h = place()
        for i in range(seq):
            ys_ref[:, i * half : (i + 1) * half] = gy_ref[:, lanes(2 * i + 1 - g, half)]
        near = z + 1 - 2 * lax.rem(z, 2)
        near_ref[:, :wrows] = columns(gy_ref, near, h)
        near_ref[:, wrows:] = columns(gy_ref, lax.rem(near + 2, line), h)

    y_send, near_send = call(
        pack, [((rows, seq * half), BF16), ((rows, 2 * wrows), BF16)], grad_y
    )
    near_cols = swap(near_send, 2)
    y_cols = swap_y(y_send)

    def local(q_ref, k_ref, v_ref, sc_ref, att_ref):
        mask = causal_mask()
        for i in range(heads):
            sc = dot(q_ref[:, head_of(i)], k_ref[:, head_of(i)], LAST_T)
            sc = jnp.where(mask, sc, 0.0).astype(BF16)
            sc_ref[:, head_of(i)] = sc
            att_ref[:, head_of(i)] = dot(sc, v_ref[:, head_of(i)], PLAIN)

    scores, att_local = call(
        local, [((rows, feats), BF16), ((rows, feats), F32)], queries, keys, values
    )

    def add(a, b):
        return (a.astype(F32) + b.astype(F32)).astype(BF16)

    x_states, near_cols = tie(x_states, near_cols)
    pair_states = add(states, x_states)
    near_states = swap(pair_states, 2)
    near_states, y_cols = tie(near_states, y_cols)
    quad_states = add(pair_states, near_states)
    got_states = x_states, near_states, swap(quad_states, 4)

    x_weight = swap(side_by_side(*z_weight), 1)

    def weight_blocks(refs):
        own, *others, x_own, x_others = refs
        g, z, x, h = place()
        blocks = []
        for k in range(line):
            zk = lax.rem(z - k + line, line)
            blocks.append((zk * 2 + x, (own, *others)[k][...]))
            if k == 0:
                block = x_own[:half, :]
            else:
                block = x_others[(k - 1) * half : k * half, :]
            blocks.append((zk * 2 + 1 - x, block))
        return blocks

    weight_args = (my_weight, *z_weight, x_weight_states, x_weight)

    def back_other(yc_ref, *refs):
        *w_refs, out_ref = refs
        total = jnp.zeros((rows, feats), F32)
        for s, block in weight_blocks(w_refs):
            total += dot(yc_ref[:, lanes(s, half)], block, PLAIN)
        out_ref[...] = total

    def back_own(gy_ref, *refs):
        *w_refs, out_ref = refs
        g = lax.axis_index("groups")
        total = jnp.zeros((rows, feats), F32)
        for s, block in weight_blocks(w_refs):
            total += dot(gy_ref[:, lanes(2 * s + g, half)], block, PLAIN)
        out_ref[...] = total

    (grad_send,) = call(
        back_other, [((rows, feats), F32)], y_cols, *weight_args
    )
    grad_other = swap_y(grad_send)
    (grad_own,) = call(
        back_own, [((rows, feats), F32)], grad_y, *weight_args
    )

    def forward(
        q_ref, local_ref, x_ref, near_ref, far_ref, gy_ref, cols_ref,
        att_ref, normed_ref, prefix_ref, send_ref,
    ):
        g, z, x, h = place()
        total = jnp.where(x == 1, x_ref[...].astype(F32), 0.0)
        total += jnp.where(lax.rem(z, 2) == 1, near_ref[...].astype(F32), 0.0)
        total += jnp.where(z >= 2, far_ref[...].astype(F32), 0.0)
        prefix = total.astype(BF16)
        prefix_ref[...] = prefix
        for i in range(heads):
            att = local_ref[:, head_of(i)] + dot(
                q_ref[:, head_of(i)], prefix[:, head_of(i)], PLAIN
            )
            att_ref[:, head_of(i)] = att
            inv = lax.rsqrt(jnp.mean(att * att, axis=-1, keepdims=True) + epsilon)
            normed = (att * inv).astype(BF16)
            normed_ref[:, head_of(i)] = normed
            send_ref[:rows, head_of(i)] = normed
        send_ref[rows:, :wrows] = columns(gy_ref, lax.rem(z + 2, line), h)
        send_ref[rows:, wrows:] = cols_ref[:, wrows:]

    attended, normed, prefix, far_send = call(
        forward,
        [((rows, feats), F32), ((rows, feats), BF16), (state, BF16)]
        + [((2 * rows, feats), BF16)],
        queries, att_local, *got_states, grad_y, near_cols,
    )
    y_normed = swap_y(normed)
    far = swap(far_send, 4)

    def turn_back(att_ref, own_ref, other_ref, q_ref, go_ref, adj_ref):
        for i in range(heads):
            att = att_ref[:, head_of(i)]
            inv = lax.rsqrt(jnp.mean(att * att, axis=-1, keepdims=True) + epsilon)
            exact = att * inv
            grad = own_ref[:, head_of(i)] + other_ref[:, head_of(i)]
            along = jnp.mean(grad * exact, axis=-1, keepdims=True)
            go = (inv * (grad - exact * along)).astype(BF16)
            go_ref[:, head_of(i)] = go
            adj_ref[:, head_of(i)] = dot(q_ref[:, head_of(i)], go, ROWS_T).astype(BF16)

    grad_out, adjoint = call(
        turn_back, [((rows, feats), BF16), (state, BF16)],
        attended, grad_own, grad_other, queries,
    )
    near_normed = swap(normed, 2)
    x_adjoint = swap(adjoint, 1)
    x_adjoint, near_normed = tie(x_adjoint, near_normed)
    def project(n_ref, yn_ref, *refs):
        *w_refs, own_ref, other_ref = refs
        for s, block in weight_blocks(w_refs):
            own_ref[:, lanes(s, half)] = dot(n_ref[...], block, LAST_T).astype(BF16)
            other_ref[:, lanes(s, half)] = dot(yn_ref[...], block, LAST_T).astype(BF16)

    out_own, out_send = call(
        project, [((rows, seq * half), BF16)] * 2, normed, y_normed, *weight_args
    )
    out_other = swap_y(out_send)
    last_normed = swap(far[:rows], 2)
    pair_adjoint = add(adjoint, x_adjoint)
    near_adjoint = swap(pair_adjoint, 2)
    def local_grads(go_ref, q_ref, k_ref, v_ref, sc_ref, pre_ref, gq_ref, gk_ref, gv_ref):
        mask = causal_mask()
        for i in range(heads):
            at = head_of(i)
            go = go_ref[:, at]
            gs = dot(go, v_ref[:, at], LAST_T)
            gs = jnp.where(mask, gs, 0.0).astype(BF16)
            gq = dot(gs, k_ref[:, at], PLAIN) + dot(go, pre_ref[:, at], LAST_T)
            gq_ref[:, at] = gq.astype(BF16)
            gk_ref[:, at] = dot(gs, q_ref[:, at], ROWS_T)
            gv_ref[:, at] = dot(sc_ref[:, at], go, ROWS_T)

    grad_queries, gk_local, gv_local = call(
        local_grads,
        [((rows, feats), BF16), ((rows, feats), F32), ((rows, feats), F32)],
        grad_out, queries, keys, values, scores, prefix,
    )

    near_adjoint, out_other, gk_local = tie(near_adjoint, out_other, gk_local)
    my_cols = jnp.concatenate([near_cols[:, :wrows], far[rows:]], axis=1)
    core_cols = swap_core(my_cols)

    quad_adjoint = add(pair_adjoint, near_adjoint)
    far_adjoint = swap(quad_adjoint, 4)
    quad_adjoint, last_normed = tie(quad_adjoint, last_normed)

    core_own = swap_core(out_own)
    core_other = swap_core(out_other)

    def weight_grad(
        gy_ref, c_ref, o_ref, n_ref, near_ref, far_ref, last_ref, keep_ref, send_ref
    ):
        g, z, x, h = place()
        same = dot(columns(gy_ref, z, h), n_ref[...], ROWS_T)
        other = dot(columns(gy_ref, z, 1 - h), n_ref[...], ROWS_T)
        for i, there in enumerate((near_ref[...], far_ref[:rows, :], last_ref[...])):
            at = slice(i * wrows, (i + 1) * wrows)
            same += dot(c_ref[:, at], there, ROWS_T)
            other += dot(o_ref[:, at], there, ROWS_T)
        keep_ref[...] = jnp.where(x == h, same, other)
        send_ref[...] = jnp.where(x == h, other, same).astype(BF16)

    gw_keep, gw_send = call(
        weight_grad, [((wrows, feats), F32), ((wrows, feats), BF16)],
        grad_y, my_cols, core_cols, normed, near_normed, far, last_normed,
    )
    gw_other = swap(gw_send, 1)

    def join(a_ref, b_ref, c_ref, d_ref, y_ref):
        g = lax.axis_index("groups")
        for i in range(seq):
            at = slice(i * half, (i + 1) * half)
            y_ref[:, lanes(2 * i + g, half)] = (
                a_ref[:, at].astype(F32) + b_ref[:, at].astype(F32)
            ).astype(BF16)
            y_ref[:, lanes(2 * i + 1 - g, half)] = (
                c_ref[:, at].astype(F32) + d_ref[:, at].astype(F32)
            ).astype(BF16)

    (out_y,) = call(
        join, [((rows, outs), BF16)], out_own, core_own, out_other, core_other,
    )
    far_adjoint, out_y = tie(far_adjoint, out_y)

    def last(gk_ref, gv_ref, k_ref, v_ref, x_ref, near_ref, far_ref, ok_ref, ov_ref):
        g, z, x, h = place()
        total = jnp.where(x == 0, x_ref[...].astype(F32), 0.0)
        total += jnp.where(lax.rem(z, 2) == 0, near_ref[...].astype(F32), 0.0)
        total += jnp.where(z < 2, far_ref[...].astype(F32), 0.0)
        suffix = total.astype(BF16)
        for i in range(heads):
            at = head_of(i)
            ok_ref[:, at] = (
                gk_ref[:, at] + dot(v_ref[:, at], suffix[:, at], LAST_T)
            ).astype(BF16)
            ov_ref[:, at] = (
                gv_ref[:, at] + dot(k_ref[:, at], suffix[:, at], PLAIN)
            ).astype(BF16)

    grad_keys, grad_values = call(
        last, [((rows, feats), BF16)] * 2,
        gk_local, gv_local, keys, values, x_adjoint, near_adjoint, far_adjoint,
    )
    gw_other, grad_keys = tie(gw_other, grad_keys)
    grad_weight = gw_keep + gw_other.astype(F32)
    return out_y, grad_queries, grad_keys, grad_values, grad_weight


def solution(mesh):
    placed = (
        P(("groups", "seq"), "head"),
        P(("groups", "seq"), "head"),
        P(("groups", "seq"), "head"),
        P("seq", "head"),
        P(("groups", "seq"), None),
    )
    size = dict(mesh.shape)

    def program(queries, keys, values, out_weight, grad_y):
        short = size["seq"] == 8 and size["groups"] == 2 and size["head"] == 2
        if short and queries.shape[0] == TILE and 2 * out_weight.shape[0] == queries.shape[1]:
            return on_short_line(
                size["seq"], queries, keys, values, out_weight, grad_y
            )
        return on_device(queries, keys, values, out_weight, grad_y)

    return jax.shard_map(
        program,
        mesh=mesh,
        in_specs=placed,
        out_specs=(
            P(("groups", "seq"), None),
            P(("groups", "seq"), "head"),
            P(("groups", "seq"), "head"),
            P(("groups", "seq"), "head"),
            P(("groups", "seq"), "head"),
        ),
        check_vma=False,
    )
```

```python
import jax
import jax.numpy as jnp
from jax import lax
from jax.experimental import pallas as pl
from jax.experimental.pallas import tpu as pltpu
from jax.sharding import PartitionSpec as P

DH = 128
TILE = 128


epsilon = 1e-06
F32 = jnp.float32
BF16 = jnp.bfloat16
ROWS_T = (((0,), (0,)), ((), ()))
LAST_T = (((1,), (1,)), ((), ()))
HINTS = {
    "own_state": 300000000,
    "pack": 3000000000,
    "local": 1000000000,
    "back_other": 1000000000,
    "back_own": 1000000000,
    "forward": 3000000000,
    "turn_back": 1048576,
    "project": 3000000000,
    "local_grads": 1048576,
    "weight_grad": 1500000000,
    "join": 1048576,
    "last": 3000000000,
}
PLAIN = (((1,), (0,)), ((), ()))


def carried_in(value, axis, join, neutral, backward):
    count, mine = (lax.axis_size(axis), lax.axis_index(axis))
    pieces = lax.all_gather(value, axis)
    if backward:
        pieces = pieces[::-1]
        mine = count - 1 - mine
    so_far = jnp.full_like(value, 0) + jnp.asarray(neutral, value.dtype)

    def turn(position, so_far):
        longer = join(so_far, pieces[position])
        return jnp.where(position < mine, longer, so_far)

    return lax.fori_loop(0, count - 1, turn, so_far)


def add_states(earlier, later):
    return earlier + later


def on_device(queries, keys, values, out_weight, grad_y):
    row_count = queries.shape[0]
    tile_count = row_count // TILE
    head_count = queries.shape[1] // DH

    def tiled(array):
        return array.reshape(tile_count, TILE, head_count, DH)

    query_tiles = tiled(queries)
    key_tiles = tiled(keys)
    value_tiles = tiled(values)
    causal = lax.broadcasted_iota(jnp.int32, (TILE, TILE), 0) >= lax.broadcasted_iota(
        jnp.int32, (TILE, TILE), 1
    )
    raw_scores = jnp.einsum(
        "nthd,nshd->nhts", query_tiles, key_tiles, preferred_element_type=jnp.float32
    )
    scores = jnp.where(causal, raw_scores, 0.0).astype(jnp.bfloat16)
    states = jnp.einsum(
        "nshd,nshe->nhde", key_tiles, value_tiles, preferred_element_type=jnp.float32
    )
    empty_state = jnp.zeros(states.shape[1:], jnp.float32)
    device_prefix = carried_in(jnp.sum(states, axis=0), "seq", add_states, empty_state, False)
    prefix_state = (device_prefix[None] + (jnp.cumsum(states, axis=0) - states)).astype(
        jnp.bfloat16
    )
    attended = jnp.einsum(
        "nhts,nshe->nthe", scores, value_tiles, preferred_element_type=jnp.float32
    )
    attended = attended + jnp.einsum(
        "nthd,nhde->nthe", query_tiles, prefix_state, preferred_element_type=jnp.float32
    )
    inverse_rms = lax.rsqrt(jnp.mean(attended * attended, axis=-1, keepdims=True) + epsilon)
    normed_exact = attended * inverse_rms
    normed = normed_exact.astype(jnp.bfloat16).reshape(row_count, -1)
    back_weight = lax.all_gather(out_weight, "seq", axis=0, tiled=True)
    grad_normed = jnp.dot(grad_y, back_weight, preferred_element_type=jnp.float32)
    fore_weight = lax.all_gather(out_weight, "seq", axis=0, tiled=True)
    partial_out = lax.dot_general(
        normed, fore_weight, LAST_T, preferred_element_type=jnp.float32
    )
    out_y = lax.psum(partial_out.astype(jnp.bfloat16), "head")
    grad_tiles = tiled(grad_normed)
    projected = jnp.mean(grad_tiles * normed_exact, axis=-1, keepdims=True)
    grad_out = (inverse_rms * (grad_tiles - normed_exact * projected)).astype(jnp.bfloat16)
    raw_grad = jnp.einsum(
        "nthe,nshe->nhts", grad_out, value_tiles, preferred_element_type=jnp.float32
    )
    grad_scores = jnp.where(causal, raw_grad, 0.0).astype(jnp.bfloat16)
    adjoint = jnp.einsum(
        "nthd,nthe->nhde", query_tiles, grad_out, preferred_element_type=jnp.float32
    )
    own_adjoint = jnp.sum(adjoint, axis=0)
    device_suffix = carried_in(own_adjoint, "seq", add_states, empty_state, True)
    later_tiles = jnp.flip(jnp.cumsum(jnp.flip(adjoint, 0), axis=0), 0) - adjoint
    suffix_state = (device_suffix[None] + later_tiles).astype(jnp.bfloat16)
    grad_queries = jnp.einsum(
        "nhts,nshd->nthd", grad_scores, key_tiles, preferred_element_type=jnp.float32
    )
    grad_queries = grad_queries + jnp.einsum(
        "nthe,nhde->nthd", grad_out, prefix_state, preferred_element_type=jnp.float32
    )
    grad_keys = jnp.einsum(
        "nhts,nthd->nshd", grad_scores, query_tiles, preferred_element_type=jnp.float32
    )
    grad_keys = grad_keys + jnp.einsum(
        "nshe,nhde->nshd", value_tiles, suffix_state, preferred_element_type=jnp.float32
    )
    grad_values = jnp.einsum(
        "nhts,nthe->nshe", scores, grad_out, preferred_element_type=jnp.float32
    )
    grad_values = grad_values + jnp.einsum(
        "nshd,nhde->nshe", key_tiles, suffix_state, preferred_element_type=jnp.float32
    )
    grad_weight = lax.psum_scatter(
        lax.dot_general(
            grad_y, normed, (((0,), (0,)), ((), ())), preferred_element_type=jnp.float32
        ),
        "seq",
        scatter_dimension=0,
        tiled=True,
    )
    return (
        out_y,
        grad_queries.reshape(row_count, -1).astype(jnp.bfloat16),
        grad_keys.reshape(row_count, -1).astype(jnp.bfloat16),
        grad_values.reshape(row_count, -1).astype(jnp.bfloat16),
        grad_weight,
    )


def dot(a, b, dims):
    return lax.dot_general(a, b, dims, preferred_element_type=F32)


def call(body, shapes, *args):
    return pl.pallas_call(
        body,
        out_shape=[jax.ShapeDtypeStruct(s, d) for s, d in shapes],
        in_specs=[pl.BlockSpec(memory_space=pltpu.VMEM)] * len(args),
        out_specs=[pl.BlockSpec(memory_space=pltpu.VMEM)] * len(shapes),
        cost_estimate=pl.CostEstimate(
            flops=HINTS[body.__name__], bytes_accessed=2**20, transcendentals=0
        ),
        compiler_params=pltpu.CompilerParams(vmem_limit_bytes=24 * 2**20),
    )(*args)


def lanes(i, size):
    return pl.ds(pl.multiple_of(i * size, size), size)


def head_of(i):
    return slice(i * DH, (i + 1) * DH)


def causal_mask():
    rows = lax.broadcasted_iota(jnp.int32, (TILE, TILE), 0)
    return rows >= lax.broadcasted_iota(jnp.int32, (TILE, TILE), 1)


def place():
    s = lax.axis_index("seq")
    return lax.axis_index("groups"), s // 2, s % 2, lax.axis_index("head")


def on_short_line(seq, queries, keys, values, out_weight, grad_y):
    rows, feats = queries.shape
    heads = feats // DH
    wrows = out_weight.shape[0]
    half = wrows // 2
    line = seq // 2
    turns = range(1, line)
    outs = grad_y.shape[1]
    state = (DH, heads * DH)

    def permute(array, pairs):
        return lax.ppermute(array, "seq", pairs)

    def rotate(array, k):
        return permute(array, [(i, (i + 2 * k) % seq) for i in range(seq)])

    def swap(array, bit):
        return permute(array, [(i, i ^ bit) for i in range(seq)])

    def swap_y(array):
        return lax.ppermute(array, "groups", [(0, 1), (1, 0)])

    def swap_core(array):
        return lax.ppermute(array, "head", [(0, 1), (1, 0)])

    def side_by_side(*arrays):
        return jnp.concatenate(arrays, axis=0)

    def tie(*arrays):
        return lax.optimization_barrier(arrays)

    g = lax.axis_index("groups")
    my_weight = lax.dynamic_slice_in_dim(out_weight, g * half, half, 0)
    z_weight = [rotate(my_weight, k) for k in turns]

    def own_state(k_ref, v_ref, out_ref):
        for i in range(heads):
            out_ref[:, head_of(i)] = dot(
                k_ref[:, head_of(i)], v_ref[:, head_of(i)], ROWS_T
            ).astype(BF16)

    (states,) = call(own_state, [(state, BF16)], keys, values)
    x_states = swap(states, 1)
    states, own_weight = tie(states, my_weight)
    x_weight_own = swap(own_weight, 1)

    def columns(gy_ref, z, h):
        return gy_ref[:, lanes(z * 2 + h, wrows)]

    def pack(gy_ref, ys_ref, near_ref):
        g, z, x, h = place()
        for i in range(seq):
            ys_ref[:, i * half : (i + 1) * half] = gy_ref[:, lanes(2 * i + 1 - g, half)]
        near = z + 1 - 2 * lax.rem(z, 2)
        near_ref[:, :wrows] = columns(gy_ref, near, h)
        near_ref[:, wrows:] = columns(gy_ref, lax.rem(near + 2, line), h)

    y_send, near_send = call(
        pack, [((rows, seq * half), BF16), ((rows, 2 * wrows), BF16)], grad_y
    )
    near_cols = swap(near_send, 2)
    y_cols = swap_y(y_send)

    def local(q_ref, k_ref, v_ref, sc_ref, att_ref):
        mask = causal_mask()
        for i in range(heads):
            sc = dot(q_ref[:, head_of(i)], k_ref[:, head_of(i)], LAST_T)
            sc = jnp.where(mask, sc, 0.0).astype(BF16)
            sc_ref[:, head_of(i)] = sc
            att_ref[:, head_of(i)] = dot(sc, v_ref[:, head_of(i)], PLAIN)

    scores, att_local = call(
        local, [((rows, feats), BF16), ((rows, feats), F32)], queries, keys, values
    )

    def add(a, b):
        return (a.astype(F32) + b.astype(F32)).astype(BF16)

    pair_states = add(states, x_states)
    near_states = swap(pair_states, 2)
    pair_states, x_weight_own, near_cols, *z_weight = tie(
        pair_states, x_weight_own, near_cols, *z_weight
    )
    near_states, y_cols = tie(near_states, y_cols)
    quad_states = add(pair_states, near_states)
    got_states = x_states, near_states, swap(quad_states, 4)

    x_weight = swap(side_by_side(*z_weight), 1)

    def weight_blocks(refs):
        own, *others, x_own, x_others = refs
        g, z, x, h = place()
        blocks = []
        for k in range(line):
            zk = lax.rem(z - k + line, line)
            blocks.append((zk * 2 + x, (own, *others)[k][...]))
            if k == 0:
                block = x_own[...]
            else:
                block = x_others[(k - 1) * half : k * half, :]
            blocks.append((zk * 2 + 1 - x, block))
        return blocks

    weight_args = (my_weight, *z_weight, x_weight_own, x_weight)

    def back_other(yc_ref, *refs):
        *w_refs, out_ref = refs
        total = jnp.zeros((rows, feats), F32)
        for s, block in weight_blocks(w_refs):
            total += dot(yc_ref[:, lanes(s, half)], block, PLAIN)
        out_ref[...] = total

    def back_own(gy_ref, *refs):
        *w_refs, out_ref = refs
        g = lax.axis_index("groups")
        total = jnp.zeros((rows, feats), F32)
        for s, block in weight_blocks(w_refs):
            total += dot(gy_ref[:, lanes(2 * s + g, half)], block, PLAIN)
        out_ref[...] = total

    (grad_send,) = call(
        back_other, [((rows, feats), F32)], y_cols, *weight_args
    )
    grad_other = swap_y(grad_send)
    (grad_own,) = call(
        back_own, [((rows, feats), F32)], grad_y, *weight_args
    )

    def forward(
        q_ref, local_ref, x_ref, near_ref, far_ref, gy_ref, cols_ref,
        att_ref, normed_ref, prefix_ref, send_ref,
    ):
        g, z, x, h = place()
        total = jnp.where(x == 1, x_ref[...].astype(F32), 0.0)
        total += jnp.where(lax.rem(z, 2) == 1, near_ref[...].astype(F32), 0.0)
        total += jnp.where(z >= 2, far_ref[...].astype(F32), 0.0)
        prefix = total.astype(BF16)
        prefix_ref[...] = prefix
        for i in range(heads):
            att = local_ref[:, head_of(i)] + dot(
                q_ref[:, head_of(i)], prefix[:, head_of(i)], PLAIN
            )
            att_ref[:, head_of(i)] = att
            inv = lax.rsqrt(jnp.mean(att * att, axis=-1, keepdims=True) + epsilon)
            normed = (att * inv).astype(BF16)
            normed_ref[:, head_of(i)] = normed
            send_ref[:rows, head_of(i)] = normed
        send_ref[rows:, :wrows] = columns(gy_ref, lax.rem(z + 2, line), h)
        send_ref[rows:, wrows:] = cols_ref[:, wrows:]

    attended, normed, prefix, far_send = call(
        forward,
        [((rows, feats), F32), ((rows, feats), BF16), (state, BF16)]
        + [((2 * rows, feats), BF16)],
        queries, att_local, *got_states, grad_y, near_cols,
    )
    y_normed = swap_y(normed)
    far = swap(far_send, 4)

    def turn_back(att_ref, own_ref, other_ref, q_ref, go_ref, adj_ref):
        for i in range(heads):
            att = att_ref[:, head_of(i)]
            inv = lax.rsqrt(jnp.mean(att * att, axis=-1, keepdims=True) + epsilon)
            exact = att * inv
            grad = own_ref[:, head_of(i)] + other_ref[:, head_of(i)]
            along = jnp.mean(grad * exact, axis=-1, keepdims=True)
            go = (inv * (grad - exact * along)).astype(BF16)
            go_ref[:, head_of(i)] = go
            adj_ref[:, head_of(i)] = dot(q_ref[:, head_of(i)], go, ROWS_T).astype(BF16)

    grad_out, adjoint = call(
        turn_back, [((rows, feats), BF16), (state, BF16)],
        attended, grad_own, grad_other, queries,
    )
    near_normed = swap(normed, 2)
    x_adjoint = swap(adjoint, 1)
    x_adjoint, near_normed = tie(x_adjoint, near_normed)
    def project(n_ref, yn_ref, *refs):
        *w_refs, own_ref, other_ref = refs
        for s, block in weight_blocks(w_refs):
            own_ref[:, lanes(s, half)] = dot(n_ref[...], block, LAST_T).astype(BF16)
            other_ref[:, lanes(s, half)] = dot(yn_ref[...], block, LAST_T).astype(BF16)

    out_own, out_send = call(
        project, [((rows, seq * half), BF16)] * 2, normed, y_normed, *weight_args
    )
    out_other = swap_y(out_send)
    last_normed = swap(far[:rows], 2)
    pair_adjoint = add(adjoint, x_adjoint)
    near_adjoint = swap(pair_adjoint, 2)
    def local_grads(go_ref, q_ref, k_ref, v_ref, sc_ref, pre_ref, gq_ref, gk_ref, gv_ref):
        mask = causal_mask()
        for i in range(heads):
            at = head_of(i)
            go = go_ref[:, at]
            gs = dot(go, v_ref[:, at], LAST_T)
            gs = jnp.where(mask, gs, 0.0).astype(BF16)
            gq = dot(gs, k_ref[:, at], PLAIN) + dot(go, pre_ref[:, at], LAST_T)
            gq_ref[:, at] = gq.astype(BF16)
            gk_ref[:, at] = dot(gs, q_ref[:, at], ROWS_T)
            gv_ref[:, at] = dot(sc_ref[:, at], go, ROWS_T)

    grad_queries, gk_local, gv_local = call(
        local_grads,
        [((rows, feats), BF16), ((rows, feats), F32), ((rows, feats), F32)],
        grad_out, queries, keys, values, scores, prefix,
    )

    near_adjoint, out_other, gk_local = tie(near_adjoint, out_other, gk_local)
    my_cols = jnp.concatenate([near_cols[:, :wrows], far[rows:]], axis=1)
    core_cols = swap_core(my_cols)

    quad_adjoint = add(pair_adjoint, near_adjoint)
    far_adjoint = swap(quad_adjoint, 4)
    quad_adjoint, last_normed = tie(quad_adjoint, last_normed)

    core_own = swap_core(out_own)
    core_other = swap_core(out_other)

    def weight_grad(
        gy_ref, c_ref, o_ref, n_ref, near_ref, far_ref, last_ref, keep_ref, send_ref
    ):
        g, z, x, h = place()
        same = dot(columns(gy_ref, z, h), n_ref[...], ROWS_T)
        other = dot(columns(gy_ref, z, 1 - h), n_ref[...], ROWS_T)
        for i, there in enumerate((near_ref[...], far_ref[:rows, :], last_ref[...])):
            at = slice(i * wrows, (i + 1) * wrows)
            same += dot(c_ref[:, at], there, ROWS_T)
            other += dot(o_ref[:, at], there, ROWS_T)
        keep_ref[...] = jnp.where(x == h, same, other)
        send_ref[...] = jnp.where(x == h, other, same).astype(BF16)

    gw_keep, gw_send = call(
        weight_grad, [((wrows, feats), F32), ((wrows, feats), BF16)],
        grad_y, my_cols, core_cols, normed, near_normed, far, last_normed,
    )
    gw_other = swap(gw_send, 1)

    def join(a_ref, b_ref, c_ref, d_ref, y_ref):
        g = lax.axis_index("groups")
        for i in range(seq):
            at = slice(i * half, (i + 1) * half)
            y_ref[:, lanes(2 * i + g, half)] = (
                a_ref[:, at].astype(F32) + b_ref[:, at].astype(F32)
            ).astype(BF16)
            y_ref[:, lanes(2 * i + 1 - g, half)] = (
                c_ref[:, at].astype(F32) + d_ref[:, at].astype(F32)
            ).astype(BF16)

    (out_y,) = call(
        join, [((rows, outs), BF16)], out_own, core_own, out_other, core_other,
    )
    far_adjoint, out_y = tie(far_adjoint, out_y)

    def last(gk_ref, gv_ref, k_ref, v_ref, x_ref, near_ref, far_ref, ok_ref, ov_ref):
        g, z, x, h = place()
        total = jnp.where(x == 0, x_ref[...].astype(F32), 0.0)
        total += jnp.where(lax.rem(z, 2) == 0, near_ref[...].astype(F32), 0.0)
        total += jnp.where(z < 2, far_ref[...].astype(F32), 0.0)
        suffix = total.astype(BF16)
        for i in range(heads):
            at = head_of(i)
            ok_ref[:, at] = (
                gk_ref[:, at] + dot(v_ref[:, at], suffix[:, at], LAST_T)
            ).astype(BF16)
            ov_ref[:, at] = (
                gv_ref[:, at] + dot(k_ref[:, at], suffix[:, at], PLAIN)
            ).astype(BF16)

    grad_keys, grad_values = call(
        last, [((rows, feats), BF16)] * 2,
        gk_local, gv_local, keys, values, x_adjoint, near_adjoint, far_adjoint,
    )
    gw_other, grad_keys = tie(gw_other, grad_keys)
    grad_weight = gw_keep + gw_other.astype(F32)
    return out_y, grad_queries, grad_keys, grad_values, grad_weight


def solution(mesh):
    placed = (
        P(("groups", "seq"), "head"),
        P(("groups", "seq"), "head"),
        P(("groups", "seq"), "head"),
        P("seq", "head"),
        P(("groups", "seq"), None),
    )
    size = dict(mesh.shape)

    def program(queries, keys, values, out_weight, grad_y):
        short = size["seq"] == 8 and size["groups"] == 2 and size["head"] == 2
        if short and queries.shape[0] == TILE and 2 * out_weight.shape[0] == queries.shape[1]:
            return on_short_line(
                size["seq"], queries, keys, values, out_weight, grad_y
            )
        return on_device(queries, keys, values, out_weight, grad_y)

    return jax.shard_map(
        program,
        mesh=mesh,
        in_specs=placed,
        out_specs=(
            P(("groups", "seq"), None),
            P(("groups", "seq"), "head"),
            P(("groups", "seq"), "head"),
            P(("groups", "seq"), "head"),
            P(("groups", "seq"), "head"),
        ),
        check_vma=False,
    )
```

```python
import jax
import jax.numpy as jnp
from jax import lax
from jax.experimental import pallas as pl
from jax.experimental.pallas import tpu as pltpu
from jax.sharding import PartitionSpec as P

DH = 128
TILE = 128


epsilon = 1e-06
F32 = jnp.float32
BF16 = jnp.bfloat16
ROWS_T = (((0,), (0,)), ((), ()))
LAST_T = (((1,), (1,)), ((), ()))
HINTS = {
    "own_state": 300000000,
    "pack": 600000000,
    "local": 3000000000,
    "back_other": 1048576,
    "back_own": 1000000000,
    "forward": 3000000000,
    "turn_back": 3000000000,
    "project": 3000000000,
    "local_grads": 1048576,
    "weight_grad": 600000000,
    "join": 1048576,
    "last": 3000000000,
}
PLAIN = (((1,), (0,)), ((), ()))


def carried_in(value, axis, join, neutral, backward):
    count, mine = (lax.axis_size(axis), lax.axis_index(axis))
    pieces = lax.all_gather(value, axis)
    if backward:
        pieces = pieces[::-1]
        mine = count - 1 - mine
    so_far = jnp.full_like(value, 0) + jnp.asarray(neutral, value.dtype)

    def turn(position, so_far):
        longer = join(so_far, pieces[position])
        return jnp.where(position < mine, longer, so_far)

    return lax.fori_loop(0, count - 1, turn, so_far)


def add_states(earlier, later):
    return earlier + later


def on_device(queries, keys, values, out_weight, grad_y):
    row_count = queries.shape[0]
    tile_count = row_count // TILE
    head_count = queries.shape[1] // DH

    def tiled(array):
        return array.reshape(tile_count, TILE, head_count, DH)

    query_tiles = tiled(queries)
    key_tiles = tiled(keys)
    value_tiles = tiled(values)
    causal = lax.broadcasted_iota(jnp.int32, (TILE, TILE), 0) >= lax.broadcasted_iota(
        jnp.int32, (TILE, TILE), 1
    )
    raw_scores = jnp.einsum(
        "nthd,nshd->nhts", query_tiles, key_tiles, preferred_element_type=jnp.float32
    )
    scores = jnp.where(causal, raw_scores, 0.0).astype(jnp.bfloat16)
    states = jnp.einsum(
        "nshd,nshe->nhde", key_tiles, value_tiles, preferred_element_type=jnp.float32
    )
    empty_state = jnp.zeros(states.shape[1:], jnp.float32)
    device_prefix = carried_in(jnp.sum(states, axis=0), "seq", add_states, empty_state, False)
    prefix_state = (device_prefix[None] + (jnp.cumsum(states, axis=0) - states)).astype(
        jnp.bfloat16
    )
    attended = jnp.einsum(
        "nhts,nshe->nthe", scores, value_tiles, preferred_element_type=jnp.float32
    )
    attended = attended + jnp.einsum(
        "nthd,nhde->nthe", query_tiles, prefix_state, preferred_element_type=jnp.float32
    )
    inverse_rms = lax.rsqrt(jnp.mean(attended * attended, axis=-1, keepdims=True) + epsilon)
    normed_exact = attended * inverse_rms
    normed = normed_exact.astype(jnp.bfloat16).reshape(row_count, -1)
    back_weight = lax.all_gather(out_weight, "seq", axis=0, tiled=True)
    grad_normed = jnp.dot(grad_y, back_weight, preferred_element_type=jnp.float32)
    fore_weight = lax.all_gather(out_weight, "seq", axis=0, tiled=True)
    partial_out = lax.dot_general(
        normed, fore_weight, LAST_T, preferred_element_type=jnp.float32
    )
    out_y = lax.psum(partial_out.astype(jnp.bfloat16), "head")
    grad_tiles = tiled(grad_normed)
    projected = jnp.mean(grad_tiles * normed_exact, axis=-1, keepdims=True)
    grad_out = (inverse_rms * (grad_tiles - normed_exact * projected)).astype(jnp.bfloat16)
    raw_grad = jnp.einsum(
        "nthe,nshe->nhts", grad_out, value_tiles, preferred_element_type=jnp.float32
    )
    grad_scores = jnp.where(causal, raw_grad, 0.0).astype(jnp.bfloat16)
    adjoint = jnp.einsum(
        "nthd,nthe->nhde", query_tiles, grad_out, preferred_element_type=jnp.float32
    )
    own_adjoint = jnp.sum(adjoint, axis=0)
    device_suffix = carried_in(own_adjoint, "seq", add_states, empty_state, True)
    later_tiles = jnp.flip(jnp.cumsum(jnp.flip(adjoint, 0), axis=0), 0) - adjoint
    suffix_state = (device_suffix[None] + later_tiles).astype(jnp.bfloat16)
    grad_queries = jnp.einsum(
        "nhts,nshd->nthd", grad_scores, key_tiles, preferred_element_type=jnp.float32
    )
    grad_queries = grad_queries + jnp.einsum(
        "nthe,nhde->nthd", grad_out, prefix_state, preferred_element_type=jnp.float32
    )
    grad_keys = jnp.einsum(
        "nhts,nthd->nshd", grad_scores, query_tiles, preferred_element_type=jnp.float32
    )
    grad_keys = grad_keys + jnp.einsum(
        "nshe,nhde->nshd", value_tiles, suffix_state, preferred_element_type=jnp.float32
    )
    grad_values = jnp.einsum(
        "nhts,nthe->nshe", scores, grad_out, preferred_element_type=jnp.float32
    )
    grad_values = grad_values + jnp.einsum(
        "nshd,nhde->nshe", key_tiles, suffix_state, preferred_element_type=jnp.float32
    )
    grad_weight = lax.psum_scatter(
        lax.dot_general(
            grad_y, normed, (((0,), (0,)), ((), ())), preferred_element_type=jnp.float32
        ),
        "seq",
        scatter_dimension=0,
        tiled=True,
    )
    return (
        out_y,
        grad_queries.reshape(row_count, -1).astype(jnp.bfloat16),
        grad_keys.reshape(row_count, -1).astype(jnp.bfloat16),
        grad_values.reshape(row_count, -1).astype(jnp.bfloat16),
        grad_weight,
    )


def dot(a, b, dims):
    return lax.dot_general(a, b, dims, preferred_element_type=F32)


def call(body, shapes, *args):
    return pl.pallas_call(
        body,
        out_shape=[jax.ShapeDtypeStruct(s, d) for s, d in shapes],
        in_specs=[pl.BlockSpec(memory_space=pltpu.VMEM)] * len(args),
        out_specs=[pl.BlockSpec(memory_space=pltpu.VMEM)] * len(shapes),
        cost_estimate=pl.CostEstimate(
            flops=HINTS[body.__name__], bytes_accessed=2**20, transcendentals=0
        ),
        compiler_params=pltpu.CompilerParams(vmem_limit_bytes=24 * 2**20),
    )(*args)


def lanes(i, size):
    return pl.ds(pl.multiple_of(i * size, size), size)


def head_of(i):
    return slice(i * DH, (i + 1) * DH)


def causal_mask():
    rows = lax.broadcasted_iota(jnp.int32, (TILE, TILE), 0)
    return rows >= lax.broadcasted_iota(jnp.int32, (TILE, TILE), 1)


def place():
    s = lax.axis_index("seq")
    return lax.axis_index("groups"), s // 2, s % 2, lax.axis_index("head")


def on_short_line(seq, queries, keys, values, out_weight, grad_y):
    rows, feats = queries.shape
    heads = feats // DH
    wrows = out_weight.shape[0]
    half = wrows // 2
    line = seq // 2
    turns = range(1, line)
    outs = grad_y.shape[1]
    state = (DH, heads * DH)

    def permute(array, pairs):
        return lax.ppermute(array, "seq", pairs)

    def rotate(array, k):
        return permute(array, [(i, (i + 2 * k) % seq) for i in range(seq)])

    def swap(array, bit):
        return permute(array, [(i, i ^ bit) for i in range(seq)])

    def swap_y(array):
        return lax.ppermute(array, "groups", [(0, 1), (1, 0)])

    def swap_core(array):
        return lax.ppermute(array, "head", [(0, 1), (1, 0)])

    def side_by_side(*arrays):
        return jnp.concatenate(arrays, axis=0)

    def tie(*arrays):
        return lax.optimization_barrier(arrays)

    g = lax.axis_index("groups")
    my_weight = lax.dynamic_slice_in_dim(out_weight, g * half, half, 0)
    z_weight = [rotate(my_weight, k) for k in turns]

    def own_state(k_ref, v_ref, out_ref):
        for i in range(heads):
            out_ref[:, head_of(i)] = dot(
                k_ref[:, head_of(i)], v_ref[:, head_of(i)], ROWS_T
            ).astype(BF16)

    (states,) = call(own_state, [(state, BF16)], keys, values)
    x_states = swap(states, 1)
    states, own_weight, packed = tie(states, my_weight, grad_y)
    x_weight_own = swap(own_weight, 1)

    def columns(gy_ref, z, h):
        return gy_ref[:, lanes(z * 2 + h, wrows)]

    def pack(gy_ref, ys_ref, near_ref):
        g, z, x, h = place()
        for i in range(seq):
            ys_ref[:, i * half : (i + 1) * half] = gy_ref[:, lanes(2 * i + 1 - g, half)]
        near = z + 1 - 2 * lax.rem(z, 2)
        near_ref[:, :wrows] = columns(gy_ref, near, h)
        near_ref[:, wrows:] = columns(gy_ref, lax.rem(near + 2, line), h)

    y_send, near_send = call(
        pack, [((rows, seq * half), BF16), ((rows, 2 * wrows), BF16)], packed
    )
    near_cols = swap(near_send, 2)
    y_send, later_values = tie(y_send, values)
    y_cols = swap_y(y_send)

    def local(q_ref, k_ref, v_ref, sc_ref, att_ref):
        mask = causal_mask()
        for i in range(heads):
            sc = dot(q_ref[:, head_of(i)], k_ref[:, head_of(i)], LAST_T)
            sc = jnp.where(mask, sc, 0.0).astype(BF16)
            sc_ref[:, head_of(i)] = sc
            att_ref[:, head_of(i)] = dot(sc, v_ref[:, head_of(i)], PLAIN)

    scores, att_local = call(
        local, [((rows, feats), BF16), ((rows, feats), F32)], queries, keys, later_values
    )

    def add(a, b):
        return (a.astype(F32) + b.astype(F32)).astype(BF16)

    x_states, x_weight_own, att_local = tie(x_states, x_weight_own, att_local)
    pair_states = add(states, x_states)
    near_states = swap(pair_states, 2)
    pair_states, *z_weight = tie(pair_states, *z_weight)
    near_states, y_cols, near_cols = tie(near_states, y_cols, near_cols)
    quad_states = add(pair_states, near_states)
    got_states = x_states, near_states, swap(quad_states, 4)

    x_weight = swap(side_by_side(*z_weight), 1)

    def weight_blocks(refs):
        own, *others, x_own, x_others = refs
        g, z, x, h = place()
        blocks = []
        for k in range(line):
            zk = lax.rem(z - k + line, line)
            blocks.append((zk * 2 + x, (own, *others)[k][...]))
            if k == 0:
                block = x_own[...]
            else:
                block = x_others[(k - 1) * half : k * half, :]
            blocks.append((zk * 2 + 1 - x, block))
        return blocks

    weight_args = (my_weight, *z_weight, x_weight_own, x_weight)

    def back_other(yc_ref, *refs):
        *w_refs, out_ref = refs
        total = jnp.zeros((rows, feats), F32)
        for s, block in weight_blocks(w_refs):
            total += dot(yc_ref[:, lanes(s, half)], block, PLAIN)
        out_ref[...] = total

    def back_own(gy_ref, *refs):
        *w_refs, out_ref = refs
        g = lax.axis_index("groups")
        total = jnp.zeros((rows, feats), F32)
        for s, block in weight_blocks(w_refs):
            total += dot(gy_ref[:, lanes(2 * s + g, half)], block, PLAIN)
        out_ref[...] = total

    (grad_send,) = call(
        back_other, [((rows, feats), F32)], y_cols, *weight_args
    )
    grad_other = swap_y(grad_send)
    (grad_own,) = call(
        back_own, [((rows, feats), F32)], grad_y, *weight_args
    )

    def forward(
        q_ref, local_ref, x_ref, near_ref, far_ref, gy_ref, cols_ref,
        att_ref, normed_ref, prefix_ref, send_ref,
    ):
        g, z, x, h = place()
        total = jnp.where(x == 1, x_ref[...].astype(F32), 0.0)
        total += jnp.where(lax.rem(z, 2) == 1, near_ref[...].astype(F32), 0.0)
        total += jnp.where(z >= 2, far_ref[...].astype(F32), 0.0)
        prefix = total.astype(BF16)
        prefix_ref[...] = prefix
        for i in range(heads):
            att = local_ref[:, head_of(i)] + dot(
                q_ref[:, head_of(i)], prefix[:, head_of(i)], PLAIN
            )
            att_ref[:, head_of(i)] = att
            inv = lax.rsqrt(jnp.mean(att * att, axis=-1, keepdims=True) + epsilon)
            normed = (att * inv).astype(BF16)
            normed_ref[:, head_of(i)] = normed
            send_ref[:rows, head_of(i)] = normed
        send_ref[rows:, :wrows] = columns(gy_ref, lax.rem(z + 2, line), h)
        send_ref[rows:, wrows:] = cols_ref[:, wrows:]

    attended, normed, prefix, far_send = call(
        forward,
        [((rows, feats), F32), ((rows, feats), BF16), (state, BF16)]
        + [((2 * rows, feats), BF16)],
        queries, att_local, *got_states, grad_y, near_cols,
    )
    y_send, grad_own = tie(normed, grad_own)
    y_normed = swap_y(y_send)
    far = swap(far_send, 4)

    def turn_back(att_ref, own_ref, other_ref, q_ref, go_ref, adj_ref):
        for i in range(heads):
            att = att_ref[:, head_of(i)]
            inv = lax.rsqrt(jnp.mean(att * att, axis=-1, keepdims=True) + epsilon)
            exact = att * inv
            grad = own_ref[:, head_of(i)] + other_ref[:, head_of(i)]
            along = jnp.mean(grad * exact, axis=-1, keepdims=True)
            go = (inv * (grad - exact * along)).astype(BF16)
            go_ref[:, head_of(i)] = go
            adj_ref[:, head_of(i)] = dot(q_ref[:, head_of(i)], go, ROWS_T).astype(BF16)

    grad_out, adjoint = call(
        turn_back, [((rows, feats), BF16), (state, BF16)],
        attended, grad_own, grad_other, queries,
    )
    near_send, grad_out = tie(normed, grad_out)
    near_normed = swap(near_send, 2)
    x_adjoint = swap(adjoint, 1)
    def project(n_ref, yn_ref, *refs):
        *w_refs, own_ref, other_ref = refs
        for s, block in weight_blocks(w_refs):
            own_ref[:, lanes(s, half)] = dot(n_ref[...], block, LAST_T).astype(BF16)
            other_ref[:, lanes(s, half)] = dot(yn_ref[...], block, LAST_T).astype(BF16)

    out_own, out_send = call(
        project, [((rows, seq * half), BF16)] * 2, normed, y_normed, *weight_args
    )
    out_other = swap_y(out_send)
    last_normed = swap(far[:rows], 2)
    x_adjoint, near_normed = tie(x_adjoint, near_normed)
    pair_adjoint = add(adjoint, x_adjoint)
    near_adjoint = swap(pair_adjoint, 2)
    def local_grads(go_ref, q_ref, k_ref, v_ref, sc_ref, pre_ref, gq_ref, gk_ref, gv_ref):
        mask = causal_mask()
        for i in range(heads):
            at = head_of(i)
            go = go_ref[:, at]
            gs = dot(go, v_ref[:, at], LAST_T)
            gs = jnp.where(mask, gs, 0.0).astype(BF16)
            gq = dot(gs, k_ref[:, at], PLAIN) + dot(go, pre_ref[:, at], LAST_T)
            gq_ref[:, at] = gq.astype(BF16)
            gk_ref[:, at] = dot(gs, q_ref[:, at], ROWS_T)
            gv_ref[:, at] = dot(sc_ref[:, at], go, ROWS_T)

    grad_queries, gk_local, gv_local = call(
        local_grads,
        [((rows, feats), BF16), ((rows, feats), F32), ((rows, feats), F32)],
        grad_out, queries, keys, values, scores, prefix,
    )

    near_adjoint, out_other, gk_local = tie(near_adjoint, out_other, gk_local)
    my_cols = jnp.concatenate([near_cols[:, :wrows], far[rows:]], axis=1)
    core_cols = swap_core(my_cols)

    quad_adjoint = add(pair_adjoint, near_adjoint)
    far_adjoint = swap(quad_adjoint, 4)
    quad_adjoint, last_normed = tie(quad_adjoint, last_normed)

    core_own = swap_core(out_own)
    core_other = swap_core(out_other)

    def weight_grad(
        gy_ref, c_ref, o_ref, n_ref, near_ref, far_ref, last_ref, keep_ref, send_ref
    ):
        g, z, x, h = place()
        same = dot(columns(gy_ref, z, h), n_ref[...], ROWS_T)
        other = dot(columns(gy_ref, z, 1 - h), n_ref[...], ROWS_T)
        for i, there in enumerate((near_ref[...], far_ref[:rows, :], last_ref[...])):
            at = slice(i * wrows, (i + 1) * wrows)
            same += dot(c_ref[:, at], there, ROWS_T)
            other += dot(o_ref[:, at], there, ROWS_T)
        keep_ref[...] = jnp.where(x == h, same, other)
        send_ref[...] = jnp.where(x == h, other, same).astype(BF16)

    gw_keep, gw_send = call(
        weight_grad, [((wrows, feats), F32), ((wrows, feats), BF16)],
        grad_y, my_cols, core_cols, normed, near_normed, far, last_normed,
    )
    gw_other = swap(gw_send, 1)

    def join(a_ref, b_ref, c_ref, d_ref, y_ref):
        g = lax.axis_index("groups")
        for i in range(seq):
            at = slice(i * half, (i + 1) * half)
            y_ref[:, lanes(2 * i + g, half)] = (
                a_ref[:, at].astype(F32) + b_ref[:, at].astype(F32)
            ).astype(BF16)
            y_ref[:, lanes(2 * i + 1 - g, half)] = (
                c_ref[:, at].astype(F32) + d_ref[:, at].astype(F32)
            ).astype(BF16)

    (out_y,) = call(
        join, [((rows, outs), BF16)], out_own, core_own, out_other, core_other,
    )
    far_adjoint, out_y = tie(far_adjoint, out_y)

    def last(gk_ref, gv_ref, k_ref, v_ref, x_ref, near_ref, far_ref, ok_ref, ov_ref):
        g, z, x, h = place()
        total = jnp.where(x == 0, x_ref[...].astype(F32), 0.0)
        total += jnp.where(lax.rem(z, 2) == 0, near_ref[...].astype(F32), 0.0)
        total += jnp.where(z < 2, far_ref[...].astype(F32), 0.0)
        suffix = total.astype(BF16)
        for i in range(heads):
            at = head_of(i)
            ok_ref[:, at] = (
                gk_ref[:, at] + dot(v_ref[:, at], suffix[:, at], LAST_T)
            ).astype(BF16)
            ov_ref[:, at] = (
                gv_ref[:, at] + dot(k_ref[:, at], suffix[:, at], PLAIN)
            ).astype(BF16)

    grad_keys, grad_values = call(
        last, [((rows, feats), BF16)] * 2,
        gk_local, gv_local, keys, values, x_adjoint, near_adjoint, far_adjoint,
    )
    gw_other, grad_keys = tie(gw_other, grad_keys)
    grad_weight = gw_keep + gw_other.astype(F32)
    return out_y, grad_queries, grad_keys, grad_values, grad_weight


def solution(mesh):
    placed = (
        P(("groups", "seq"), "head"),
        P(("groups", "seq"), "head"),
        P(("groups", "seq"), "head"),
        P("seq", "head"),
        P(("groups", "seq"), None),
    )
    size = dict(mesh.shape)

    def program(queries, keys, values, out_weight, grad_y):
        short = size["seq"] == 8 and size["groups"] == 2 and size["head"] == 2
        if short and queries.shape[0] == TILE and 2 * out_weight.shape[0] == queries.shape[1]:
            return on_short_line(
                size["seq"], queries, keys, values, out_weight, grad_y
            )
        return on_device(queries, keys, values, out_weight, grad_y)

    return jax.shard_map(
        program,
        mesh=mesh,
        in_specs=placed,
        out_specs=(
            P(("groups", "seq"), None),
            P(("groups", "seq"), "head"),
            P(("groups", "seq"), "head"),
            P(("groups", "seq"), "head"),
            P(("groups", "seq"), "head"),
        ),
        check_vma=False,
    )
```

```python
import jax
import jax.numpy as jnp
from jax import lax
from jax.experimental import pallas as pl
from jax.experimental.pallas import tpu as pltpu
from jax.sharding import PartitionSpec as P

DH = 128
TILE = 128


epsilon = 1e-06
F32 = jnp.float32
BF16 = jnp.bfloat16
ROWS_T = (((0,), (0,)), ((), ()))
LAST_T = (((1,), (1,)), ((), ()))
HINTS = {
    "own_state": 300000000,
    "pack": 600000000,
    "local": 3000000000,
    "back_other": 1048576,
    "back_own": 1000000000,
    "forward": 3000000000,
    "turn_back": 3000000000,
    "project": 3000000000,
    "local_grads": 1048576,
    "weight_grad": 600000000,
    "join": 1048576,
    "last": 3000000000,
}
PLAIN = (((1,), (0,)), ((), ()))


def carried_in(value, axis, join, neutral, backward):
    count, mine = (lax.axis_size(axis), lax.axis_index(axis))
    pieces = lax.all_gather(value, axis)
    if backward:
        pieces = pieces[::-1]
        mine = count - 1 - mine
    so_far = jnp.full_like(value, 0) + jnp.asarray(neutral, value.dtype)

    def turn(position, so_far):
        longer = join(so_far, pieces[position])
        return jnp.where(position < mine, longer, so_far)

    return lax.fori_loop(0, count - 1, turn, so_far)


def add_states(earlier, later):
    return earlier + later


def on_device(queries, keys, values, out_weight, grad_y):
    row_count = queries.shape[0]
    tile_count = row_count // TILE
    head_count = queries.shape[1] // DH

    def tiled(array):
        return array.reshape(tile_count, TILE, head_count, DH)

    query_tiles = tiled(queries)
    key_tiles = tiled(keys)
    value_tiles = tiled(values)
    causal = lax.broadcasted_iota(jnp.int32, (TILE, TILE), 0) >= lax.broadcasted_iota(
        jnp.int32, (TILE, TILE), 1
    )
    raw_scores = jnp.einsum(
        "nthd,nshd->nhts", query_tiles, key_tiles, preferred_element_type=jnp.float32
    )
    scores = jnp.where(causal, raw_scores, 0.0).astype(jnp.bfloat16)
    states = jnp.einsum(
        "nshd,nshe->nhde", key_tiles, value_tiles, preferred_element_type=jnp.float32
    )
    empty_state = jnp.zeros(states.shape[1:], jnp.float32)
    device_prefix = carried_in(jnp.sum(states, axis=0), "seq", add_states, empty_state, False)
    prefix_state = (device_prefix[None] + (jnp.cumsum(states, axis=0) - states)).astype(
        jnp.bfloat16
    )
    attended = jnp.einsum(
        "nhts,nshe->nthe", scores, value_tiles, preferred_element_type=jnp.float32
    )
    attended = attended + jnp.einsum(
        "nthd,nhde->nthe", query_tiles, prefix_state, preferred_element_type=jnp.float32
    )
    inverse_rms = lax.rsqrt(jnp.mean(attended * attended, axis=-1, keepdims=True) + epsilon)
    normed_exact = attended * inverse_rms
    normed = normed_exact.astype(jnp.bfloat16).reshape(row_count, -1)
    back_weight = lax.all_gather(out_weight, "seq", axis=0, tiled=True)
    grad_normed = jnp.dot(grad_y, back_weight, preferred_element_type=jnp.float32)
    fore_weight = lax.all_gather(out_weight, "seq", axis=0, tiled=True)
    partial_out = lax.dot_general(
        normed, fore_weight, LAST_T, preferred_element_type=jnp.float32
    )
    out_y = lax.psum(partial_out.astype(jnp.bfloat16), "head")
    grad_tiles = tiled(grad_normed)
    projected = jnp.mean(grad_tiles * normed_exact, axis=-1, keepdims=True)
    grad_out = (inverse_rms * (grad_tiles - normed_exact * projected)).astype(jnp.bfloat16)
    raw_grad = jnp.einsum(
        "nthe,nshe->nhts", grad_out, value_tiles, preferred_element_type=jnp.float32
    )
    grad_scores = jnp.where(causal, raw_grad, 0.0).astype(jnp.bfloat16)
    adjoint = jnp.einsum(
        "nthd,nthe->nhde", query_tiles, grad_out, preferred_element_type=jnp.float32
    )
    own_adjoint = jnp.sum(adjoint, axis=0)
    device_suffix = carried_in(own_adjoint, "seq", add_states, empty_state, True)
    later_tiles = jnp.flip(jnp.cumsum(jnp.flip(adjoint, 0), axis=0), 0) - adjoint
    suffix_state = (device_suffix[None] + later_tiles).astype(jnp.bfloat16)
    grad_queries = jnp.einsum(
        "nhts,nshd->nthd", grad_scores, key_tiles, preferred_element_type=jnp.float32
    )
    grad_queries = grad_queries + jnp.einsum(
        "nthe,nhde->nthd", grad_out, prefix_state, preferred_element_type=jnp.float32
    )
    grad_keys = jnp.einsum(
        "nhts,nthd->nshd", grad_scores, query_tiles, preferred_element_type=jnp.float32
    )
    grad_keys = grad_keys + jnp.einsum(
        "nshe,nhde->nshd", value_tiles, suffix_state, preferred_element_type=jnp.float32
    )
    grad_values = jnp.einsum(
        "nhts,nthe->nshe", scores, grad_out, preferred_element_type=jnp.float32
    )
    grad_values = grad_values + jnp.einsum(
        "nshd,nhde->nshe", key_tiles, suffix_state, preferred_element_type=jnp.float32
    )
    grad_weight = lax.psum_scatter(
        lax.dot_general(
            grad_y, normed, (((0,), (0,)), ((), ())), preferred_element_type=jnp.float32
        ),
        "seq",
        scatter_dimension=0,
        tiled=True,
    )
    return (
        out_y,
        grad_queries.reshape(row_count, -1).astype(jnp.bfloat16),
        grad_keys.reshape(row_count, -1).astype(jnp.bfloat16),
        grad_values.reshape(row_count, -1).astype(jnp.bfloat16),
        grad_weight,
    )


def dot(a, b, dims):
    return lax.dot_general(a, b, dims, preferred_element_type=F32)


def call(body, shapes, *args):
    return pl.pallas_call(
        body,
        out_shape=[jax.ShapeDtypeStruct(s, d) for s, d in shapes],
        in_specs=[pl.BlockSpec(memory_space=pltpu.VMEM)] * len(args),
        out_specs=[pl.BlockSpec(memory_space=pltpu.VMEM)] * len(shapes),
        cost_estimate=pl.CostEstimate(
            flops=HINTS[body.__name__], bytes_accessed=2**20, transcendentals=0
        ),
        compiler_params=pltpu.CompilerParams(vmem_limit_bytes=24 * 2**20),
    )(*args)


def lanes(i, size):
    return pl.ds(pl.multiple_of(i * size, size), size)


def head_of(i):
    return slice(i * DH, (i + 1) * DH)


def causal_mask():
    rows = lax.broadcasted_iota(jnp.int32, (TILE, TILE), 0)
    return rows >= lax.broadcasted_iota(jnp.int32, (TILE, TILE), 1)


def place():
    s = lax.axis_index("seq")
    return lax.axis_index("groups"), s // 2, s % 2, lax.axis_index("head")


def on_short_line(seq, queries, keys, values, out_weight, grad_y):
    rows, feats = queries.shape
    heads = feats // DH
    wrows = out_weight.shape[0]
    half = wrows // 2
    line = seq // 2
    turns = range(1, line)
    outs = grad_y.shape[1]
    state = (DH, heads * DH)

    def permute(array, pairs):
        return lax.ppermute(array, "seq", pairs)

    def rotate(array, k):
        return permute(array, [(i, (i + 2 * k) % seq) for i in range(seq)])

    def swap(array, bit):
        return permute(array, [(i, i ^ bit) for i in range(seq)])

    def swap_y(array):
        return lax.ppermute(array, "groups", [(0, 1), (1, 0)])

    def swap_core(array):
        return lax.ppermute(array, "head", [(0, 1), (1, 0)])

    def side_by_side(*arrays):
        return jnp.concatenate(arrays, axis=0)

    def tie(*arrays):
        return lax.optimization_barrier(arrays)

    g = lax.axis_index("groups")
    my_weight = lax.dynamic_slice_in_dim(out_weight, g * half, half, 0)
    z_weight = [rotate(my_weight, k) for k in turns]

    def own_state(k_ref, v_ref, out_ref):
        for i in range(heads):
            out_ref[:, head_of(i)] = dot(
                k_ref[:, head_of(i)], v_ref[:, head_of(i)], ROWS_T
            ).astype(BF16)

    (states,) = call(own_state, [(state, BF16)], keys, values)
    x_states = swap(states, 1)
    states, own_weight, packed = tie(states, my_weight, grad_y)
    x_weight_own = swap(own_weight, 1)

    def columns(gy_ref, z, h):
        return gy_ref[:, lanes(z * 2 + h, wrows)]

    def pack(gy_ref, ys_ref, near_ref):
        g, z, x, h = place()
        for i in range(seq):
            ys_ref[:, i * half : (i + 1) * half] = gy_ref[:, lanes(2 * i + 1 - g, half)]
        near = z + 1 - 2 * lax.rem(z, 2)
        near_ref[:, :wrows] = columns(gy_ref, near, h)
        near_ref[:, wrows:] = columns(gy_ref, lax.rem(near + 2, line), h)

    y_send, near_send = call(
        pack, [((rows, seq * half), BF16), ((rows, 2 * wrows), BF16)], packed
    )
    near_cols = swap(near_send, 2)
    y_send, later_values = tie(y_send, values)
    y_cols = swap_y(y_send)

    def local(q_ref, k_ref, v_ref, sc_ref, att_ref):
        mask = causal_mask()
        for i in range(heads):
            sc = dot(q_ref[:, head_of(i)], k_ref[:, head_of(i)], LAST_T)
            sc = jnp.where(mask, sc, 0.0).astype(BF16)
            sc_ref[:, head_of(i)] = sc
            att_ref[:, head_of(i)] = dot(sc, v_ref[:, head_of(i)], PLAIN)

    scores, att_local = call(
        local, [((rows, feats), BF16), ((rows, feats), F32)], queries, keys, later_values
    )

    def add(a, b):
        return (a.astype(F32) + b.astype(F32)).astype(BF16)

    x_states, x_weight_own, att_local = tie(x_states, x_weight_own, att_local)
    pair_states = add(states, x_states)
    near_states = swap(pair_states, 2)
    pair_states, *z_weight = tie(pair_states, *z_weight)
    near_states, y_cols, near_cols = tie(near_states, y_cols, near_cols)
    quad_states = add(pair_states, near_states)
    got_states = x_states, near_states, swap(quad_states, 4)

    x_weight = swap(side_by_side(*z_weight), 1)

    def weight_blocks(refs):
        own, *others, x_own, x_others = refs
        g, z, x, h = place()
        blocks = []
        for k in range(line):
            zk = lax.rem(z - k + line, line)
            blocks.append((zk * 2 + x, (own, *others)[k][...]))
            if k == 0:
                block = x_own[...]
            else:
                block = x_others[(k - 1) * half : k * half, :]
            blocks.append((zk * 2 + 1 - x, block))
        return blocks

    weight_args = (my_weight, *z_weight, x_weight_own, x_weight)

    def back_other(yc_ref, *refs):
        *w_refs, out_ref = refs
        total = jnp.zeros((rows, feats), F32)
        for s, block in weight_blocks(w_refs):
            total += dot(yc_ref[:, lanes(s, half)], block, PLAIN)
        out_ref[...] = total

    def back_own(gy_ref, *refs):
        *w_refs, out_ref = refs
        g = lax.axis_index("groups")
        total = jnp.zeros((rows, feats), F32)
        for s, block in weight_blocks(w_refs):
            total += dot(gy_ref[:, lanes(2 * s + g, half)], block, PLAIN)
        out_ref[...] = total

    (grad_send,) = call(
        back_other, [((rows, feats), F32)], y_cols, *weight_args
    )
    grad_other = swap_y(grad_send)
    (grad_own,) = call(
        back_own, [((rows, feats), F32)], grad_y, *weight_args
    )

    def forward(
        q_ref, local_ref, x_ref, near_ref, far_ref, gy_ref, cols_ref,
        att_ref, normed_ref, prefix_ref, send_ref,
    ):
        g, z, x, h = place()
        total = jnp.where(x == 1, x_ref[...].astype(F32), 0.0)
        total += jnp.where(lax.rem(z, 2) == 1, near_ref[...].astype(F32), 0.0)
        total += jnp.where(z >= 2, far_ref[...].astype(F32), 0.0)
        prefix = total.astype(BF16)
        prefix_ref[...] = prefix
        for i in range(heads):
            att = local_ref[:, head_of(i)] + dot(
                q_ref[:, head_of(i)], prefix[:, head_of(i)], PLAIN
            )
            att_ref[:, head_of(i)] = att
            inv = lax.rsqrt(jnp.mean(att * att, axis=-1, keepdims=True) + epsilon)
            normed = (att * inv).astype(BF16)
            normed_ref[:, head_of(i)] = normed
            send_ref[:rows, head_of(i)] = normed
        send_ref[rows:, :wrows] = columns(gy_ref, lax.rem(z + 2, line), h)
        send_ref[rows:, wrows:] = cols_ref[:, wrows:]

    attended, normed, prefix, far_send = call(
        forward,
        [((rows, feats), F32), ((rows, feats), BF16), (state, BF16)]
        + [((2 * rows, feats), BF16)],
        queries, att_local, *got_states, grad_y, near_cols,
    )
    swap_send, grad_own = tie(normed, grad_own)
    y_normed = swap_y(swap_send)
    near_normed = swap(swap_send, 2)
    far = swap(far_send, 4)

    def turn_back(att_ref, own_ref, other_ref, q_ref, go_ref, adj_ref):
        for i in range(heads):
            att = att_ref[:, head_of(i)]
            inv = lax.rsqrt(jnp.mean(att * att, axis=-1, keepdims=True) + epsilon)
            exact = att * inv
            grad = own_ref[:, head_of(i)] + other_ref[:, head_of(i)]
            along = jnp.mean(grad * exact, axis=-1, keepdims=True)
            go = (inv * (grad - exact * along)).astype(BF16)
            go_ref[:, head_of(i)] = go
            adj_ref[:, head_of(i)] = dot(q_ref[:, head_of(i)], go, ROWS_T).astype(BF16)

    grad_out, adjoint = call(
        turn_back, [((rows, feats), BF16), (state, BF16)],
        attended, grad_own, grad_other, queries,
    )
    x_adjoint = swap(adjoint, 1)
    def project(n_ref, yn_ref, *refs):
        *w_refs, own_ref, other_ref = refs
        for s, block in weight_blocks(w_refs):
            own_ref[:, lanes(s, half)] = dot(n_ref[...], block, LAST_T).astype(BF16)
            other_ref[:, lanes(s, half)] = dot(yn_ref[...], block, LAST_T).astype(BF16)

    out_own, out_send = call(
        project, [((rows, seq * half), BF16)] * 2, normed, y_normed, *weight_args
    )
    out_other = swap_y(out_send)
    last_normed = swap(far[:rows], 2)
    x_adjoint, near_normed = tie(x_adjoint, near_normed)
    pair_adjoint = add(adjoint, x_adjoint)
    near_adjoint = swap(pair_adjoint, 2)
    def local_grads(go_ref, q_ref, k_ref, v_ref, sc_ref, pre_ref, gq_ref, gk_ref, gv_ref):
        mask = causal_mask()
        for i in range(heads):
            at = head_of(i)
            go = go_ref[:, at]
            gs = dot(go, v_ref[:, at], LAST_T)
            gs = jnp.where(mask, gs, 0.0).astype(BF16)
            gq = dot(gs, k_ref[:, at], PLAIN) + dot(go, pre_ref[:, at], LAST_T)
            gq_ref[:, at] = gq.astype(BF16)
            gk_ref[:, at] = dot(gs, q_ref[:, at], ROWS_T)
            gv_ref[:, at] = dot(sc_ref[:, at], go, ROWS_T)

    grad_queries, gk_local, gv_local = call(
        local_grads,
        [((rows, feats), BF16), ((rows, feats), F32), ((rows, feats), F32)],
        grad_out, queries, keys, values, scores, prefix,
    )

    near_adjoint, out_other, gk_local = tie(near_adjoint, out_other, gk_local)
    my_cols = jnp.concatenate([near_cols[:, :wrows], far[rows:]], axis=1)
    core_cols = swap_core(my_cols)

    quad_adjoint = add(pair_adjoint, near_adjoint)
    far_adjoint = swap(quad_adjoint, 4)
    quad_adjoint, last_normed = tie(quad_adjoint, last_normed)

    core_own = swap_core(out_own)
    core_other = swap_core(out_other)

    def weight_grad(
        gy_ref, c_ref, o_ref, n_ref, near_ref, far_ref, last_ref, keep_ref, send_ref
    ):
        g, z, x, h = place()
        same = dot(columns(gy_ref, z, h), n_ref[...], ROWS_T)
        other = dot(columns(gy_ref, z, 1 - h), n_ref[...], ROWS_T)
        for i, there in enumerate((near_ref[...], far_ref[:rows, :], last_ref[...])):
            at = slice(i * wrows, (i + 1) * wrows)
            same += dot(c_ref[:, at], there, ROWS_T)
            other += dot(o_ref[:, at], there, ROWS_T)
        keep_ref[...] = jnp.where(x == h, same, other)
        send_ref[...] = jnp.where(x == h, other, same).astype(BF16)

    gw_keep, gw_send = call(
        weight_grad, [((wrows, feats), F32), ((wrows, feats), BF16)],
        grad_y, my_cols, core_cols, normed, near_normed, far, last_normed,
    )
    gw_other = swap(gw_send, 1)

    def join(a_ref, b_ref, c_ref, d_ref, y_ref):
        g = lax.axis_index("groups")
        for i in range(seq):
            at = slice(i * half, (i + 1) * half)
            y_ref[:, lanes(2 * i + g, half)] = (
                a_ref[:, at].astype(F32) + b_ref[:, at].astype(F32)
            ).astype(BF16)
            y_ref[:, lanes(2 * i + 1 - g, half)] = (
                c_ref[:, at].astype(F32) + d_ref[:, at].astype(F32)
            ).astype(BF16)

    (out_y,) = call(
        join, [((rows, outs), BF16)], out_own, core_own, out_other, core_other,
    )
    far_adjoint, out_y = tie(far_adjoint, out_y)

    def last(gk_ref, gv_ref, k_ref, v_ref, x_ref, near_ref, far_ref, ok_ref, ov_ref):
        g, z, x, h = place()
        total = jnp.where(x == 0, x_ref[...].astype(F32), 0.0)
        total += jnp.where(lax.rem(z, 2) == 0, near_ref[...].astype(F32), 0.0)
        total += jnp.where(z < 2, far_ref[...].astype(F32), 0.0)
        suffix = total.astype(BF16)
        for i in range(heads):
            at = head_of(i)
            ok_ref[:, at] = (
                gk_ref[:, at] + dot(v_ref[:, at], suffix[:, at], LAST_T)
            ).astype(BF16)
            ov_ref[:, at] = (
                gv_ref[:, at] + dot(k_ref[:, at], suffix[:, at], PLAIN)
            ).astype(BF16)

    grad_keys, grad_values = call(
        last, [((rows, feats), BF16)] * 2,
        gk_local, gv_local, keys, values, x_adjoint, near_adjoint, far_adjoint,
    )
    gw_other, grad_keys = tie(gw_other, grad_keys)
    grad_weight = gw_keep + gw_other.astype(F32)
    return out_y, grad_queries, grad_keys, grad_values, grad_weight


def solution(mesh):
    placed = (
        P(("groups", "seq"), "head"),
        P(("groups", "seq"), "head"),
        P(("groups", "seq"), "head"),
        P("seq", "head"),
        P(("groups", "seq"), None),
    )
    size = dict(mesh.shape)

    def program(queries, keys, values, out_weight, grad_y):
        short = size["seq"] == 8 and size["groups"] == 2 and size["head"] == 2
        if short and queries.shape[0] == TILE and 2 * out_weight.shape[0] == queries.shape[1]:
            return on_short_line(
                size["seq"], queries, keys, values, out_weight, grad_y
            )
        return on_device(queries, keys, values, out_weight, grad_y)

    return jax.shard_map(
        program,
        mesh=mesh,
        in_specs=placed,
        out_specs=(
            P(("groups", "seq"), None),
            P(("groups", "seq"), "head"),
            P(("groups", "seq"), "head"),
            P(("groups", "seq"), "head"),
            P(("groups", "seq"), "head"),
        ),
        check_vma=False,
    )
```

```python
import jax
import jax.numpy as jnp
from jax import lax
from jax.experimental import pallas as pl
from jax.experimental.pallas import tpu as pltpu
from jax.sharding import PartitionSpec as P

DH = 128
TILE = 128


epsilon = 1e-06
F32 = jnp.float32
BF16 = jnp.bfloat16
ROWS_T = (((0,), (0,)), ((), ()))
LAST_T = (((1,), (1,)), ((), ()))
HINTS = {
    "own_state": 300000000,
    "pack": 600000000,
    "local": 3000000000,
    "back_other": 1048576,
    "back_own": 1000000000,
    "forward": 3000000000,
    "turn_back": 3000000000,
    "project": 3000000000,
    "local_grads": 1048576,
    "weight_grad": 600000000,
    "join": 1048576,
    "last": 3000000000,
}
PLAIN = (((1,), (0,)), ((), ()))


def carried_in(value, axis, join, neutral, backward):
    count, mine = (lax.axis_size(axis), lax.axis_index(axis))
    pieces = lax.all_gather(value, axis)
    if backward:
        pieces = pieces[::-1]
        mine = count - 1 - mine
    so_far = jnp.full_like(value, 0) + jnp.asarray(neutral, value.dtype)

    def turn(position, so_far):
        longer = join(so_far, pieces[position])
        return jnp.where(position < mine, longer, so_far)

    return lax.fori_loop(0, count - 1, turn, so_far)


def add_states(earlier, later):
    return earlier + later


def on_device(queries, keys, values, out_weight, grad_y):
    row_count = queries.shape[0]
    tile_count = row_count // TILE
    head_count = queries.shape[1] // DH

    def tiled(array):
        return array.reshape(tile_count, TILE, head_count, DH)

    query_tiles = tiled(queries)
    key_tiles = tiled(keys)
    value_tiles = tiled(values)
    causal = lax.broadcasted_iota(jnp.int32, (TILE, TILE), 0) >= lax.broadcasted_iota(
        jnp.int32, (TILE, TILE), 1
    )
    raw_scores = jnp.einsum(
        "nthd,nshd->nhts", query_tiles, key_tiles, preferred_element_type=jnp.float32
    )
    scores = jnp.where(causal, raw_scores, 0.0).astype(jnp.bfloat16)
    states = jnp.einsum(
        "nshd,nshe->nhde", key_tiles, value_tiles, preferred_element_type=jnp.float32
    )
    empty_state = jnp.zeros(states.shape[1:], jnp.float32)
    device_prefix = carried_in(jnp.sum(states, axis=0), "seq", add_states, empty_state, False)
    prefix_state = (device_prefix[None] + (jnp.cumsum(states, axis=0) - states)).astype(
        jnp.bfloat16
    )
    attended = jnp.einsum(
        "nhts,nshe->nthe", scores, value_tiles, preferred_element_type=jnp.float32
    )
    attended = attended + jnp.einsum(
        "nthd,nhde->nthe", query_tiles, prefix_state, preferred_element_type=jnp.float32
    )
    inverse_rms = lax.rsqrt(jnp.mean(attended * attended, axis=-1, keepdims=True) + epsilon)
    normed_exact = attended * inverse_rms
    normed = normed_exact.astype(jnp.bfloat16).reshape(row_count, -1)
    back_weight = lax.all_gather(out_weight, "seq", axis=0, tiled=True)
    grad_normed = jnp.dot(grad_y, back_weight, preferred_element_type=jnp.float32)
    fore_weight = lax.all_gather(out_weight, "seq", axis=0, tiled=True)
    partial_out = lax.dot_general(
        normed, fore_weight, LAST_T, preferred_element_type=jnp.float32
    )
    out_y = lax.psum(partial_out.astype(jnp.bfloat16), "head")
    grad_tiles = tiled(grad_normed)
    projected = jnp.mean(grad_tiles * normed_exact, axis=-1, keepdims=True)
    grad_out = (inverse_rms * (grad_tiles - normed_exact * projected)).astype(jnp.bfloat16)
    raw_grad = jnp.einsum(
        "nthe,nshe->nhts", grad_out, value_tiles, preferred_element_type=jnp.float32
    )
    grad_scores = jnp.where(causal, raw_grad, 0.0).astype(jnp.bfloat16)
    adjoint = jnp.einsum(
        "nthd,nthe->nhde", query_tiles, grad_out, preferred_element_type=jnp.float32
    )
    own_adjoint = jnp.sum(adjoint, axis=0)
    device_suffix = carried_in(own_adjoint, "seq", add_states, empty_state, True)
    later_tiles = jnp.flip(jnp.cumsum(jnp.flip(adjoint, 0), axis=0), 0) - adjoint
    suffix_state = (device_suffix[None] + later_tiles).astype(jnp.bfloat16)
    grad_queries = jnp.einsum(
        "nhts,nshd->nthd", grad_scores, key_tiles, preferred_element_type=jnp.float32
    )
    grad_queries = grad_queries + jnp.einsum(
        "nthe,nhde->nthd", grad_out, prefix_state, preferred_element_type=jnp.float32
    )
    grad_keys = jnp.einsum(
        "nhts,nthd->nshd", grad_scores, query_tiles, preferred_element_type=jnp.float32
    )
    grad_keys = grad_keys + jnp.einsum(
        "nshe,nhde->nshd", value_tiles, suffix_state, preferred_element_type=jnp.float32
    )
    grad_values = jnp.einsum(
        "nhts,nthe->nshe", scores, grad_out, preferred_element_type=jnp.float32
    )
    grad_values = grad_values + jnp.einsum(
        "nshd,nhde->nshe", key_tiles, suffix_state, preferred_element_type=jnp.float32
    )
    grad_weight = lax.psum_scatter(
        lax.dot_general(
            grad_y, normed, (((0,), (0,)), ((), ())), preferred_element_type=jnp.float32
        ),
        "seq",
        scatter_dimension=0,
        tiled=True,
    )
    return (
        out_y,
        grad_queries.reshape(row_count, -1).astype(jnp.bfloat16),
        grad_keys.reshape(row_count, -1).astype(jnp.bfloat16),
        grad_values.reshape(row_count, -1).astype(jnp.bfloat16),
        grad_weight,
    )


def dot(a, b, dims):
    return lax.dot_general(a, b, dims, preferred_element_type=F32)


def call(body, shapes, *args):
    return pl.pallas_call(
        body,
        out_shape=[jax.ShapeDtypeStruct(s, d) for s, d in shapes],
        in_specs=[pl.BlockSpec(memory_space=pltpu.VMEM)] * len(args),
        out_specs=[pl.BlockSpec(memory_space=pltpu.VMEM)] * len(shapes),
        cost_estimate=pl.CostEstimate(
            flops=HINTS[body.__name__], bytes_accessed=2**20, transcendentals=0
        ),
        compiler_params=pltpu.CompilerParams(vmem_limit_bytes=24 * 2**20),
    )(*args)


def lanes(i, size):
    return pl.ds(pl.multiple_of(i * size, size), size)


def head_of(i):
    return slice(i * DH, (i + 1) * DH)


def causal_mask():
    rows = lax.broadcasted_iota(jnp.int32, (TILE, TILE), 0)
    return rows >= lax.broadcasted_iota(jnp.int32, (TILE, TILE), 1)


def place():
    s = lax.axis_index("seq")
    return lax.axis_index("groups"), s // 2, s % 2, lax.axis_index("head")


def on_short_line(seq, queries, keys, values, out_weight, grad_y):
    rows, feats = queries.shape
    heads = feats // DH
    wrows = out_weight.shape[0]
    half = wrows // 2
    line = seq // 2
    turns = range(1, line)
    outs = grad_y.shape[1]
    state = (DH, heads * DH)

    def permute(array, pairs):
        return lax.ppermute(array, "seq", pairs)

    def rotate(array, k):
        return permute(array, [(i, (i + 2 * k) % seq) for i in range(seq)])

    def swap(array, bit):
        return permute(array, [(i, i ^ bit) for i in range(seq)])

    def swap_y(array):
        return lax.ppermute(array, "groups", [(0, 1), (1, 0)])

    def swap_core(array):
        return lax.ppermute(array, "head", [(0, 1), (1, 0)])

    def side_by_side(*arrays):
        return jnp.concatenate(arrays, axis=0)

    def tie(*arrays):
        return lax.optimization_barrier(arrays)

    g = lax.axis_index("groups")
    my_weight = lax.dynamic_slice_in_dim(out_weight, g * half, half, 0)
    hops = [*turns[1:], turns[0]]
    z_weight = [rotate(my_weight, k) for k in hops]

    def own_state(k_ref, v_ref, out_ref):
        for i in range(heads):
            out_ref[:, head_of(i)] = dot(
                k_ref[:, head_of(i)], v_ref[:, head_of(i)], ROWS_T
            ).astype(BF16)

    (states,) = call(own_state, [(state, BF16)], keys, values)
    x_states = swap(states, 1)
    states, own_weight, packed = tie(states, my_weight, grad_y)
    x_weight_own = swap(own_weight, 1)

    def columns(gy_ref, z, h):
        return gy_ref[:, lanes(z * 2 + h, wrows)]

    def pack(gy_ref, ys_ref, near_ref):
        g, z, x, h = place()
        for i in range(seq):
            ys_ref[:, i * half : (i + 1) * half] = gy_ref[:, lanes(2 * i + 1 - g, half)]
        near = z + 1 - 2 * lax.rem(z, 2)
        near_ref[:, :wrows] = columns(gy_ref, near, h)
        near_ref[:, wrows:] = columns(gy_ref, lax.rem(near + 2, line), h)

    y_send, near_send = call(
        pack, [((rows, seq * half), BF16), ((rows, 2 * wrows), BF16)], packed
    )
    near_cols = swap(near_send, 2)
    y_send, later_values = tie(y_send, values)
    y_cols = swap_y(y_send)

    def local(q_ref, k_ref, v_ref, sc_ref, att_ref):
        mask = causal_mask()
        for i in range(heads):
            sc = dot(q_ref[:, head_of(i)], k_ref[:, head_of(i)], LAST_T)
            sc = jnp.where(mask, sc, 0.0).astype(BF16)
            sc_ref[:, head_of(i)] = sc
            att_ref[:, head_of(i)] = dot(sc, v_ref[:, head_of(i)], PLAIN)

    scores, att_local = call(
        local, [((rows, feats), BF16), ((rows, feats), F32)], queries, keys, later_values
    )

    def add(a, b):
        return (a.astype(F32) + b.astype(F32)).astype(BF16)

    x_states, x_weight_own, att_local = tie(x_states, x_weight_own, att_local)
    pair_states = add(states, x_states)
    near_states = swap(pair_states, 2)
    pair_states, *z_weight = tie(pair_states, *z_weight)
    near_states, y_cols, near_cols = tie(near_states, y_cols, near_cols)
    quad_states = add(pair_states, near_states)
    got_states = x_states, near_states, swap(quad_states, 4)

    x_weight = swap(side_by_side(*z_weight), 1)

    def weight_blocks(refs):
        own, *others, x_own, x_others = refs
        g, z, x, h = place()
        blocks = []
        for i, k in enumerate((0, *hops)):
            zk = lax.rem(z - k + line, line)
            blocks.append((zk * 2 + x, (own, *others)[i][...]))
            if i == 0:
                block = x_own[...]
            else:
                block = x_others[(i - 1) * half : i * half, :]
            blocks.append((zk * 2 + 1 - x, block))
        return blocks

    weight_args = (my_weight, *z_weight, x_weight_own, x_weight)

    def back_other(yc_ref, *refs):
        *w_refs, out_ref = refs
        total = jnp.zeros((rows, feats), F32)
        for s, block in weight_blocks(w_refs):
            total += dot(yc_ref[:, lanes(s, half)], block, PLAIN)
        out_ref[...] = total

    def back_own(gy_ref, *refs):
        *w_refs, out_ref = refs
        g = lax.axis_index("groups")
        total = jnp.zeros((rows, feats), F32)
        for s, block in weight_blocks(w_refs):
            total += dot(gy_ref[:, lanes(2 * s + g, half)], block, PLAIN)
        out_ref[...] = total

    (grad_send,) = call(
        back_other, [((rows, feats), F32)], y_cols, *weight_args
    )
    grad_other = swap_y(grad_send)
    (grad_own,) = call(
        back_own, [((rows, feats), F32)], grad_y, *weight_args
    )

    def forward(
        q_ref, local_ref, x_ref, near_ref, far_ref, gy_ref, cols_ref,
        att_ref, normed_ref, prefix_ref, send_ref,
    ):
        g, z, x, h = place()
        total = jnp.where(x == 1, x_ref[...].astype(F32), 0.0)
        total += jnp.where(lax.rem(z, 2) == 1, near_ref[...].astype(F32), 0.0)
        total += jnp.where(z >= 2, far_ref[...].astype(F32), 0.0)
        prefix = total.astype(BF16)
        prefix_ref[...] = prefix
        for i in range(heads):
            att = local_ref[:, head_of(i)] + dot(
                q_ref[:, head_of(i)], prefix[:, head_of(i)], PLAIN
            )
            att_ref[:, head_of(i)] = att
            inv = lax.rsqrt(jnp.mean(att * att, axis=-1, keepdims=True) + epsilon)
            normed = (att * inv).astype(BF16)
            normed_ref[:, head_of(i)] = normed
            send_ref[:rows, head_of(i)] = normed
        send_ref[rows:, :wrows] = columns(gy_ref, lax.rem(z + 2, line), h)
        send_ref[rows:, wrows:] = cols_ref[:, wrows:]

    attended, normed, prefix, far_send = call(
        forward,
        [((rows, feats), F32), ((rows, feats), BF16), (state, BF16)]
        + [((2 * rows, feats), BF16)],
        queries, att_local, *got_states, grad_y, near_cols,
    )
    swap_send, grad_own = tie(normed, grad_own)
    y_normed = swap_y(swap_send)
    near_normed = swap(swap_send, 2)
    far = swap(far_send, 4)

    def turn_back(att_ref, own_ref, other_ref, q_ref, go_ref, adj_ref):
        for i in range(heads):
            att = att_ref[:, head_of(i)]
            inv = lax.rsqrt(jnp.mean(att * att, axis=-1, keepdims=True) + epsilon)
            exact = att * inv
            grad = own_ref[:, head_of(i)] + other_ref[:, head_of(i)]
            along = jnp.mean(grad * exact, axis=-1, keepdims=True)
            go = (inv * (grad - exact * along)).astype(BF16)
            go_ref[:, head_of(i)] = go
            adj_ref[:, head_of(i)] = dot(q_ref[:, head_of(i)], go, ROWS_T).astype(BF16)

    grad_out, adjoint = call(
        turn_back, [((rows, feats), BF16), (state, BF16)],
        attended, grad_own, grad_other, queries,
    )
    x_adjoint = swap(adjoint, 1)
    def project(n_ref, yn_ref, *refs):
        *w_refs, own_ref, other_ref = refs
        for s, block in weight_blocks(w_refs):
            own_ref[:, lanes(s, half)] = dot(n_ref[...], block, LAST_T).astype(BF16)
            other_ref[:, lanes(s, half)] = dot(yn_ref[...], block, LAST_T).astype(BF16)

    out_own, out_send = call(
        project, [((rows, seq * half), BF16)] * 2, normed, y_normed, *weight_args
    )
    out_other = swap_y(out_send)
    last_normed = swap(far[:rows], 2)
    x_adjoint, near_normed = tie(x_adjoint, near_normed)
    pair_adjoint = add(adjoint, x_adjoint)
    near_adjoint = swap(pair_adjoint, 2)
    def local_grads(go_ref, q_ref, k_ref, v_ref, sc_ref, pre_ref, gq_ref, gk_ref, gv_ref):
        mask = causal_mask()
        for i in range(heads):
            at = head_of(i)
            go = go_ref[:, at]
            gs = dot(go, v_ref[:, at], LAST_T)
            gs = jnp.where(mask, gs, 0.0).astype(BF16)
            gq = dot(gs, k_ref[:, at], PLAIN) + dot(go, pre_ref[:, at], LAST_T)
            gq_ref[:, at] = gq.astype(BF16)
            gk_ref[:, at] = dot(gs, q_ref[:, at], ROWS_T)
            gv_ref[:, at] = dot(sc_ref[:, at], go, ROWS_T)

    grad_queries, gk_local, gv_local = call(
        local_grads,
        [((rows, feats), BF16), ((rows, feats), F32), ((rows, feats), F32)],
        grad_out, queries, keys, values, scores, prefix,
    )

    near_adjoint, out_other, gk_local = tie(near_adjoint, out_other, gk_local)
    my_cols = jnp.concatenate([near_cols[:, :wrows], far[rows:]], axis=1)
    core_cols = swap_core(my_cols)

    quad_adjoint = add(pair_adjoint, near_adjoint)
    far_adjoint = swap(quad_adjoint, 4)
    quad_adjoint, last_normed = tie(quad_adjoint, last_normed)

    core_own = swap_core(out_own)
    core_other = swap_core(out_other)

    def weight_grad(
        gy_ref, c_ref, o_ref, n_ref, near_ref, far_ref, last_ref, keep_ref, send_ref
    ):
        g, z, x, h = place()
        same = dot(columns(gy_ref, z, h), n_ref[...], ROWS_T)
        other = dot(columns(gy_ref, z, 1 - h), n_ref[...], ROWS_T)
        for i, there in enumerate((near_ref[...], far_ref[:rows, :], last_ref[...])):
            at = slice(i * wrows, (i + 1) * wrows)
            same += dot(c_ref[:, at], there, ROWS_T)
            other += dot(o_ref[:, at], there, ROWS_T)
        keep_ref[...] = jnp.where(x == h, same, other)
        send_ref[...] = jnp.where(x == h, other, same).astype(BF16)

    gw_keep, gw_send = call(
        weight_grad, [((wrows, feats), F32), ((wrows, feats), BF16)],
        grad_y, my_cols, core_cols, normed, near_normed, far, last_normed,
    )
    gw_other = swap(gw_send, 1)

    def join(a_ref, b_ref, c_ref, d_ref, y_ref):
        g = lax.axis_index("groups")
        for i in range(seq):
            at = slice(i * half, (i + 1) * half)
            y_ref[:, lanes(2 * i + g, half)] = (
                a_ref[:, at].astype(F32) + b_ref[:, at].astype(F32)
            ).astype(BF16)
            y_ref[:, lanes(2 * i + 1 - g, half)] = (
                c_ref[:, at].astype(F32) + d_ref[:, at].astype(F32)
            ).astype(BF16)

    (out_y,) = call(
        join, [((rows, outs), BF16)], out_own, core_own, out_other, core_other,
    )
    far_adjoint, out_y = tie(far_adjoint, out_y)

    def last(gk_ref, gv_ref, k_ref, v_ref, x_ref, near_ref, far_ref, ok_ref, ov_ref):
        g, z, x, h = place()
        total = jnp.where(x == 0, x_ref[...].astype(F32), 0.0)
        total += jnp.where(lax.rem(z, 2) == 0, near_ref[...].astype(F32), 0.0)
        total += jnp.where(z < 2, far_ref[...].astype(F32), 0.0)
        suffix = total.astype(BF16)
        for i in range(heads):
            at = head_of(i)
            ok_ref[:, at] = (
                gk_ref[:, at] + dot(v_ref[:, at], suffix[:, at], LAST_T)
            ).astype(BF16)
            ov_ref[:, at] = (
                gv_ref[:, at] + dot(k_ref[:, at], suffix[:, at], PLAIN)
            ).astype(BF16)

    grad_keys, grad_values = call(
        last, [((rows, feats), BF16)] * 2,
        gk_local, gv_local, keys, values, x_adjoint, near_adjoint, far_adjoint,
    )
    gw_other, grad_keys = tie(gw_other, grad_keys)
    grad_weight = gw_keep + gw_other.astype(F32)
    return out_y, grad_queries, grad_keys, grad_values, grad_weight


def solution(mesh):
    placed = (
        P(("groups", "seq"), "head"),
        P(("groups", "seq"), "head"),
        P(("groups", "seq"), "head"),
        P("seq", "head"),
        P(("groups", "seq"), None),
    )
    size = dict(mesh.shape)

    def program(queries, keys, values, out_weight, grad_y):
        short = size["seq"] == 8 and size["groups"] == 2 and size["head"] == 2
        if short and queries.shape[0] == TILE and 2 * out_weight.shape[0] == queries.shape[1]:
            return on_short_line(
                size["seq"], queries, keys, values, out_weight, grad_y
            )
        return on_device(queries, keys, values, out_weight, grad_y)

    return jax.shard_map(
        program,
        mesh=mesh,
        in_specs=placed,
        out_specs=(
            P(("groups", "seq"), None),
            P(("groups", "seq"), "head"),
            P(("groups", "seq"), "head"),
            P(("groups", "seq"), "head"),
            P(("groups", "seq"), "head"),
        ),
        check_vma=False,
    )
```
